512 devices in a mesh: mem: 32 (over y, x), tile: 16 (over z, core).
Axes of the slice: x: 4, y: 8, z: 8, core: 2. Of those that a mesh axis runs over, the one named last changes fastest.
Arguments:
- latents: bfloat16 [64, 64, 8192], P('mem', 'tile'), may hold values from -3 to 3
- in_weight: bfloat16 [2, 576, 256], replicated, may hold values from -0.25 to 0.25
- out_weight: bfloat16 [2, 2304, 64], replicated, may hold values from -0.125 to 0.125
- observe_weight: bfloat16 [576, 8], replicated, may hold values from -0.25 to 0.25
- obs_cells: int32 [64, 32], P('tile'), may hold values from 0 to 127, all different within a row
- obs_values: float32 [64, 256], P('tile'), may hold values from -6 to 6
- obs_precision: float32 [64, 256], P('tile'), may hold values from 0.3 to 3
Outputs:
- analysis: float32 [64, 64, 8192], P('mem', 'tile')
- covariance: float32 [64, 64], replicated
The draws below stay inside these ranges and needn't reach their ends.
Inputs may be any that keep to these rules, and one draw needn't show every extreme that they name: `obs_cells`: each row lists 32 different columns of the slab.
All inputs are finite; a program needn't handle non-finite values.
Results may differ from the reference program's by a relative error of at most 0.009.
Values may be sent and summed in bfloat16 or wider, within the bound.
No kernel may reach another device: no remote copies, remote signals or barrier semaphores. Data moves between devices by JAX's collectives and lax.ppermute only.
A program may use at most 64 MiB of HBM per device.

```python
import math
import jax
import jax.numpy as jnp
from jax import lax

MEM_DEV = 2
COLS = 128
CH = 64
HID = 256
OBS_COLS = 32
OBS_CH = 8
ENS = 64
ROWS = 64


def block_levels(rng, shape, cuts, smallest, top_value):
    factor_of, own = 1.0, jax.random.fold_in(rng, 6)
    for axis_at, blocks in cuts:
        draws = jnp.exp(jax.random.uniform(jax.random.fold_in(own, axis_at), (blocks,), jnp.float32, smallest / len(cuts), top_value / len(cuts)))
        factor_of = factor_of * jnp.repeat(draws, shape[axis_at] // blocks).reshape([-1 if axis == axis_at else 1 for axis in range(len(shape))])
    return factor_of


def distinct(rng, rows, count, top, lift):
    order = jax.random.permutation(jax.random.fold_in(rng, 1), count)
    favour = order
    for power in range(3):
        favour = favour * favour // count
    favour = favour * lift // count
    chance = jax.random.randint(jax.random.fold_in(rng, 2), (rows, count), 0, 4096) + favour
    sure = jax.random.permutation(jax.random.fold_in(rng, 3), rows)[jnp.arange(count) % rows]
    chance = jnp.where(jnp.arange(rows)[:, None] == sure[None, :], 1 << 14, chance)
    score = chance * count + jnp.arange(count)
    return lax.top_k(score.astype(jnp.int32), top)[1].astype(jnp.int32)


def gaussian(key, dims, width, reach, split=(), kind=jnp.bfloat16):
    array = jax.random.normal(key, dims, jnp.float32) * width
    if len(split) > 0:
        array = block_levels(key, dims, split, -0.22, 0.18) * array
    return jnp.clip(array, min=-reach, max=reach).astype(kind)


def setup_inputs(seed: int = 0) -> dict:
    splits = jax.random.split(jax.random.key(seed), 8)
    latents = gaussian(splits[0], (ENS, ROWS, COLS * CH), 0.5, 3.0, ((0, 32), (1, 16)))
    in_weight = gaussian(splits[1], (2, 9 * CH, HID), (9 * CH) ** -0.5, 0.25)
    out_weight = gaussian(splits[2], (2, 9 * HID, CH), (9 * HID) ** -0.5, 0.125)
    observe_weight = gaussian(splits[3], (9 * CH, OBS_CH), (9 * CH) ** -0.5, 0.25)
    obs_cells = distinct(splits[4], ROWS, COLS, OBS_COLS, 0)
    obs_values = gaussian(splits[5], (ROWS, OBS_COLS * OBS_CH), 1.0, 6.0, ((0, 16),), jnp.float32)
    obs_precision = jnp.clip(jnp.exp(math.log(3.0) - 2.3025851 * jax.random.uniform(splits[6], (ROWS, OBS_COLS * OBS_CH), jnp.float32) ** block_levels(splits[6], (ROWS, OBS_COLS * OBS_CH), ((0, 16),), -0.2, 0.2)), 0.3, 3.0)
    return {"latents": latents, "in_weight": in_weight, "out_weight": out_weight, "observe_weight": observe_weight, "obs_cells": obs_cells, "obs_values": obs_values, "obs_precision": obs_precision}


eps = 1e-06
guide_step = 0.5

def rms_norm(values):
    return values * lax.rsqrt(lax.optimization_barrier(jnp.mean(values * values, axis=-1, keepdims=True)) + eps)

def pad_all(values):
    return jnp.pad(values, ((0, 0), (1, 1), (1, 1), (0, 0)))

def conv_rows(padded, weight):
    row_count = padded.shape[1] - 2
    col_count = padded.shape[2] - 2
    in_ch = padded.shape[3]
    summed = None
    for row_tap in range(3):
        row_band = padded[:, row_tap:row_tap + row_count]
        col_patch = jnp.concatenate([row_band[:, :, col_tap:col_tap + col_count] for col_tap in range(3)], axis=-1)
        part_sum = jnp.dot(col_patch, weight[row_tap * 3 * in_ch:(row_tap + 1) * 3 * in_ch], preferred_element_type=jnp.float32)
        summed = part_sum if summed is None else summed + part_sum
    return summed

def res_block(current, first_weight, second_weight):
    normed = rms_norm(current.astype(jnp.float32)).astype(jnp.bfloat16)
    hidden = jax.nn.silu(conv_rows(pad_all(normed), first_weight)).astype(jnp.bfloat16)
    return (current.astype(jnp.float32) + conv_rows(pad_all(hidden), second_weight)).astype(jnp.bfloat16)

def observe_padded(padded, obs_cells, observe_weight):
    row_count = padded.shape[1] - 2
    patches = []
    for row_tap in range(3):
        row_band = padded[:, row_tap:row_tap + row_count]
        for col_tap in range(3):
            col_index = (obs_cells + col_tap)[None, :, :, None]
            patches.append(jnp.take_along_axis(row_band, col_index, axis=2))
    stacked = jnp.concatenate(patches, axis=-1)
    predicted = jnp.dot(stacked, observe_weight, preferred_element_type=jnp.float32)
    return predicted.reshape(predicted.shape[0], predicted.shape[1], -1)

def reference(latents, in_weight, out_weight, observe_weight, obs_cells, obs_values, obs_precision):
    blocks = latents.reshape(ENS // MEM_DEV, MEM_DEV, ROWS, COLS, CH)

    def denoise(member_block):
        current = member_block
        for layer_idx in range(2):
            current = res_block(current, in_weight[layer_idx], out_weight[layer_idx])
        return (current, observe_padded(pad_all(current), obs_cells, observe_weight))
    denoised, predicted = lax.map(denoise, blocks)
    denoised = denoised.reshape(ENS, ROWS, COLS * CH)
    predicted = predicted.reshape(ENS, ROWS, OBS_COLS * OBS_CH)
    ens_mean = lax.optimization_barrier(jnp.mean(predicted, axis=0))
    anomaly = predicted - ens_mean
    innovation = obs_values - predicted
    covariance = jnp.einsum('jrc,mrc->jm', anomaly * obs_precision, innovation, precision=lax.Precision.HIGHEST)
    covariance = covariance / (ROWS * OBS_COLS * OBS_CH)

    def update_row(row_state):
        values = row_state.astype(jnp.float32)
        spread = values - lax.optimization_barrier(jnp.mean(values, axis=0))
        moved = jnp.einsum('jc,jm->mc', spread, covariance, precision=lax.Precision.HIGHEST)
        return values + guide_step * moved
    analysis = jnp.transpose(lax.map(update_row, jnp.transpose(denoised, (1, 0, 2))), (1, 0, 2))
    return (analysis, covariance)
```

```python
import functools

import jax
import jax.numpy as jnp
from jax import lax
from jax.experimental import pallas as pl
from jax.experimental.pallas import tpu as pltpu
from jax.sharding import Mesh
from jax.sharding import PartitionSpec as P

MEM = ("y", "x")
TILE = ("z", "c")
PAIRS = 64
HID = 256
PEERS = 32
EPS = 1e-06
STEP = 0.5
F32 = jnp.float32
BF16 = jnp.bfloat16
LIMIT = 24 * 1024 * 1024
NT = (((1,), (1,)), ((), ()))
TN = (((0,), (0,)), ((), ()))
BLOCKS = (0, 1, 2, -1)


def kernel_call(body, outs, scratch=(), flops=0, moved=0, limit=LIMIT):
    return pl.pallas_call(
        body,
        out_shape=outs,
        scratch_shapes=scratch,
        cost_estimate=pl.CostEstimate(flops=flops, bytes_accessed=moved, transcendentals=0),
        compiler_params=pltpu.CompilerParams(vmem_limit_bytes=limit),
    )


def shaped(shape, dtype=BF16):
    return jax.ShapeDtypeStruct(shape, dtype)


def rows_kernel(x_ref, rows_ref, inner_ref, outer_ref, flat):
    upper = lax.axis_index("c") == 1
    for m in range(2):
        for t in range(PAIRS):
            flat[256 * m + 4 * t : 256 * m + 4 * t + 4, :] = x_ref[m, :, 128 * t : 128 * t + 128].astype(F32)
    for m in range(2):
        rows = [flat[pl.ds(256 * m + r, PAIRS, stride=4), :] for r in range(4)]
        for r in range(4):
            rows_ref[m, r] = rows[r].astype(BF16)
        inner_ref[m] = jnp.where(upper, rows[3], rows[0]).astype(BF16)
        outer_ref[m] = jnp.where(upper, rows[0], rows[3]).astype(BF16)


def weights_kernel(in_ref, out_ref, first_ref, second_ref):
    first_ref[...] = jnp.zeros_like(first_ref)
    second_ref[...] = jnp.zeros_like(second_ref)
    for layer in range(2):
        for dr in range(3):
            for b, j in enumerate(BLOCKS):
                for h in range(2):
                    dc = j - h + 1
                    if 0 <= dc <= 2:
                        at = 64 * (3 * dr + dc)
                        first_ref[layer, 256 * dr + 64 * b : 256 * dr + 64 * b + 64, 256 * h : 256 * h + 256] = (
                            in_ref[layer, at : at + 64, :] * jnp.asarray(0.5, BF16)
                        )
                    dc = h - j + 1
                    if 0 <= dc <= 2:
                        at = 256 * (3 * dr + dc)
                        second_ref[layer, 64 * b : 64 * b + 64, 512 * dr + 256 * h : 512 * dr + 256 * h + 256] = (
                            out_ref[layer, :, at : at + 256]
                        )


def beside(values, lower):
    at = lax.broadcasted_iota(jnp.int32, values.shape, 1)
    after = jnp.where(at == PAIRS - 1, 0.0, pltpu.roll(values, PAIRS - 1, 1))
    before = jnp.where(at == 0, 0.0, pltpu.roll(values, 1, 1))
    return jnp.where(lower, after, before), jnp.where(lower, before, after)


def patches(a_ref, m, row, count, values, ones, norm):
    wide = values.astype(F32)
    lower = lax.broadcasted_iota(jnp.int32, wide.shape, 2) < 64
    if norm:
        square = (values * values).reshape(count * PAIRS, 128)
        mean = jnp.dot(square, ones, preferred_element_type=F32).reshape(count, PAIRS, 128)
        wide = wide * lax.rsqrt(mean + EPS)
    a_ref[m, pl.ds(row, count), :, 0:128] = wide.astype(BF16)
    a_ref[m, pl.ds(row, count), :, 128:256] = beside(wide, lower)[0].astype(BF16)


def denoise_kernel(chip_ref, outer_ref, inner_row, outer_row, w1_ref, w2_ref, obs_ref, cells_ref, pay_ref,
                   x_ref, a_ref, h_ref, flat):
    c = lax.axis_index("c")
    tile = 2 * lax.axis_index("z") + c
    ones = jnp.where(
        (lax.broadcasted_iota(jnp.int32, (128, 128), 0) < 64) == (lax.broadcasted_iota(jnp.int32, (128, 128), 1) < 64),
        1.0 / 64, 0.0,
    ).astype(BF16)
    for m in range(2):
        x_ref[m, 13 - 13 * c] = inner_row[m]
        x_ref[m, 13 * c] = outer_row[m]
        x_ref[m, pl.ds(1 + 8 * c, 4)] = outer_ref[m]
        for k in range(2):
            x_ref[m, pl.ds(5 - 4 * c + 4 * k, 4)] = chip_ref[k, m]

    def clear(ref, low, high, size):
        @pl.when(tile == 0)
        def _():
            for m in range(2):
                ref[m, 0:low] = jnp.zeros((low, *ref.shape[2:]), ref.dtype)

        @pl.when(tile == 15)
        def _():
            for m in range(2):
                ref[m, high:size] = jnp.zeros((size - high, *ref.shape[2:]), ref.dtype)

    for layer, (size, step1, step2) in enumerate(((14, 4, 5), (10, 4, 3))):
        half = size // 2
        for m in range(2):
            for row in (0, half):
                patches(a_ref, m, row, half, x_ref[m, row : row + half], ones, True)
        hidden = size - 2
        for m in range(2):
            for row in range(0, hidden, step1):
                left = jnp.concatenate(
                    [a_ref[m, row + dr : row + dr + step1].reshape(step1 * PAIRS, 256) for dr in range(3)], axis=1
                )
                v = jnp.dot(left, w1_ref[layer], preferred_element_type=F32)
                v = v + v * jnp.tanh(v)
                h_ref[m, row : row + step1] = v.astype(BF16).reshape(step1, PAIRS, 512)
        edge = 4 - 2 * layer
        clear(h_ref, edge, hidden - edge, hidden)
        kept = size - 4
        for m in range(2):
            for row in range(0, kept, step2):
                left = jnp.concatenate(
                    [h_ref[m, row + dr : row + dr + step2].reshape(step2 * PAIRS, 512) for dr in range(3)], axis=1
                )
                y = lax.dot_general(left, w2_ref[layer], NT, preferred_element_type=F32)
                own = y[:, 0:128].reshape(step2, PAIRS, 128)
                side = y[:, 128:256].reshape(step2, PAIRS, 128)
                lower = lax.broadcasted_iota(jnp.int32, side.shape, 2) < 64
                total = x_ref[m, row + 2 : row + 2 + step2].astype(F32) + own + beside(side, lower)[1]
                x_ref[m, row : row + step2] = total.astype(BF16)
        clear(x_ref, 3 - 2 * layer, kept - 3 + 2 * layer, kept)

    cell = cells_ref[...]
    pair = lax.shift_right_logical(cell, 1)
    lane_row = lax.broadcasted_iota(jnp.int32, (1, 128), 1) // 32
    index = lax.broadcasted_iota(jnp.int32, (384, 128), 0)
    pick = jnp.concatenate(
        [jnp.where(index == (lane_row + dr) * PAIRS + pair, 1.0, 0.0).astype(BF16) for dr in range(3)], axis=0
    )
    parts = []
    for m in range(2):
        patches(a_ref, m, 0, 6, x_ref[m, 0:6], ones, False)
        y = lax.dot_general(obs_ref[...], a_ref[m, 0:6].reshape(384, 256), NT, preferred_element_type=F32)
        y = jnp.concatenate([y[16 * dr : 16 * dr + 16] for dr in range(3)], axis=1)
        high = y.astype(BF16).astype(F32)
        parts += [high, y - high]
    seen = jnp.dot(jnp.concatenate(parts, axis=0).astype(BF16), pick, preferred_element_type=F32)
    odd = jnp.broadcast_to((cell & 1) == 1, (8, 128))
    got = [jnp.where(odd, seen[16 * i + 8 : 16 * i + 16], seen[16 * i : 16 * i + 8]) for i in range(4)]
    high = jnp.concatenate([got[0], got[2]], axis=0).astype(BF16)
    low = jnp.concatenate([got[1], got[3]], axis=0).astype(BF16)
    for m in range(2):
        for r in range(4):
            flat[pl.ds(256 * m + r, PAIRS, stride=4), :] = x_ref[m, 1 + r].astype(F32)
    for p in range(PEERS):
        both = jnp.concatenate([flat[8 * p : 8 * p + 8], flat[256 + 8 * p : 256 + 8 * p + 8]], axis=0)
        pay_ref[p, 0:16] = both.astype(BF16)
        pay_ref[p, 16:32] = high
        pay_ref[p, 32:48] = low


def gram_kernel(got_ref, values_ref, precision_ref, out_ref, flat):
    for p in range(PEERS):
        flat[16 * p : 16 * p + 16] = got_ref[p, 16:32].astype(F32) + got_ref[p, 32:48].astype(F32)
    shape = (64, 128)
    left, right = [], []
    for o in range(8):
        members = flat[pl.ds(o, 64, stride=8), :]
        mean = jnp.sum(members, axis=0, keepdims=True) * (1.0 / 64)
        left.append((members - mean) * jnp.broadcast_to(precision_ref[o : o + 1], shape))
        right.append(jnp.broadcast_to(values_ref[o : o + 1], shape) - members)
    left = jnp.concatenate(left, axis=1)
    right = jnp.concatenate(right, axis=1)
    none = jnp.zeros_like(right)
    total = lax.dot_general(
        left[0:32], jnp.concatenate([right, none], axis=0), NT, precision=lax.Precision.HIGHEST,
        preferred_element_type=F32,
    ) + lax.dot_general(
        left[32:64], jnp.concatenate([none, right], axis=0), NT, precision=lax.Precision.HIGHEST,
        preferred_element_type=F32,
    )
    for t in range(16):
        out_ref[t] = total


def update_kernel(got_ref, parts_ref, covariance_ref, back_ref, flat):
    total = parts_ref[0]
    for t in range(1, 16):
        total = total + parts_ref[t]
    total = total * (1.0 / 16384)
    covariance = jnp.concatenate([total[:, 0:64], total[:, 64:128]], axis=0)
    covariance_ref[...] = covariance
    center = (covariance - jnp.mean(covariance, axis=0, keepdims=True)) * STEP
    high = center.astype(BF16)
    both = jnp.concatenate([high, (center - high.astype(F32)).astype(BF16)], axis=0)
    for p in range(PEERS):
        flat[16 * p : 16 * p + 16] = got_ref[p, 0:16].astype(F32)
    for s in range(8):
        members = flat[pl.ds(s, 64, stride=8), :]
        narrow = members.astype(BF16)
        moved = lax.dot_general(both, jnp.concatenate([narrow, narrow], axis=0), TN, preferred_element_type=F32)
        flat[pl.ds(s, 64, stride=8), :] = members + moved
    for p in range(PEERS):
        back_ref[p] = flat[16 * p : 16 * p + 16].astype(BF16)


def final_kernel(got_ref, out_ref):
    for p in range(PEERS):
        values = got_ref[p].astype(F32)
        for m in range(2):
            for t in range(2):
                at = 128 * (2 * p + t)
                out_ref[m, :, at : at + 128] = values[8 * m + 4 * t : 8 * m + 4 * t + 4]


def observed_weights(weight):
    taps = jnp.transpose(weight.reshape(3, 3, 64, 8), (0, 1, 3, 2))
    none = jnp.zeros_like(taps[:, 0])
    sides = []
    for h in range(2):
        sides.append(jnp.concatenate([taps[:, j - h + 1] if 0 <= j - h + 1 <= 2 else none for j in BLOCKS], axis=-1))
    return jnp.stack(sides, axis=1).reshape(48, 256)


def exchange_pairs():
    across, inner, outer = [], [], []
    for z in range(7):
        across += [(2 * z + 1, 2 * z + 2), (2 * z + 2, 2 * z + 1)]
        inner += [(2 * z + 1, 2 * z + 3), (2 * z + 2, 2 * z)]
        outer += [(2 * z, 2 * z + 2), (2 * z + 3, 2 * z + 1)]
    return across, inner, outer


def per_device(latents, in_weight, out_weight, observe_weight, obs_cells, obs_values, obs_precision):
    across, inner, outer = exchange_pairs()
    rows, inner_row, outer_row = kernel_call(
        rows_kernel,
        (shaped((2, 4, PAIRS, 128)), shaped((2, PAIRS, 128)), shaped((2, PAIRS, 128))),
        [pltpu.VMEM((512, 128), F32)], moved=300_000,
    )(latents)
    outer_tile = lax.ppermute(rows, TILE, across)
    outer_row = lax.ppermute(outer_row, TILE, outer)
    inner_row = lax.ppermute(inner_row, TILE, inner)
    chip = lax.all_gather(rows, "c")
    first, second = kernel_call(
        weights_kernel, (shaped((2, 768, 512)), shaped((2, 256, 1536))), moved=4_300_000,
    )(in_weight, jnp.transpose(out_weight, (0, 2, 1)))
    pay = kernel_call(
        denoise_kernel,
        shaped((PEERS, 48, 128)),
        [
            pltpu.VMEM((2, 14, PAIRS, 128), BF16),
            pltpu.VMEM((2, 14, PAIRS, 256), BF16),
            pltpu.VMEM((2, 12, PAIRS, 512), BF16),
            pltpu.VMEM((512, 128), F32),
        ],
        flops=4_000_000_000, moved=4_300_000, limit=40 * 1024 * 1024,
    )(chip, outer_tile, inner_row, outer_row, first, second, observed_weights(observe_weight),
      obs_cells.reshape(1, 128))
    got = lax.all_to_all(pay, MEM, 0, 0, tiled=True)

    def by_channel(values):
        return jnp.transpose(values.reshape(4, 32, 8), (2, 0, 1)).reshape(8, 128)

    parts = kernel_call(
        gram_kernel, shaped((16, 32, 128), F32), [pltpu.VMEM((512, 128), F32)], moved=700_000,
    )(got, by_channel(obs_values), by_channel(obs_precision))
    parts = lax.all_to_all(parts, TILE, 0, 0, tiled=True)
    covariance, back = kernel_call(
        update_kernel, (shaped((64, 64), F32), shaped((PEERS, 16, 128))), [pltpu.VMEM((512, 128), F32)],
        moved=700_000,
    )(got, parts)
    back = lax.all_to_all(back, MEM, 0, 0, tiled=True)
    analysis = kernel_call(final_kernel, shaped((2, 4, 8192), F32), moved=400_000)(back)
    return analysis, covariance


def solution(mesh):
    split = Mesh(mesh.devices.reshape(8, 4, 8, 2), ("y", "x", "z", "c"))
    return jax.shard_map(
        per_device,
        mesh=split,
        in_specs=(P(MEM, TILE, None), P(), P(), P(), P(TILE, None), P(TILE, None), P(TILE, None)),
        out_specs=(P(MEM, TILE, None), P()),
        check_vma=False,
    )
```

```python
import functools

import jax
import jax.numpy as jnp
from jax import lax
from jax.experimental import pallas as pl
from jax.experimental.pallas import tpu as pltpu
from jax.sharding import Mesh
from jax.sharding import PartitionSpec as P

MEM = ("y", "x")
TILE = ("z", "c")
PAIRS = 64
HID = 256
PEERS = 32
EPS = 1e-06
STEP = 0.5
F32 = jnp.float32
BF16 = jnp.bfloat16
LIMIT = 24 * 1024 * 1024
NT = (((1,), (1,)), ((), ()))
TN = (((0,), (0,)), ((), ()))
BLOCKS = (0, 1, 2, -1)


def kernel_call(body, outs, scratch=(), flops=0, moved=0, limit=LIMIT):
    return pl.pallas_call(
        body,
        out_shape=outs,
        scratch_shapes=scratch,
        cost_estimate=pl.CostEstimate(flops=flops, bytes_accessed=moved, transcendentals=0),
        compiler_params=pltpu.CompilerParams(vmem_limit_bytes=limit),
    )


def shaped(shape, dtype=BF16):
    return jax.ShapeDtypeStruct(shape, dtype)


def rows_kernel(x_ref, rows_ref, inner_ref, outer_ref, flat):
    upper = lax.axis_index("c") == 1
    for m in range(2):
        for t in range(PAIRS):
            flat[256 * m + 4 * t : 256 * m + 4 * t + 4, :] = x_ref[m, :, 128 * t : 128 * t + 128].astype(F32)
    for m in range(2):
        rows = [flat[pl.ds(256 * m + r, PAIRS, stride=4), :] for r in range(4)]
        for r in range(4):
            rows_ref[m, r] = rows[r].astype(BF16)
        inner_ref[m] = jnp.where(upper, rows[3], rows[0]).astype(BF16)
        outer_ref[m] = jnp.where(upper, rows[0], rows[3]).astype(BF16)


def spread_weights(in_ref, out_ref, seen_ref, first_ref, second_ref, obs_ref):
    first_ref[...] = jnp.zeros_like(first_ref)
    second_ref[...] = jnp.zeros_like(second_ref)
    for layer in range(2):
        for dr in range(3):
            for b, j in enumerate(BLOCKS):
                for h in range(2):
                    dc = j - h + 1
                    if 0 <= dc <= 2:
                        at = 64 * (3 * dr + dc)
                        first_ref[layer, 256 * dr + 64 * b : 256 * dr + 64 * b + 64, 256 * h : 256 * h + 256] = (
                            in_ref[layer, at : at + 64, :] * jnp.asarray(0.5, BF16)
                        )
                    dc = h - j + 1
                    if 0 <= dc <= 2:
                        at = 256 * (3 * dr + dc)
                        second_ref[layer, 64 * b : 64 * b + 64, 512 * dr + 256 * h : 512 * dr + 256 * h + 256] = (
                            out_ref[layer, :, at : at + 256]
                        )
    taps = seen_ref[...].astype(F32)
    none = jnp.zeros((8, 64), F32)
    for dr in range(3):
        for h in range(2):
            blocks = [j - h + 1 for j in BLOCKS]
            obs_ref[8 * (2 * dr + h) : 8 * (2 * dr + h) + 8, :] = jnp.concatenate(
                [taps[:, 64 * (3 * dr + dc) : 64 * (3 * dr + dc) + 64] if 0 <= dc <= 2 else none for dc in blocks],
                axis=1,
            )


def beside(values, lower):
    at = lax.broadcasted_iota(jnp.int32, values.shape, 1)
    after = jnp.where(at == PAIRS - 1, 0.0, pltpu.roll(values, PAIRS - 1, 1))
    before = jnp.where(at == 0, 0.0, pltpu.roll(values, 1, 1))
    return jnp.where(lower, after, before), jnp.where(lower, before, after)


def patches(a_ref, m, row, count, values, ones, norm):
    wide = values.astype(F32)
    lower = lax.broadcasted_iota(jnp.int32, wide.shape, 2) < 64
    if norm:
        square = (values * values).reshape(count * PAIRS, 128)
        mean = jnp.dot(square, ones, preferred_element_type=F32).reshape(count, PAIRS, 128)
        wide = wide * lax.rsqrt(mean + EPS)
    a_ref[m, pl.ds(row, count), :, 0:128] = wide.astype(BF16)
    a_ref[m, pl.ds(row, count), :, 128:256] = beside(wide, lower)[0].astype(BF16)


def by_channel(values_ref, precision_ref, sides_ref):
    own = lax.broadcasted_iota(jnp.int32, (8, 256), 1) % 8 == lax.broadcasted_iota(jnp.int32, (8, 256), 0)
    spread = [
        jnp.concatenate(
            [jnp.where(own, jnp.broadcast_to(ref[r : r + 1, :], (8, 256)), 0.0) for r in range(4)], axis=1
        )
        for ref in (values_ref, precision_ref)
    ]
    whole = jnp.concatenate(spread, axis=0)
    at = lax.broadcasted_iota(jnp.int32, (1024, 128), 0)
    place = jnp.where(at // 8 == lax.broadcasted_iota(jnp.int32, (1024, 128), 1), 1.0, 0.0).astype(BF16)
    high = whole.astype(BF16)
    rest = whole - high.astype(F32)
    middle = rest.astype(BF16)
    low = (rest - middle.astype(F32)).astype(BF16)
    placed = jnp.dot(jnp.concatenate([high, middle, low], axis=0), place, preferred_element_type=F32)
    sides_ref[...] = placed[0:16] + placed[16:32] + placed[32:48]


def denoise_kernel(chip_ref, outer_ref, inner_row, outer_row, in_hbm, out_hbm, seen_ref, cells_ref, values_ref,
                   precision_ref, pay_ref, sides_ref,
                   x_ref, a_ref, h_ref, flat, in_ref, out_ref, w1_ref, w2_ref, obs_ref, sems):
    fetches = [pltpu.make_async_copy(in_hbm, in_ref, sems.at[0]), pltpu.make_async_copy(out_hbm, out_ref, sems.at[1])]
    for fetch in fetches:
        fetch.start()
    c = lax.axis_index("c")
    tile = 2 * lax.axis_index("z") + c
    ones = jnp.where(
        (lax.broadcasted_iota(jnp.int32, (128, 128), 0) < 64) == (lax.broadcasted_iota(jnp.int32, (128, 128), 1) < 64),
        1.0 / 64, 0.0,
    ).astype(BF16)
    for m in range(2):
        x_ref[m, 13 - 13 * c] = inner_row[m]
        x_ref[m, 13 * c] = outer_row[m]
        x_ref[m, pl.ds(1 + 8 * c, 4)] = outer_ref[m]
        for k in range(2):
            x_ref[m, pl.ds(5 - 4 * c + 4 * k, 4)] = chip_ref[k, m]

    def clear(ref, low, high, size):
        @pl.when(tile == 0)
        def _():
            for m in range(2):
                ref[m, 0:low] = jnp.zeros((low, *ref.shape[2:]), ref.dtype)

        @pl.when(tile == 15)
        def _():
            for m in range(2):
                ref[m, high:size] = jnp.zeros((size - high, *ref.shape[2:]), ref.dtype)

    by_channel(values_ref, precision_ref, sides_ref)
    for layer, (size, step1, step2) in enumerate(((14, 4, 5), (10, 4, 3))):
        half = size // 2
        for m in range(2):
            for row in (0, half):
                patches(a_ref, m, row, half, x_ref[m, row : row + half], ones, True)
        hidden = size - 2
        if layer == 0:
            for fetch in fetches:
                fetch.wait()
            spread_weights(in_ref, out_ref, seen_ref, w1_ref, w2_ref, obs_ref)
        for m in range(2):
            for row in range(0, hidden, step1):
                left = jnp.concatenate(
                    [a_ref[m, row + dr : row + dr + step1].reshape(step1 * PAIRS, 256) for dr in range(3)], axis=1
                )
                v = jnp.dot(left, w1_ref[layer], preferred_element_type=F32)
                v = v + v * jnp.tanh(v)
                h_ref[m, row : row + step1] = v.astype(BF16).reshape(step1, PAIRS, 512)
        edge = 4 - 2 * layer
        clear(h_ref, edge, hidden - edge, hidden)
        kept = size - 4
        for m in range(2):
            for row in range(0, kept, step2):
                left = jnp.concatenate(
                    [h_ref[m, row + dr : row + dr + step2].reshape(step2 * PAIRS, 512) for dr in range(3)], axis=1
                )
                y = lax.dot_general(left, w2_ref[layer], NT, preferred_element_type=F32)
                own = y[:, 0:128].reshape(step2, PAIRS, 128)
                side = y[:, 128:256].reshape(step2, PAIRS, 128)
                lower = lax.broadcasted_iota(jnp.int32, side.shape, 2) < 64
                total = x_ref[m, row + 2 : row + 2 + step2].astype(F32) + own + beside(side, lower)[1]
                x_ref[m, row : row + step2] = total.astype(BF16)
        clear(x_ref, 3 - 2 * layer, kept - 3 + 2 * layer, kept)

    cell = jnp.concatenate([cells_ref[r : r + 1, :] for r in range(4)], axis=1)
    pair = lax.shift_right_logical(cell, 1)
    lane_row = lax.broadcasted_iota(jnp.int32, (1, 128), 1) // 32
    index = lax.broadcasted_iota(jnp.int32, (384, 128), 0)
    pick = jnp.concatenate(
        [jnp.where(index == (lane_row + dr) * PAIRS + pair, 1.0, 0.0).astype(BF16) for dr in range(3)], axis=0
    )
    parts = []
    for m in range(2):
        patches(a_ref, m, 0, 6, x_ref[m, 0:6], ones, False)
        y = lax.dot_general(obs_ref[...].astype(BF16), a_ref[m, 0:6].reshape(384, 256), NT, preferred_element_type=F32)
        parts.append(y)
    seen = []
    for y in parts:
        taps = [y[16 * dr : 16 * dr + 16] for dr in range(3)]
        whole = jnp.concatenate(taps, axis=1)
        high = whole.astype(BF16).astype(F32)
        both = jnp.concatenate([high, whole - high], axis=0).astype(BF16)
        picked = jnp.dot(both, pick, preferred_element_type=F32)
        seen.append(picked[0:16] + picked[16:32])
    seen = jnp.concatenate(seen, axis=0)
    odd = jnp.broadcast_to((cell & 1) == 1, (8, 128))
    got = [jnp.where(odd, seen[16 * m + 8 : 16 * m + 16], seen[16 * m : 16 * m + 8]) for m in range(2)]
    got = jnp.concatenate(got, axis=0).astype(BF16)
    for m in range(2):
        for r in range(4):
            flat[pl.ds(256 * m + r, PAIRS, stride=4), :] = x_ref[m, 1 + r].astype(F32)
    for p in range(PEERS):
        both = jnp.concatenate([flat[8 * p : 8 * p + 8], flat[256 + 8 * p : 256 + 8 * p + 8]], axis=0)
        pay_ref[p, 0:16] = both.astype(BF16)
        pay_ref[p, 16:32] = got


def gram_kernel(got_ref, sides_ref, out_ref, flat):
    for p in range(PEERS):
        flat[16 * p : 16 * p + 16] = got_ref[p, 16:32].astype(F32)
    shape = (64, 128)
    left, right = [], []
    for o in range(8):
        members = flat[pl.ds(o, 64, stride=8), :]
        mean = jnp.sum(members, axis=0, keepdims=True) * (1.0 / 64)
        left.append((members - mean) * jnp.broadcast_to(sides_ref[8 + o : 9 + o], shape))
        right.append(jnp.broadcast_to(sides_ref[o : o + 1], shape) - members)
    left = jnp.concatenate(left, axis=1)
    right = jnp.concatenate(right, axis=1)
    none = jnp.zeros_like(right)
    total = lax.dot_general(
        left[0:32], jnp.concatenate([right, none], axis=0), NT, precision=lax.Precision.HIGHEST,
        preferred_element_type=F32,
    ) + lax.dot_general(
        left[32:64], jnp.concatenate([none, right], axis=0), NT, precision=lax.Precision.HIGHEST,
        preferred_element_type=F32,
    )
    for t in range(16):
        out_ref[t] = total.astype(BF16)


def update_kernel(got_ref, parts_ref, covariance_ref, back_ref, flat):
    total = parts_ref[0].astype(F32)
    for t in range(1, 16):
        total = total + parts_ref[t].astype(F32)
    total = total * (1.0 / 16384)
    covariance = jnp.concatenate([total[:, 0:64], total[:, 64:128]], axis=0)
    covariance_ref[...] = covariance
    center = (covariance - jnp.mean(covariance, axis=0, keepdims=True)) * STEP
    high = center.astype(BF16)
    both = jnp.concatenate([high, (center - high.astype(F32)).astype(BF16)], axis=0)
    for p in range(PEERS):
        flat[16 * p : 16 * p + 16] = got_ref[p, 0:16].astype(F32)
    for s in range(8):
        members = flat[pl.ds(s, 64, stride=8), :]
        narrow = members.astype(BF16)
        moved = lax.dot_general(both, jnp.concatenate([narrow, narrow], axis=0), TN, preferred_element_type=F32)
        flat[pl.ds(s, 64, stride=8), :] = members + moved
    for p in range(PEERS):
        back_ref[p] = flat[16 * p : 16 * p + 16].astype(BF16)


def final_kernel(got_ref, out_ref):
    for p in range(PEERS):
        values = got_ref[p].astype(F32)
        for m in range(2):
            for t in range(2):
                at = 128 * (2 * p + t)
                out_ref[m, :, at : at + 128] = values[8 * m + 4 * t : 8 * m + 4 * t + 4]


def exchange_pairs():
    across, inner, outer = [], [], []
    for z in range(7):
        across += [(2 * z + 1, 2 * z + 2), (2 * z + 2, 2 * z + 1)]
        inner += [(2 * z + 1, 2 * z + 3), (2 * z + 2, 2 * z)]
        outer += [(2 * z, 2 * z + 2), (2 * z + 3, 2 * z + 1)]
    return across, inner, outer


def per_device(latents, in_weight, out_weight, observe_weight, obs_cells, obs_values, obs_precision):
    across, inner, outer = exchange_pairs()
    rows, inner_row, outer_row = kernel_call(
        rows_kernel,
        (shaped((2, 4, PAIRS, 128)), shaped((2, PAIRS, 128)), shaped((2, PAIRS, 128))),
        [pltpu.VMEM((512, 128), F32)], moved=300_000,
    )(latents)
    outer_tile = lax.ppermute(rows, TILE, across)
    outer_row = lax.ppermute(outer_row, TILE, outer)
    inner_row = lax.ppermute(inner_row, TILE, inner)
    chip = lax.all_gather(rows, "c")

    vmem, hbm = pl.BlockSpec(memory_space=pltpu.VMEM), pl.BlockSpec(memory_space=pltpu.HBM)
    pay, sides = pl.pallas_call(
        denoise_kernel,
        out_shape=(shaped((PEERS, 32, 128)), shaped((16, 128), F32)),
        in_specs=[vmem] * 4 + [hbm] * 2 + [vmem] * 4,
        scratch_shapes=[
            pltpu.VMEM((2, 14, PAIRS, 128), BF16),
            pltpu.VMEM((2, 14, PAIRS, 256), BF16),
            pltpu.VMEM((2, 12, PAIRS, 512), BF16),
            pltpu.VMEM((512, 128), F32),
            pltpu.VMEM((2, 576, 256), BF16),
            pltpu.VMEM((2, 64, 2304), BF16),
            pltpu.VMEM((2, 768, 512), BF16),
            pltpu.VMEM((2, 256, 1536), BF16),
            pltpu.VMEM((48, 256), F32),
            pltpu.SemaphoreType.DMA((2,)),
        ],
        cost_estimate=pl.CostEstimate(flops=4_000_000_000, bytes_accessed=4_300_000, transcendentals=0),
        compiler_params=pltpu.CompilerParams(vmem_limit_bytes=52 * 1024 * 1024),
    )(chip, outer_tile, inner_row, outer_row, pltpu.with_memory_space_constraint(in_weight, pltpu.HBM),
      pltpu.with_memory_space_constraint(jnp.transpose(out_weight, (0, 2, 1)), pltpu.HBM),
      jnp.transpose(observe_weight), obs_cells, obs_values, obs_precision)
    got = lax.all_to_all(pay, MEM, 0, 0, tiled=True)

    parts = kernel_call(
        gram_kernel, shaped((16, 32, 128)), [pltpu.VMEM((512, 128), F32)], moved=700_000,
    )(got, sides)
    parts = lax.all_to_all(parts, TILE, 0, 0, tiled=True)
    covariance, back = kernel_call(
        update_kernel, (shaped((64, 64), F32), shaped((PEERS, 16, 128))), [pltpu.VMEM((512, 128), F32)],
        moved=700_000,
    )(got, parts)
    back = lax.all_to_all(back, MEM, 0, 0, tiled=True)
    analysis = kernel_call(final_kernel, shaped((2, 4, 8192), F32), moved=400_000)(back)
    return analysis, covariance


def solution(mesh):
    split = Mesh(mesh.devices.reshape(8, 4, 8, 2), ("y", "x", "z", "c"))
    return jax.shard_map(
        per_device,
        mesh=split,
        in_specs=(P(MEM, TILE, None), P(), P(), P(), P(TILE, None), P(TILE, None), P(TILE, None)),
        out_specs=(P(MEM, TILE, None), P()),
        check_vma=False,
    )
```

```python
import functools

import jax
import jax.numpy as jnp
from jax import lax
from jax.experimental import pallas as pl
from jax.experimental.pallas import tpu as pltpu
from jax.sharding import Mesh
from jax.sharding import PartitionSpec as P

MEM = ("y", "x")
TILE = ("z", "c")
PAIRS = 64
HID = 256
PEERS = 32
EPS = 1e-06
STEP = 0.5
F32 = jnp.float32
BF16 = jnp.bfloat16
LIMIT = 24 * 1024 * 1024
NT = (((1,), (1,)), ((), ()))
TN = (((0,), (0,)), ((), ()))
BLOCKS = (0, 1, 2, -1)


def kernel_call(body, outs, scratch=(), flops=0, moved=0, limit=LIMIT):
    return pl.pallas_call(
        body,
        out_shape=outs,
        scratch_shapes=scratch,
        cost_estimate=pl.CostEstimate(flops=flops, bytes_accessed=moved, transcendentals=0),
        compiler_params=pltpu.CompilerParams(vmem_limit_bytes=limit),
    )


def shaped(shape, dtype=BF16):
    return jax.ShapeDtypeStruct(shape, dtype)


def rows_kernel(x_ref, rows_ref, flat):
    for m in range(2):
        for t in range(PAIRS):
            flat[256 * m + 4 * t : 256 * m + 4 * t + 4, :] = x_ref[m, :, 128 * t : 128 * t + 128].astype(F32)
    for m in range(2):
        for r in range(4):
            rows_ref[r, m] = flat[pl.ds(256 * m + r, PAIRS, stride=4), :].astype(BF16)


def spread_weights(in_ref, out_ref, seen_ref, first_ref, second_ref, obs_ref):
    first_ref[...] = jnp.zeros_like(first_ref)
    second_ref[...] = jnp.zeros_like(second_ref)
    for layer in range(2):
        for dr in range(3):
            for b, j in enumerate(BLOCKS):
                for h in range(2):
                    dc = j - h + 1
                    if 0 <= dc <= 2:
                        at = 64 * (3 * dr + dc)
                        first_ref[layer, 256 * dr + 64 * b : 256 * dr + 64 * b + 64, 256 * h : 256 * h + 256] = (
                            in_ref[layer, at : at + 64, :] * jnp.asarray(0.5, BF16)
                        )
                    dc = h - j + 1
                    if 0 <= dc <= 2:
                        at = 256 * (3 * dr + dc)
                        second_ref[layer, 64 * b : 64 * b + 64, 512 * dr + 256 * h : 512 * dr + 256 * h + 256] = (
                            out_ref[layer, :, at : at + 256]
                        )
    taps = seen_ref[...].astype(F32)
    none = jnp.zeros((8, 64), F32)
    rows = []
    for dr in range(3):
        for h in range(2):
            blocks = [j - h + 1 for j in BLOCKS]
            rows.append(jnp.concatenate(
                [taps[:, 64 * (3 * dr + dc) : 64 * (3 * dr + dc) + 64] if 0 <= dc <= 2 else none for dc in blocks],
                axis=1,
            ))
    obs_ref[...] = jnp.concatenate(rows, axis=0).astype(BF16)


def beside(values, lower):
    at = lax.broadcasted_iota(jnp.int32, values.shape, 1)
    after = jnp.where(at == PAIRS - 1, 0.0, pltpu.roll(values, PAIRS - 1, 1))
    before = jnp.where(at == 0, 0.0, pltpu.roll(values, 1, 1))
    return jnp.where(lower, after, before), jnp.where(lower, before, after)


def mean_over_channels():
    return jnp.where(
        (lax.broadcasted_iota(jnp.int32, (128, 128), 0) < 64) == (lax.broadcasted_iota(jnp.int32, (128, 128), 1) < 64),
        1.0 / 64, 0.0,
    ).astype(BF16)


def patches(a_ref, m, row, values, norm):
    count = values.shape[0]
    wide = values.astype(F32)
    lower = lax.broadcasted_iota(jnp.int32, wide.shape, 2) < 64
    if norm is not None:
        square = (values * values).reshape(count * PAIRS, 128)
        mean = jnp.dot(square, norm, preferred_element_type=F32).reshape(count, PAIRS, 128)
        wide = wide * lax.rsqrt(mean + EPS)
    a_ref[m, pl.ds(row, count), :, 0:128] = wide.astype(BF16)
    a_ref[m, pl.ds(row, count), :, 128:256] = beside(wide, lower)[0].astype(BF16)


def taps_of(ref, m, row, count):
    width = ref.shape[3]
    return jnp.concatenate(
        [ref[m, pl.ds(row + dr, count)].reshape(count * PAIRS, width) for dr in range(3)], axis=1
    )


def hidden_of(left, weight):
    v = jnp.dot(left, weight, preferred_element_type=F32)
    return v + v * jnp.tanh(v)


def scaled_rows(values, factors):
    return jnp.concatenate(
        [values[i : i + 1] * factors[i] if i in factors else values[i : i + 1] for i in range(values.shape[0])], axis=0
    )


def by_channel(values_ref, precision_ref, sides_ref):
    own = lax.broadcasted_iota(jnp.int32, (8, 256), 1) % 8 == lax.broadcasted_iota(jnp.int32, (8, 256), 0)
    spread = [
        jnp.concatenate(
            [jnp.where(own, jnp.broadcast_to(ref[r : r + 1, :], (8, 256)), 0.0) for r in range(4)], axis=1
        )
        for ref in (values_ref, precision_ref)
    ]
    whole = jnp.concatenate(spread, axis=0)
    at = lax.broadcasted_iota(jnp.int32, (1024, 128), 0)
    place = jnp.where(at // 8 == lax.broadcasted_iota(jnp.int32, (1024, 128), 1), 1.0, 0.0).astype(BF16)
    high = whole.astype(BF16)
    rest = whole - high.astype(F32)
    middle = rest.astype(BF16)
    low = (rest - middle.astype(F32)).astype(BF16)
    placed = jnp.dot(jnp.concatenate([high, middle, low], axis=0), place, preferred_element_type=F32)
    sides_ref[0:16] = placed[0:16] + placed[16:32] + placed[32:48]


def inner_kernel(chip_ref, in_hbm, out_hbm, seen_hbm, cells_hbm, values_hbm, precision_hbm,
                 a_ref, h_ref, w1_ref, w2_ref, obs_ref, pick_ref, sides_ref,
                 in_ref, out_ref, seen_ref, cells_ref, values_ref, precision_ref, sems):
    sources = (cells_hbm, values_hbm, precision_hbm, seen_hbm, in_hbm, out_hbm)
    targets = (cells_ref, values_ref, precision_ref, seen_ref, in_ref, out_ref)
    fetches = [pltpu.make_async_copy(a, b, sems.at[i]) for i, (a, b) in enumerate(zip(sources, targets))]
    for fetch in fetches:
        fetch.start()
    norm = mean_over_channels()
    for m in range(2):
        for row in (0, 4):
            patches(a_ref, m, row, chip_ref[row : row + 4, m], norm)
    for fetch in fetches[:3]:
        fetch.wait()
    by_channel(values_ref, precision_ref, sides_ref)
    cell = jnp.concatenate([cells_ref[r : r + 1, :] for r in range(4)], axis=1)
    pair = lax.shift_right_logical(cell, 1)
    lane_row = lax.broadcasted_iota(jnp.int32, (1, 128), 1) // 32
    index = lax.broadcasted_iota(jnp.int32, (384, 128), 0)
    for dr in range(3):
        pick_ref[384 * dr : 384 * dr + 384, :] = jnp.where(index == (lane_row + dr) * PAIRS + pair, 1.0, 0.0).astype(BF16)
    sides_ref[16:24] = jnp.broadcast_to((cell & 1).astype(F32), (8, 128))
    for fetch in fetches[3:]:
        fetch.wait()
    spread_weights(in_ref, out_ref, seen_ref, w1_ref, w2_ref, obs_ref)
    for m in range(2):
        for row in (0, 3):
            hidden = hidden_of(taps_of(a_ref, m, row, 3), w1_ref[0])
            h_ref[m, row : row + 3] = hidden.astype(BF16).reshape(3, PAIRS, 512)


def denoise_kernel(chip_ref, outer_ref, edge_ref, a_part, h_part, w1_ref, w2_ref, obs_ref, pick_ref, sides_ref,
                   pay_ref, x_ref, a_ref, h_ref, flat, sems):
    c = lax.axis_index("c")
    tile = 2 * lax.axis_index("z") + c
    first = jnp.where(tile == 0, 0.0, 1.0).astype(F32)
    last = jnp.where(tile == 15, 0.0, 1.0).astype(F32)
    start = 5 - 4 * c
    moves = [
        pltpu.make_async_copy(a_part.at[m], a_ref.at[m, pl.ds(start, 8)], sems.at[m]) for m in range(2)
    ] + [
        pltpu.make_async_copy(h_part.at[m], h_ref.at[m, pl.ds(start, 6)], sems.at[2 + m]) for m in range(2)
    ] + [pltpu.make_async_copy(chip_ref, x_ref.at[pl.ds(start, 8)], sems.at[4])]
    for move in moves:
        move.start()
    norm = mean_over_channels()
    edge = edge_ref[1 - c]
    for m in range(2):
        patches(a_ref, m, 9 * c, outer_ref[:, m], norm)
        patches(a_ref, m, 13 - 13 * c, edge[m : m + 1], norm)
    x_ref[pl.ds(9 * c, 5)] = outer_ref[...]
    x_ref[13 - 13 * c] = edge
    for move in moves:
        move.wait()
    upper = c == 1
    group = {q: jnp.where(upper, last if q else 1.0, first if q < 4 else 1.0) for q in range(5)}
    for m in range(2):
        left = jnp.concatenate([taps_of(a_ref, m, 7 * c, 5), taps_of(a_ref, m, 11 - 11 * c, 1)], axis=0)
        hidden = hidden_of(left, w1_ref[0])
        outer = scaled_rows(hidden[0 : 5 * PAIRS].reshape(5, PAIRS, 512), group)
        h_ref[m, pl.ds(7 * c, 5)] = outer.astype(BF16)
        h_ref[m, 11 - 11 * c] = hidden[5 * PAIRS :].astype(BF16)

    def finish(layer, m, kept, step, factors):
        for row in range(0, kept, step):
            y = lax.dot_general(taps_of(h_ref, m, row, step), w2_ref[layer], NT, preferred_element_type=F32)
            own = y[:, 0:128].reshape(step, PAIRS, 128)
            side = y[:, 128:256].reshape(step, PAIRS, 128)
            lower = lax.broadcasted_iota(jnp.int32, side.shape, 2) < 64
            total = x_ref[row + 2 : row + 2 + step, m].astype(F32) + own + beside(side, lower)[1]
            total = scaled_rows(total, {i - row: f for i, f in factors.items() if row <= i < row + step})
            x_ref[row : row + step, m] = total.astype(BF16)

    edges = {**{i: first for i in range(3)}, **{i: last for i in range(7, 10)}}
    for m in range(2):
        finish(0, m, 10, 5, edges)
    for m in range(2):
        for row in (0, 5):
            patches(a_ref, m, row, x_ref[row : row + 5, m], norm)
        for row, factors in ((0, {0: first, 1: first}), (4, {2: last, 3: last})):
            hidden = hidden_of(taps_of(a_ref, m, row, 4), w1_ref[1]).reshape(4, PAIRS, 512)
            h_ref[m, row : row + 4] = scaled_rows(hidden, factors).astype(BF16)
    seen = []
    for m in range(2):
        finish(1, m, 6, 3, {0: first, 5: last})
        patches(a_ref, m, 0, x_ref[0:6, m], None)
        y = lax.dot_general(obs_ref[...], a_ref[m, 0:6].reshape(384, 256), NT, preferred_element_type=F32)
        whole = jnp.concatenate([y[16 * dr : 16 * dr + 16] for dr in range(3)], axis=1)
        high = whole.astype(BF16).astype(F32)
        both = jnp.concatenate([high, whole - high], axis=0).astype(BF16)
        picked = jnp.dot(both, pick_ref[...], preferred_element_type=F32)
        seen.append(picked[0:16] + picked[16:32])
    odd = sides_ref[16:24] > 0.5
    got = jnp.concatenate([jnp.where(odd, y[8:16], y[0:8]) for y in seen], axis=0).astype(BF16)
    for m in range(2):
        for r in range(4):
            flat[pl.ds(256 * m + r, PAIRS, stride=4), :] = x_ref[1 + r, m].astype(F32)
    for p in range(PEERS):
        both = jnp.concatenate([flat[8 * p : 8 * p + 8], flat[256 + 8 * p : 256 + 8 * p + 8]], axis=0)
        pay_ref[p, 0:16] = both.astype(BF16)
        pay_ref[p, 16:32] = got


def gram_kernel(got_ref, sides_ref, out_ref, flat):
    for p in range(PEERS):
        flat[16 * p : 16 * p + 16] = got_ref[p, 16:32].astype(F32)
    shape = (64, 128)
    left, right = [], []
    for o in range(8):
        members = flat[pl.ds(o, 64, stride=8), :]
        mean = jnp.sum(members, axis=0, keepdims=True) * (1.0 / 64)
        left.append((members - mean) * jnp.broadcast_to(sides_ref[8 + o : 9 + o], shape))
        right.append(jnp.broadcast_to(sides_ref[o : o + 1], shape) - members)
    left = jnp.concatenate(left, axis=1)
    right = jnp.concatenate(right, axis=1)
    none = jnp.zeros_like(right)
    total = lax.dot_general(
        left[0:32], jnp.concatenate([right, none], axis=0), NT, precision=lax.Precision.HIGHEST,
        preferred_element_type=F32,
    ) + lax.dot_general(
        left[32:64], jnp.concatenate([none, right], axis=0), NT, precision=lax.Precision.HIGHEST,
        preferred_element_type=F32,
    )
    for t in range(16):
        out_ref[t] = total.astype(BF16)


def update_kernel(got_ref, parts_ref, covariance_ref, back_ref, flat):
    total = parts_ref[0].astype(F32)
    for t in range(1, 16):
        total = total + parts_ref[t].astype(F32)
    total = total * (1.0 / 16384)
    covariance = jnp.concatenate([total[:, 0:64], total[:, 64:128]], axis=0)
    covariance_ref[...] = covariance
    center = (covariance - jnp.mean(covariance, axis=0, keepdims=True)) * STEP
    high = center.astype(BF16)
    both = jnp.concatenate([high, (center - high.astype(F32)).astype(BF16)], axis=0)
    for p in range(PEERS):
        flat[16 * p : 16 * p + 16] = got_ref[p, 0:16].astype(F32)
    for s in range(8):
        members = flat[pl.ds(s, 64, stride=8), :]
        narrow = members.astype(BF16)
        moved = lax.dot_general(both, jnp.concatenate([narrow, narrow], axis=0), TN, preferred_element_type=F32)
        flat[pl.ds(s, 64, stride=8), :] = members + moved
    for p in range(PEERS):
        back_ref[p] = flat[16 * p : 16 * p + 16].astype(BF16)


def final_kernel(got_ref, out_ref):
    for p in range(PEERS):
        values = got_ref[p].astype(F32)
        for m in range(2):
            for t in range(2):
                at = 128 * (2 * p + t)
                out_ref[m, :, at : at + 128] = values[8 * m + 4 * t : 8 * m + 4 * t + 4]


def per_device(latents, in_weight, out_weight, observe_weight, obs_cells, obs_values, obs_precision):
    c = lax.axis_index("c")
    across = [pair for z in range(7) for pair in ((2 * z + 1, 2 * z + 2), (2 * z + 2, 2 * z + 1))]
    vmem = pl.BlockSpec(memory_space=pltpu.VMEM)
    hbm = pl.BlockSpec(memory_space=pltpu.HBM)
    rows = kernel_call(
        rows_kernel, shaped((4, 2, PAIRS, 128)), [pltpu.VMEM((512, 128), F32)], moved=300_000,
    )(latents)
    chip = lax.all_gather(rows, "c", axis=0, tiled=True)
    outer = lax.ppermute(lax.dynamic_slice_in_dim(chip, 3 * c, 5, axis=0), TILE, across)
    a_part, h_part, first, second, obs, pick, sides = pl.pallas_call(
        inner_kernel,
        out_shape=(
            shaped((2, 8, PAIRS, 256)), shaped((2, 6, PAIRS, 512)), shaped((2, 768, 512)), shaped((2, 256, 1536)),
            shaped((48, 256)), shaped((1152, 128)), shaped((24, 128), F32),
        ),
        in_specs=[vmem] + [hbm] * 6,
        scratch_shapes=[
            pltpu.VMEM((2, 576, 256), BF16), pltpu.VMEM((2, 64, 2304), BF16), pltpu.VMEM((8, 576), BF16),
            pltpu.VMEM((4, 32), jnp.int32), pltpu.VMEM((4, 256), F32), pltpu.VMEM((4, 256), F32),
            pltpu.SemaphoreType.DMA((6,)),
        ],
        cost_estimate=pl.CostEstimate(flops=1_000_000_000, bytes_accessed=6_000_000, transcendentals=0),
        compiler_params=pltpu.CompilerParams(vmem_limit_bytes=16 * 1024 * 1024),
    )(chip, *(pltpu.with_memory_space_constraint(v, pltpu.HBM) for v in (
        in_weight, jnp.transpose(out_weight, (0, 2, 1)), jnp.transpose(observe_weight), obs_cells, obs_values,
        obs_precision,
    )))
    edge = lax.all_gather(lax.dynamic_slice_in_dim(outer, 4 * (1 - c), 1, axis=0), "c", axis=0, tiled=True)
    pay = kernel_call(
        denoise_kernel,
        shaped((PEERS, 32, 128)),
        [
            pltpu.VMEM((14, 2, PAIRS, 128), BF16),
            pltpu.VMEM((2, 14, PAIRS, 256), BF16),
            pltpu.VMEM((2, 12, PAIRS, 512), BF16),
            pltpu.VMEM((512, 128), F32),
            pltpu.SemaphoreType.DMA((5,)),
        ],
        flops=4_000_000_000, moved=4_300_000,
    )(chip, outer, edge, a_part, h_part, first, second, obs, pick, sides)
    got = lax.all_to_all(pay, MEM, 0, 0, tiled=True)

    parts = kernel_call(
        gram_kernel, shaped((16, 32, 128)), [pltpu.VMEM((512, 128), F32)], moved=700_000,
    )(got, sides)
    parts = lax.all_to_all(parts, TILE, 0, 0, tiled=True)
    covariance, back = kernel_call(
        update_kernel, (shaped((64, 64), F32), shaped((PEERS, 16, 128))), [pltpu.VMEM((512, 128), F32)],
        moved=700_000,
    )(got, parts)
    back = lax.all_to_all(back, MEM, 0, 0, tiled=True)
    analysis = kernel_call(final_kernel, shaped((2, 4, 8192), F32), moved=400_000)(back)
    return analysis, covariance


def solution(mesh):
    split = Mesh(mesh.devices.reshape(8, 4, 8, 2), ("y", "x", "z", "c"))
    return jax.shard_map(
        per_device,
        mesh=split,
        in_specs=(P(MEM, TILE, None), P(), P(), P(), P(TILE, None), P(TILE, None), P(TILE, None)),
        out_specs=(P(MEM, TILE, None), P()),
        check_vma=False,
    )
```

```python
import functools

import jax
import jax.numpy as jnp
from jax import lax
from jax.experimental import pallas as pl
from jax.experimental.pallas import tpu as pltpu
from jax.sharding import Mesh
from jax.sharding import PartitionSpec as P

MEM = ("y", "x")
TILE = ("z", "c")
PAIRS = 64
HID = 256
PEERS = 32
EPS = 1e-06
STEP = 0.5
F32 = jnp.float32
BF16 = jnp.bfloat16
LIMIT = 24 * 1024 * 1024
NT = (((1,), (1,)), ((), ()))
TN = (((0,), (0,)), ((), ()))
BLOCKS = (0, 1, 2, -1)


def kernel_call(body, outs, scratch=(), flops=0, moved=0, limit=LIMIT):
    return pl.pallas_call(
        body,
        out_shape=outs,
        scratch_shapes=scratch,
        cost_estimate=pl.CostEstimate(flops=flops, bytes_accessed=moved, transcendentals=0),
        compiler_params=pltpu.CompilerParams(vmem_limit_bytes=limit),
    )


def shaped(shape, dtype=BF16):
    return jax.ShapeDtypeStruct(shape, dtype)


def rows_kernel(x_ref, chip_ref, five_ref, one_ref, flat):
    c = lax.axis_index("c")
    for k in range(2):
        for m in range(2):
            for t in range(PAIRS):
                flat[256 * m + 4 * t : 256 * m + 4 * t + 4, :] = x_ref[k, m, :, 128 * t : 128 * t + 128].astype(F32)
        for m in range(2):
            for r in range(4):
                chip_ref[4 * k + r, m] = flat[pl.ds(256 * m + r, PAIRS, stride=4), :].astype(BF16)
    five_ref[...] = chip_ref[pl.ds(3 * c, 5)]
    one_ref[...] = chip_ref[7 * c]


def spread_weights(in_ref, out_ref, seen_ref, first_ref, second_ref, obs_ref):
    first_ref[...] = jnp.zeros_like(first_ref)
    second_ref[...] = jnp.zeros_like(second_ref)
    for layer in range(2):
        for dr in range(3):
            for b, j in enumerate(BLOCKS):
                for h in range(2):
                    dc = j - h + 1
                    if 0 <= dc <= 2:
                        at = 64 * (3 * dr + dc)
                        first_ref[layer, 256 * dr + 64 * b : 256 * dr + 64 * b + 64, 256 * h : 256 * h + 256] = (
                            in_ref[layer, at : at + 64, :] * jnp.asarray(0.5, BF16)
                        )
                    dc = h - j + 1
                    if 0 <= dc <= 2:
                        at = 256 * (3 * dr + dc)
                        second_ref[layer, 64 * b : 64 * b + 64, 512 * dr + 256 * h : 512 * dr + 256 * h + 256] = (
                            out_ref[layer, :, at : at + 256]
                        )
    taps = seen_ref[...].astype(F32)
    none = jnp.zeros((8, 64), F32)
    rows = []
    for dr in range(3):
        for h in range(2):
            blocks = [j - h + 1 for j in BLOCKS]
            rows.append(jnp.concatenate(
                [taps[:, 64 * (3 * dr + dc) : 64 * (3 * dr + dc) + 64] if 0 <= dc <= 2 else none for dc in blocks],
                axis=1,
            ))
    obs_ref[...] = jnp.concatenate(rows, axis=0).astype(BF16)


def beside(values, lower):
    at = lax.broadcasted_iota(jnp.int32, values.shape, 1)
    after = jnp.where(at == PAIRS - 1, 0.0, pltpu.roll(values, PAIRS - 1, 1))
    before = jnp.where(at == 0, 0.0, pltpu.roll(values, 1, 1))
    return jnp.where(lower, after, before), jnp.where(lower, before, after)


def mean_over_channels():
    return jnp.where(
        (lax.broadcasted_iota(jnp.int32, (128, 128), 0) < 64) == (lax.broadcasted_iota(jnp.int32, (128, 128), 1) < 64),
        1.0 / 64, 0.0,
    ).astype(BF16)


def patches(a_ref, m, row, values, norm):
    count = values.shape[0]
    wide = values.astype(F32)
    lower = lax.broadcasted_iota(jnp.int32, wide.shape, 2) < 64
    if norm is not None:
        square = (values * values).reshape(count * PAIRS, 128)
        mean = jnp.dot(square, norm, preferred_element_type=F32).reshape(count, PAIRS, 128)
        wide = wide * lax.rsqrt(mean + EPS)
    a_ref[m, pl.ds(row, count), :, 0:128] = wide.astype(BF16)
    a_ref[m, pl.ds(row, count), :, 128:256] = beside(wide, lower)[0].astype(BF16)


def taps_of(ref, m, row, count):
    width = ref.shape[3]
    return jnp.concatenate(
        [ref[m, pl.ds(row + dr, count)].reshape(count * PAIRS, width) for dr in range(3)], axis=1
    )


def hidden_of(left, weight):
    v = jnp.dot(left, weight, preferred_element_type=F32)
    return v + v * jnp.tanh(v)


def scaled_rows(values, factors):
    return jnp.concatenate(
        [values[i : i + 1] * factors[i] if i in factors else values[i : i + 1] for i in range(values.shape[0])], axis=0
    )


def updated(left, weight, current):
    count = current.shape[0]
    y = lax.dot_general(left, weight, NT, preferred_element_type=F32)
    own = y[:, 0:128].reshape(count, PAIRS, 128)
    side = y[:, 128:256].reshape(count, PAIRS, 128)
    lower = lax.broadcasted_iota(jnp.int32, side.shape, 2) < 64
    return current.astype(F32) + own + beside(side, lower)[1]


def by_channel(values_ref, precision_ref, sides_ref):
    own = lax.broadcasted_iota(jnp.int32, (8, 256), 1) % 8 == lax.broadcasted_iota(jnp.int32, (8, 256), 0)
    spread = [
        jnp.concatenate(
            [jnp.where(own, jnp.broadcast_to(ref[r : r + 1, :], (8, 256)), 0.0) for r in range(4)], axis=1
        )
        for ref in (values_ref, precision_ref)
    ]
    whole = jnp.concatenate(spread, axis=0)
    at = lax.broadcasted_iota(jnp.int32, (1024, 128), 0)
    place = jnp.where(at // 8 == lax.broadcasted_iota(jnp.int32, (1024, 128), 1), 1.0, 0.0).astype(BF16)
    high = whole.astype(BF16)
    rest = whole - high.astype(F32)
    middle = rest.astype(BF16)
    low = (rest - middle.astype(F32)).astype(BF16)
    placed = jnp.dot(jnp.concatenate([high, middle, low], axis=0), place, preferred_element_type=F32)
    sides_ref[0:16] = placed[0:16] + placed[16:32] + placed[32:48]


def inner_kernel(chip_ref, in_hbm, out_hbm, seen_hbm, cells_hbm, values_hbm, precision_hbm,
                 a_ref, h_ref, x1_ref, a2_ref, h2_ref, w1_ref, w2_ref, obs_ref, pick_ref, sides_ref,
                 in_ref, out_ref, seen_ref, cells_ref, values_ref, precision_ref, sems):
    sources = (cells_hbm, values_hbm, precision_hbm, seen_hbm, in_hbm, out_hbm)
    targets = (cells_ref, values_ref, precision_ref, seen_ref, in_ref, out_ref)
    fetches = [pltpu.make_async_copy(a, b, sems.at[i]) for i, (a, b) in enumerate(zip(sources, targets))]
    for fetch in fetches:
        fetch.start()
    norm = mean_over_channels()
    for m in range(2):
        for row in (0, 4):
            patches(a_ref, m, row, chip_ref[row : row + 4, m], norm)
    for fetch in fetches[:3]:
        fetch.wait()
    by_channel(values_ref, precision_ref, sides_ref)
    cell = jnp.concatenate([cells_ref[r : r + 1, :] for r in range(4)], axis=1)
    pair = lax.shift_right_logical(cell, 1)
    lane_row = lax.broadcasted_iota(jnp.int32, (1, 128), 1) // 32
    index = lax.broadcasted_iota(jnp.int32, (384, 128), 0)
    for dr in range(3):
        pick_ref[384 * dr : 384 * dr + 384, :] = jnp.where(index == (lane_row + dr) * PAIRS + pair, 1.0, 0.0).astype(BF16)
    sides_ref[16:24] = jnp.broadcast_to((cell & 1).astype(F32), (8, 128))
    for fetch in fetches[3:]:
        fetch.wait()
    spread_weights(in_ref, out_ref, seen_ref, w1_ref, w2_ref, obs_ref)
    for m in range(2):
        for row in (0, 3):
            hidden = hidden_of(taps_of(a_ref, m, row, 3), w1_ref[0])
            h_ref[m, row : row + 3] = hidden.astype(BF16).reshape(3, PAIRS, 512)
    for m in range(2):
        x1_ref[:, m] = updated(taps_of(h_ref, m, 0, 4), w2_ref[0], chip_ref[2:6, m]).astype(BF16)
        patches(a2_ref, m, 0, x1_ref[:, m], norm)
    for m in range(2):
        h2_ref[m] = hidden_of(taps_of(a2_ref, m, 0, 2), w1_ref[1]).astype(BF16).reshape(2, PAIRS, 512)


def denoise_kernel(chip_ref, five_ref, one_ref, a_part, h_part, x1_part, a2_part, h2_part, w1_ref, w2_ref, obs_ref,
                   pick_ref, sides_ref, pay_ref, x_ref, a_ref, h_ref, x1_ref, a2_ref, h2_ref, x2_ref, flat, sems):
    c = lax.axis_index("c")
    tile = 2 * lax.axis_index("z") + c
    first = jnp.where(tile == 0, 0.0, 1.0).astype(F32)
    last = jnp.where(tile == 15, 0.0, 1.0).astype(F32)
    start = 5 - 4 * c
    pairs = [(chip_ref, x_ref.at[pl.ds(start, 8)]), (x1_part, x1_ref.at[pl.ds(start, 4)])]
    for m in range(2):
        for k in (0, 6):
            pairs.append((a_part.at[m, pl.ds(k, 2)], a_ref.at[m, pl.ds(start + k, 2)]))
        for k in (0, 4):
            pairs.append((h_part.at[m, pl.ds(k, 2)], h_ref.at[m, pl.ds(start + k, 2)]))
        pairs.append((a2_part.at[m], a2_ref.at[m, pl.ds(start, 4)]))
        pairs.append((h2_part.at[m], h2_ref.at[m, pl.ds(start, 2)]))
    moves = [pltpu.make_async_copy(source, target, sems.at[i]) for i, (source, target) in enumerate(pairs)]
    for move in moves:
        move.start()
    norm = mean_over_channels()
    for m in range(2):
        patches(a_ref, m, 9 * c, five_ref[:, m], norm)
        patches(a_ref, m, 13 - 13 * c, one_ref[m : m + 1], norm)
    x_ref[pl.ds(9 * c, 5)] = five_ref[...]
    x_ref[13 - 13 * c] = one_ref[...]
    for move in moves:
        move.wait()

    def edges(low, high):
        group = {}
        for q in range(5):
            if q < low or q >= high:
                group[q] = jnp.where(c == 1, last if q >= high else 1.0, first if q < low else 1.0)
        return group

    def split(values, factors):
        width = values.shape[1]
        rows = values.reshape(6, PAIRS, width)
        return scaled_rows(rows[0:5], factors).astype(BF16), rows[5].astype(BF16)

    for m in range(2):
        left = jnp.concatenate([taps_of(a_ref, m, 7 * c, 5), taps_of(a_ref, m, 11 - 11 * c, 1)], axis=0)
        h_ref[m, pl.ds(7 * c, 5)], h_ref[m, 11 - 11 * c] = split(hidden_of(left, w1_ref[0]), edges(4, 1))
    for m in range(2):
        left = jnp.concatenate([taps_of(h_ref, m, 5 * c, 5), taps_of(h_ref, m, 9 - 9 * c, 1)], axis=0)
        current = jnp.concatenate([x_ref[pl.ds(5 * c + 2, 5), m], x_ref[pl.ds(11 - 9 * c, 1), m]], axis=0)
        group, single = split(updated(left, w2_ref[0], current).reshape(6 * PAIRS, 128), edges(3, 2))
        x1_ref[pl.ds(5 * c, 5), m] = group
        x1_ref[9 - 9 * c, m] = single
        patches(a2_ref, m, 5 * c, group, norm)
        patches(a2_ref, m, 9 - 9 * c, single[None], norm)
    for m in range(2):
        left = jnp.concatenate([taps_of(a2_ref, m, 3 * c, 5), taps_of(a2_ref, m, 7 - 7 * c, 1)], axis=0)
        h2_ref[m, pl.ds(3 * c, 5)], h2_ref[m, 7 - 7 * c] = split(hidden_of(left, w1_ref[1]), edges(2, 3))
    seen = []
    for m in range(2):
        for row, factors in ((0, {0: first}), (3, {2: last})):
            rows = updated(taps_of(h2_ref, m, row, 3), w2_ref[1], x1_ref[row + 2 : row + 5, m])
            x2_ref[row : row + 3, m] = scaled_rows(rows, factors).astype(BF16)
        patches(a_ref, m, 0, x2_ref[:, m], None)
        y = lax.dot_general(obs_ref[...], a_ref[m, 0:6].reshape(384, 256), NT, preferred_element_type=F32)
        whole = jnp.concatenate([y[16 * dr : 16 * dr + 16] for dr in range(3)], axis=1)
        high = whole.astype(BF16).astype(F32)
        both = jnp.concatenate([high, whole - high], axis=0).astype(BF16)
        picked = jnp.dot(both, pick_ref[...], preferred_element_type=F32)
        seen.append(picked[0:16] + picked[16:32])
    odd = sides_ref[16:24] > 0.5
    got = jnp.concatenate([jnp.where(odd, y[8:16], y[0:8]) for y in seen], axis=0).astype(BF16)
    for m in range(2):
        for r in range(4):
            flat[pl.ds(256 * m + r, PAIRS, stride=4), :] = x2_ref[1 + r, m].astype(F32)
    for p in range(PEERS):
        both = jnp.concatenate([flat[8 * p : 8 * p + 8], flat[256 + 8 * p : 256 + 8 * p + 8]], axis=0)
        pay_ref[p, 0:16] = both.astype(BF16)
        pay_ref[p, 16:32] = got


def gram_kernel(got_ref, sides_ref, out_ref, flat):
    for p in range(PEERS):
        flat[16 * p : 16 * p + 16] = got_ref[p, 16:32].astype(F32)
    shape = (64, 128)
    left, right, values = [], [], []
    for o in range(8):
        members = flat[pl.ds(o, 64, stride=8), :]
        mean = jnp.sum(members, axis=0, keepdims=True) * (1.0 / 64)
        left.append((members - mean) * jnp.broadcast_to(sides_ref[8 + o : 9 + o], shape))
        right.append(members.astype(BF16))
        values.append(left[-1] * jnp.broadcast_to(sides_ref[o : o + 1], shape))
    offset = jnp.sum(functools.reduce(jnp.add, values), axis=1, keepdims=True)
    left = jnp.concatenate(left, axis=1)
    right = jnp.concatenate(right, axis=1)
    high = left.astype(BF16)
    halves = jnp.concatenate([high, (left - high.astype(F32)).astype(BF16)], axis=0)
    product = lax.dot_general(halves, jnp.concatenate([right, right], axis=0), NT, preferred_element_type=F32)
    total = offset - (product[0:64] + product[64:128])
    lower = lax.broadcasted_iota(jnp.int32, (32, 128), 1) < 64
    packed = jnp.where(lower, total[0:32], total[32:64]).astype(BF16)
    for t in range(16):
        out_ref[t] = packed


def update_kernel(got_ref, parts_ref, covariance_ref, back_ref, flat):
    total = parts_ref[0].astype(F32)
    for t in range(1, 16):
        total = total + parts_ref[t].astype(F32)
    total = total * (1.0 / 16384)
    covariance = jnp.concatenate([total[:, 0:64], total[:, 64:128]], axis=0)
    covariance_ref[...] = covariance
    center = (covariance - jnp.mean(covariance, axis=0, keepdims=True)) * STEP
    high = center.astype(BF16)
    both = jnp.concatenate([high, (center - high.astype(F32)).astype(BF16)], axis=0)
    for p in range(PEERS):
        flat[16 * p : 16 * p + 16] = got_ref[p, 0:16].astype(F32)
    for s in range(8):
        members = flat[pl.ds(s, 64, stride=8), :]
        narrow = members.astype(BF16)
        moved = lax.dot_general(both, jnp.concatenate([narrow, narrow], axis=0), TN, preferred_element_type=F32)
        flat[pl.ds(s, 64, stride=8), :] = members + moved
    for p in range(PEERS):
        back_ref[p] = flat[16 * p : 16 * p + 16].astype(BF16)


def final_kernel(got_ref, out_ref):
    for p in range(PEERS):
        values = got_ref[p].astype(F32)
        for m in range(2):
            for t in range(2):
                at = 128 * (2 * p + t)
                out_ref[m, :, at : at + 128] = values[8 * m + 4 * t : 8 * m + 4 * t + 4]


def per_device(latents, in_weight, out_weight, observe_weight, obs_cells, obs_values, obs_precision):
    across = [pair for z in range(7) for pair in ((2 * z + 1, 2 * z + 2), (2 * z + 2, 2 * z + 1))]
    along = [pair for z in range(7) for pair in ((2 * z + 1, 2 * z + 3), (2 * z + 2, 2 * z))]
    vmem = pl.BlockSpec(memory_space=pltpu.VMEM)
    hbm = pl.BlockSpec(memory_space=pltpu.HBM)
    chip, five, one = kernel_call(
        rows_kernel, (shaped((8, 2, PAIRS, 128)), shaped((5, 2, PAIRS, 128)), shaped((2, PAIRS, 128))),
        [pltpu.VMEM((512, 128), F32)], moved=300_000,
    )(lax.all_gather(latents, "c"))
    five = lax.ppermute(five, TILE, across)
    one = lax.ppermute(one, TILE, along)
    *parts, sides = pl.pallas_call(
        inner_kernel,
        out_shape=(
            shaped((2, 8, PAIRS, 256)), shaped((2, 6, PAIRS, 512)), shaped((4, 2, PAIRS, 128)),
            shaped((2, 4, PAIRS, 256)), shaped((2, 2, PAIRS, 512)), shaped((2, 768, 512)), shaped((2, 256, 1536)),
            shaped((48, 256)), shaped((1152, 128)), shaped((24, 128), F32),
        ),
        in_specs=[vmem] + [hbm] * 6,
        scratch_shapes=[
            pltpu.VMEM((2, 576, 256), BF16), pltpu.VMEM((2, 64, 2304), BF16), pltpu.VMEM((8, 576), BF16),
            pltpu.VMEM((4, 32), jnp.int32), pltpu.VMEM((4, 256), F32), pltpu.VMEM((4, 256), F32),
            pltpu.SemaphoreType.DMA((6,)),
        ],
        cost_estimate=pl.CostEstimate(flops=2_000_000_000, bytes_accessed=6_000_000, transcendentals=0),
        compiler_params=pltpu.CompilerParams(vmem_limit_bytes=16 * 1024 * 1024),
    )(chip, *(pltpu.with_memory_space_constraint(v, pltpu.HBM) for v in (
        in_weight, jnp.transpose(out_weight, (0, 2, 1)), jnp.transpose(observe_weight), obs_cells, obs_values,
        obs_precision,
    )))
    pay = kernel_call(
        denoise_kernel,
        shaped((PEERS, 32, 128)),
        [
            pltpu.VMEM((14, 2, PAIRS, 128), BF16),
            pltpu.VMEM((2, 14, PAIRS, 256), BF16),
            pltpu.VMEM((2, 12, PAIRS, 512), BF16),
            pltpu.VMEM((10, 2, PAIRS, 128), BF16),
            pltpu.VMEM((2, 10, PAIRS, 256), BF16),
            pltpu.VMEM((2, 8, PAIRS, 512), BF16),
            pltpu.VMEM((6, 2, PAIRS, 128), BF16),
            pltpu.VMEM((512, 128), F32),
            pltpu.SemaphoreType.DMA((14,)),
        ],
        flops=3_000_000_000, moved=4_300_000,
    )(chip, five, one, *parts, sides)
    got = lax.all_to_all(pay, MEM, 0, 0, tiled=True)

    parts = kernel_call(
        gram_kernel, shaped((16, 32, 128)), [pltpu.VMEM((512, 128), F32)], moved=700_000,
    )(got, sides)
    parts = lax.all_to_all(parts, TILE, 0, 0, tiled=True)
    covariance, back = kernel_call(
        update_kernel, (shaped((64, 64), F32), shaped((PEERS, 16, 128))), [pltpu.VMEM((512, 128), F32)],
        moved=700_000,
    )(got, parts)
    back = lax.all_to_all(back, MEM, 0, 0, tiled=True)
    analysis = kernel_call(final_kernel, shaped((2, 4, 8192), F32), moved=400_000)(back)
    return analysis, covariance


def solution(mesh):
    split = Mesh(mesh.devices.reshape(8, 4, 8, 2), ("y", "x", "z", "c"))
    return jax.shard_map(
        per_device,
        mesh=split,
        in_specs=(P(MEM, TILE, None), P(), P(), P(), P(TILE, None), P(TILE, None), P(TILE, None)),
        out_specs=(P(MEM, TILE, None), P()),
        check_vma=False,
    )
```

```python
import functools

import jax
import jax.numpy as jnp
from jax import lax
from jax.experimental import pallas as pl
from jax.experimental.pallas import tpu as pltpu
from jax.sharding import Mesh
from jax.sharding import PartitionSpec as P

MEM = ("y", "x")
TILE = ("z", "c")
PAIRS = 64
HID = 256
PEERS = 32
EPS = 1e-06
STEP = 0.5
F32 = jnp.float32
BF16 = jnp.bfloat16
LIMIT = 24 * 1024 * 1024
NT = (((1,), (1,)), ((), ()))
TN = (((0,), (0,)), ((), ()))
BLOCKS = (0, 1, 2, -1)


def kernel_call(body, outs, scratch=(), flops=0, moved=0, limit=LIMIT):
    return pl.pallas_call(
        body,
        out_shape=outs,
        scratch_shapes=scratch,
        cost_estimate=pl.CostEstimate(flops=flops, bytes_accessed=moved, transcendentals=0),
        compiler_params=pltpu.CompilerParams(vmem_limit_bytes=limit),
    )


def shaped(shape, dtype=BF16):
    return jax.ShapeDtypeStruct(shape, dtype)


def rows_kernel(x_ref, chip_ref, five_ref, flat):
    c = lax.axis_index("c")
    for k in range(2):
        for m in range(2):
            for t in range(PAIRS):
                flat[256 * m + 4 * t : 256 * m + 4 * t + 4, :] = x_ref[k, m, :, 128 * t : 128 * t + 128].astype(F32)
        for m in range(2):
            for r in range(4):
                chip_ref[4 * k + r, m] = flat[pl.ds(256 * m + r, PAIRS, stride=4), :].astype(BF16)
    five_ref[...] = chip_ref[pl.ds(3 * c, 5)]


def spread_weights(in_ref, out_ref, seen_ref, first_ref, second_ref, obs_ref):
    first_ref[...] = jnp.zeros_like(first_ref)
    second_ref[...] = jnp.zeros_like(second_ref)
    for layer in range(2):
        for dr in range(3):
            for b, j in enumerate(BLOCKS):
                for h in range(2):
                    dc = j - h + 1
                    if 0 <= dc <= 2:
                        at = 64 * (3 * dr + dc)
                        first_ref[layer, 256 * dr + 64 * b : 256 * dr + 64 * b + 64, 256 * h : 256 * h + 256] = (
                            in_ref[layer, at : at + 64, :] * jnp.asarray(0.5, BF16)
                        )
                    dc = h - j + 1
                    if 0 <= dc <= 2:
                        at = 256 * (3 * dr + dc)
                        second_ref[layer, 64 * b : 64 * b + 64, 512 * dr + 256 * h : 512 * dr + 256 * h + 256] = (
                            out_ref[layer, :, at : at + 256]
                        )
    taps = seen_ref[...].astype(F32)
    none = jnp.zeros((8, 64), F32)
    rows = []
    for dr in range(3):
        for h in range(2):
            blocks = [j - h + 1 for j in BLOCKS]
            rows.append(jnp.concatenate(
                [taps[:, 64 * (3 * dr + dc) : 64 * (3 * dr + dc) + 64] if 0 <= dc <= 2 else none for dc in blocks],
                axis=1,
            ))
    obs_ref[...] = jnp.concatenate(rows, axis=0).astype(BF16)


def beside(values, lower):
    at = lax.broadcasted_iota(jnp.int32, values.shape, 1)
    after = jnp.where(at == PAIRS - 1, 0.0, pltpu.roll(values, PAIRS - 1, 1))
    before = jnp.where(at == 0, 0.0, pltpu.roll(values, 1, 1))
    return jnp.where(lower, after, before), jnp.where(lower, before, after)


def mean_over_channels():
    return jnp.where(
        (lax.broadcasted_iota(jnp.int32, (128, 128), 0) < 64) == (lax.broadcasted_iota(jnp.int32, (128, 128), 1) < 64),
        1.0 / 64, 0.0,
    ).astype(BF16)


def patches(a_ref, m, row, values, norm):
    count = values.shape[0]
    wide = values.astype(F32)
    lower = lax.broadcasted_iota(jnp.int32, wide.shape, 2) < 64
    if norm is not None:
        square = (values * values).reshape(count * PAIRS, 128)
        mean = jnp.dot(square, norm, preferred_element_type=F32).reshape(count, PAIRS, 128)
        wide = wide * lax.rsqrt(mean + EPS)
    a_ref[m, pl.ds(row, count), :, 0:128] = wide.astype(BF16)
    a_ref[m, pl.ds(row, count), :, 128:256] = beside(wide, lower)[0].astype(BF16)


def taps_of(ref, m, row, count):
    width = ref.shape[3]
    return jnp.concatenate(
        [ref[m, pl.ds(row + dr, count)].reshape(count * PAIRS, width) for dr in range(3)], axis=1
    )


def hidden_of(left, weight):
    v = jnp.dot(left, weight, preferred_element_type=F32)
    return v + v * jnp.tanh(v)


def scaled_rows(values, factors):
    return jnp.concatenate(
        [values[i : i + 1] * factors[i] if i in factors else values[i : i + 1] for i in range(values.shape[0])], axis=0
    )


def second(left, weight):
    half = left.shape[1] // 2
    return [lax.dot_general(left[:, k : k + half], weight[:, k : k + half], NT, preferred_element_type=F32) for k in (0, half)]


def updated(products, current):
    count = current.shape[0]
    y = products[0] + products[1]
    own = y[:, 0:128].reshape(count, PAIRS, 128)
    side = y[:, 128:256].reshape(count, PAIRS, 128)
    lower = lax.broadcasted_iota(jnp.int32, side.shape, 2) < 64
    return current.astype(F32) + own + beside(side, lower)[1]


def by_channel(values_ref, precision_ref, sides_ref):
    own = lax.broadcasted_iota(jnp.int32, (8, 256), 1) % 8 == lax.broadcasted_iota(jnp.int32, (8, 256), 0)
    spread = [
        jnp.concatenate(
            [jnp.where(own, jnp.broadcast_to(ref[r : r + 1, :], (8, 256)), 0.0) for r in range(4)], axis=1
        )
        for ref in (values_ref, precision_ref)
    ]
    whole = jnp.concatenate(spread, axis=0)
    at = lax.broadcasted_iota(jnp.int32, (1024, 128), 0)
    place = jnp.where(at // 8 == lax.broadcasted_iota(jnp.int32, (1024, 128), 1), 1.0, 0.0).astype(BF16)
    high = whole.astype(BF16)
    rest = whole - high.astype(F32)
    middle = rest.astype(BF16)
    low = (rest - middle.astype(F32)).astype(BF16)
    placed = jnp.dot(jnp.concatenate([high, middle, low], axis=0), place, preferred_element_type=F32)
    sides_ref[0:16] = placed[0:16] + placed[16:32] + placed[32:48]


def inner_kernel(chip_ref, in_hbm, out_hbm, seen_hbm, cells_hbm, values_hbm, precision_hbm,
                 a_ref, h_ref, x1_ref, a2_ref, h2_ref, w1_ref, w2_ref, obs_ref, pick_ref, sides_ref,
                 in_ref, out_ref, seen_ref, cells_ref, values_ref, precision_ref, sems):
    sources = (cells_hbm, values_hbm, precision_hbm, seen_hbm, in_hbm, out_hbm)
    targets = (cells_ref, values_ref, precision_ref, seen_ref, in_ref, out_ref)
    fetches = [pltpu.make_async_copy(a, b, sems.at[i]) for i, (a, b) in enumerate(zip(sources, targets))]
    for fetch in fetches:
        fetch.start()
    norm = mean_over_channels()
    for m in range(2):
        for row in (0, 4):
            patches(a_ref, m, row, chip_ref[row : row + 4, m], norm)
    for fetch in fetches[:3]:
        fetch.wait()
    by_channel(values_ref, precision_ref, sides_ref)
    cell = jnp.concatenate([cells_ref[r : r + 1, :] for r in range(4)], axis=1)
    pair = lax.shift_right_logical(cell, 1)
    lane_row = lax.broadcasted_iota(jnp.int32, (1, 128), 1) // 32
    index = lax.broadcasted_iota(jnp.int32, (384, 128), 0)
    for dr in range(3):
        pick_ref[384 * dr : 384 * dr + 384, :] = jnp.where(index == (lane_row + dr) * PAIRS + pair, 1.0, 0.0).astype(BF16)
    sides_ref[16:24] = jnp.broadcast_to((cell & 1).astype(F32), (8, 128))
    for fetch in fetches[3:]:
        fetch.wait()
    spread_weights(in_ref, out_ref, seen_ref, w1_ref, w2_ref, obs_ref)
    for m in range(2):
        for row in (0, 3):
            hidden = hidden_of(taps_of(a_ref, m, row, 3), w1_ref[0])
            h_ref[m, row : row + 3] = hidden.astype(BF16).reshape(3, PAIRS, 512)
    products = [second(taps_of(h_ref, m, 0, 4), w2_ref[0]) for m in range(2)]
    for m in range(2):
        x1_ref[:, m] = updated(products[m], chip_ref[2:6, m]).astype(BF16)
        patches(a2_ref, m, 0, x1_ref[:, m], norm)
    for m in range(2):
        h2_ref[m] = hidden_of(taps_of(a2_ref, m, 0, 2), w1_ref[1]).astype(BF16).reshape(2, PAIRS, 512)


def denoise_kernel(chip_ref, five_ref, one_ref, a_part, h_part, x1_part, a2_part, h2_part, w1_ref, w2_ref, obs_ref,
                   pick_ref, sides_ref, pay_ref, x_ref, a_ref, h_ref, x1_ref, a2_ref, h2_ref, x2_ref, flat):
    c = lax.axis_index("c")
    tile = 2 * lax.axis_index("z") + c
    first = jnp.where(tile == 0, 0.0, 1.0).astype(F32)
    last = jnp.where(tile == 15, 0.0, 1.0).astype(F32)
    start = 5 - 4 * c
    one = one_ref[1 - c]
    norm = mean_over_channels()
    for m in range(2):
        patches(a_ref, m, 9 * c, five_ref[:, m], norm)
        patches(a_ref, m, 13 - 13 * c, one[m : m + 1], norm)
        for k in (0, 6):
            a_ref[m, pl.ds(start + k, 2)] = a_part[m, k : k + 2]
        for k in (0, 4):
            h_ref[m, pl.ds(start + k, 2)] = h_part[m, k : k + 2]
        a2_ref[m, pl.ds(start, 4)] = a2_part[m]
        h2_ref[m, pl.ds(start, 2)] = h2_part[m]
    x_ref[pl.ds(start, 8)] = chip_ref[...]
    x1_ref[pl.ds(start, 4)] = x1_part[...]
    x_ref[pl.ds(9 * c, 5)] = five_ref[...]

    def edges(low, high):
        group = {}
        for q in range(5):
            if q < low or q >= high:
                group[q] = jnp.where(c == 1, last if q >= high else 1.0, first if q < low else 1.0)
        return group

    def split(values, factors):
        width = values.shape[1]
        rows = values.reshape(6, PAIRS, width)
        return scaled_rows(rows[0:5], factors).astype(BF16), rows[5].astype(BF16)

    for m in range(2):
        left = jnp.concatenate([taps_of(a_ref, m, 7 * c, 5), taps_of(a_ref, m, 11 - 11 * c, 1)], axis=0)
        h_ref[m, pl.ds(7 * c, 5)], h_ref[m, 11 - 11 * c] = split(hidden_of(left, w1_ref[0]), edges(4, 1))
    products = []
    for m in range(2):
        left = jnp.concatenate([taps_of(h_ref, m, 5 * c, 5), taps_of(h_ref, m, 9 - 9 * c, 1)], axis=0)
        products.append(second(left, w2_ref[0]))
    for m in range(2):
        current = jnp.concatenate([x_ref[pl.ds(5 * c + 2, 5), m], x_ref[pl.ds(11 - 9 * c, 1), m]], axis=0)
        group, single = split(updated(products[m], current).reshape(6 * PAIRS, 128), edges(3, 2))
        x1_ref[pl.ds(5 * c, 5), m] = group
        x1_ref[9 - 9 * c, m] = single
        patches(a2_ref, m, 5 * c, group, norm)
        patches(a2_ref, m, 9 - 9 * c, single[None], norm)
    for m in range(2):
        left = jnp.concatenate([taps_of(a2_ref, m, 3 * c, 5), taps_of(a2_ref, m, 7 - 7 * c, 1)], axis=0)
        h2_ref[m, pl.ds(3 * c, 5)], h2_ref[m, 7 - 7 * c] = split(hidden_of(left, w1_ref[1]), edges(2, 3))
    products = [second(taps_of(h2_ref, m, 0, 6), w2_ref[1]) for m in range(2)]
    seen = []
    for m in range(2):
        x2_ref[:, m] = scaled_rows(updated(products[m], x1_ref[2:8, m]), {0: first, 5: last}).astype(BF16)
        patches(a_ref, m, 0, x2_ref[:, m], None)
        y = lax.dot_general(obs_ref[...], a_ref[m, 0:6].reshape(384, 256), NT, preferred_element_type=F32)
        whole = jnp.concatenate([y[16 * dr : 16 * dr + 16] for dr in range(3)], axis=1)
        high = whole.astype(BF16).astype(F32)
        both = jnp.concatenate([high, whole - high], axis=0).astype(BF16)
        picked = jnp.dot(both, pick_ref[...], preferred_element_type=F32)
        seen.append(picked[0:16] + picked[16:32])
    odd = sides_ref[16:24] > 0.5
    got = jnp.concatenate([jnp.where(odd, y[8:16], y[0:8]) for y in seen], axis=0).astype(BF16)
    for m in range(2):
        for r in range(4):
            flat[pl.ds(256 * m + r, PAIRS, stride=4), :] = x2_ref[1 + r, m].astype(F32)
    for p in range(PEERS):
        both = jnp.concatenate([flat[8 * p : 8 * p + 8], flat[256 + 8 * p : 256 + 8 * p + 8]], axis=0)
        pay_ref[p, 0:16] = both.astype(BF16)
        pay_ref[p, 16:32] = got


def gram_kernel(got_ref, sides_ref, out_ref, flat):
    for p in range(PEERS):
        flat[16 * p : 16 * p + 16] = got_ref[p, 16:32].astype(F32)
    shape = (64, 128)
    left, right, values = [], [], []
    for o in range(8):
        members = flat[pl.ds(o, 64, stride=8), :]
        mean = jnp.sum(members, axis=0, keepdims=True) * (1.0 / 64)
        left.append((members - mean) * jnp.broadcast_to(sides_ref[8 + o : 9 + o], shape))
        right.append(members.astype(BF16))
        values.append(left[-1] * jnp.broadcast_to(sides_ref[o : o + 1], shape))
    offset = jnp.sum(functools.reduce(jnp.add, values), axis=1, keepdims=True)
    left = jnp.concatenate(left, axis=1)
    right = jnp.concatenate(right, axis=1)
    high = left.astype(BF16)
    halves = jnp.concatenate([high, (left - high.astype(F32)).astype(BF16)], axis=0)
    product = lax.dot_general(halves, jnp.concatenate([right, right], axis=0), NT, preferred_element_type=F32)
    total = offset - (product[0:64] + product[64:128])
    lower = lax.broadcasted_iota(jnp.int32, (32, 128), 1) < 64
    packed = jnp.where(lower, total[0:32], total[32:64]).astype(BF16)
    for t in range(16):
        out_ref[t] = packed


def update_kernel(got_ref, parts_ref, covariance_ref, back_ref, flat):
    total = parts_ref[0].astype(F32)
    for t in range(1, 16):
        total = total + parts_ref[t].astype(F32)
    total = total * (1.0 / 16384)
    covariance = jnp.concatenate([total[:, 0:64], total[:, 64:128]], axis=0)
    covariance_ref[...] = covariance
    center = (covariance - jnp.mean(covariance, axis=0, keepdims=True)) * STEP
    high = center.astype(BF16)
    both = jnp.concatenate([high, (center - high.astype(F32)).astype(BF16)], axis=0)
    for p in range(PEERS):
        flat[16 * p : 16 * p + 16] = got_ref[p, 0:16].astype(F32)
    for s in range(8):
        members = flat[pl.ds(s, 64, stride=8), :]
        narrow = members.astype(BF16)
        moved = lax.dot_general(both, jnp.concatenate([narrow, narrow], axis=0), TN, preferred_element_type=F32)
        flat[pl.ds(s, 64, stride=8), :] = members + moved
    for p in range(PEERS):
        back_ref[p] = flat[16 * p : 16 * p + 16].astype(BF16)


def final_kernel(got_ref, covariance_in, out_ref, covariance_ref):
    covariance_ref[...] = covariance_in[...]
    for p in range(PEERS):
        values = got_ref[p].astype(F32)
        for m in range(2):
            for t in range(2):
                at = 128 * (2 * p + t)
                out_ref[m, :, at : at + 128] = values[8 * m + 4 * t : 8 * m + 4 * t + 4]


def per_device(latents, in_weight, out_weight, observe_weight, obs_cells, obs_values, obs_precision):
    c = lax.axis_index("c")
    across = [pair for z in range(7) for pair in ((2 * z + 1, 2 * z + 2), (2 * z + 2, 2 * z + 1))]
    vmem = pl.BlockSpec(memory_space=pltpu.VMEM)
    hbm = pl.BlockSpec(memory_space=pltpu.HBM)
    chip, five = kernel_call(
        rows_kernel, (shaped((8, 2, PAIRS, 128)), shaped((5, 2, PAIRS, 128))),
        [pltpu.VMEM((512, 128), F32)], moved=300_000,
    )(lax.all_gather(latents, "c"))
    five = lax.ppermute(five, TILE, across)
    *parts, sides = pl.pallas_call(
        inner_kernel,
        out_shape=(
            shaped((2, 8, PAIRS, 256)), shaped((2, 6, PAIRS, 512)), shaped((4, 2, PAIRS, 128)),
            shaped((2, 4, PAIRS, 256)), shaped((2, 2, PAIRS, 512)), shaped((2, 768, 512)), shaped((2, 256, 1536)),
            shaped((48, 256)), shaped((1152, 128)), shaped((24, 128), F32),
        ),
        in_specs=[vmem] + [hbm] * 6,
        scratch_shapes=[
            pltpu.VMEM((2, 576, 256), BF16), pltpu.VMEM((2, 64, 2304), BF16), pltpu.VMEM((8, 576), BF16),
            pltpu.VMEM((4, 32), jnp.int32), pltpu.VMEM((4, 256), F32), pltpu.VMEM((4, 256), F32),
            pltpu.SemaphoreType.DMA((6,)),
        ],
        cost_estimate=pl.CostEstimate(flops=2_000_000_000, bytes_accessed=6_000_000, transcendentals=0),
        compiler_params=pltpu.CompilerParams(vmem_limit_bytes=16 * 1024 * 1024),
    )(chip, *(pltpu.with_memory_space_constraint(v, pltpu.HBM) for v in (
        in_weight, jnp.transpose(out_weight, (0, 2, 1)), jnp.transpose(observe_weight), obs_cells, obs_values,
        obs_precision,
    )))
    one = lax.all_gather(lax.dynamic_slice_in_dim(five, 4 * (1 - c), 1, axis=0), "c", axis=0, tiled=True)
    pay = kernel_call(
        denoise_kernel,
        shaped((PEERS, 32, 128)),
        [
            pltpu.VMEM((14, 2, PAIRS, 128), BF16),
            pltpu.VMEM((2, 14, PAIRS, 256), BF16),
            pltpu.VMEM((2, 12, PAIRS, 512), BF16),
            pltpu.VMEM((10, 2, PAIRS, 128), BF16),
            pltpu.VMEM((2, 10, PAIRS, 256), BF16),
            pltpu.VMEM((2, 8, PAIRS, 512), BF16),
            pltpu.VMEM((6, 2, PAIRS, 128), BF16),
            pltpu.VMEM((512, 128), F32),
        ],
        flops=3_000_000_000, moved=4_300_000,
    )(chip, five, one, *parts, sides)
    got = lax.all_to_all(pay, MEM, 0, 0, tiled=True)

    parts = kernel_call(
        gram_kernel, shaped((16, 32, 128)), [pltpu.VMEM((512, 128), F32)], moved=700_000,
    )(got, sides)
    parts = lax.all_to_all(parts, TILE, 0, 0, tiled=True)
    covariance, back = kernel_call(
        update_kernel, (shaped((64, 64), F32), shaped((PEERS, 16, 128))), [pltpu.VMEM((512, 128), F32)],
        moved=700_000,
    )(got, parts)
    back = lax.all_to_all(back, MEM, 0, 0, tiled=True)
    return kernel_call(final_kernel, (shaped((2, 4, 8192), F32), shaped((64, 64), F32)), moved=400_000)(back, covariance)


def solution(mesh):
    split = Mesh(mesh.devices.reshape(8, 4, 8, 2), ("y", "x", "z", "c"))
    return jax.shard_map(
        per_device,
        mesh=split,
        in_specs=(P(MEM, TILE, None), P(), P(), P(), P(TILE, None), P(TILE, None), P(TILE, None)),
        out_specs=(P(MEM, TILE, None), P()),
        check_vma=False,
    )
```

```python
import functools

import jax
import jax.numpy as jnp
from jax import lax
from jax.experimental import pallas as pl
from jax.experimental.pallas import tpu as pltpu
from jax.sharding import Mesh
from jax.sharding import PartitionSpec as P

MEM = ("y", "x")
TILE = ("z", "c")
PAIRS = 64
HID = 256
PEERS = 32
EPS = 1e-06
STEP = 0.5
F32 = jnp.float32
BF16 = jnp.bfloat16
LIMIT = 24 * 1024 * 1024
NT = (((1,), (1,)), ((), ()))
TN = (((0,), (0,)), ((), ()))
BLOCKS = (0, 1, 2, -1)


def kernel_call(body, outs, scratch=(), flops=0, moved=0, limit=LIMIT):
    return pl.pallas_call(
        body,
        out_shape=outs,
        scratch_shapes=scratch,
        cost_estimate=pl.CostEstimate(flops=flops, bytes_accessed=moved, transcendentals=0),
        compiler_params=pltpu.CompilerParams(vmem_limit_bytes=limit),
    )


def shaped(shape, dtype=BF16):
    return jax.ShapeDtypeStruct(shape, dtype)


def rows_kernel(x_ref, chip_ref, five_ref, flat):
    c = lax.axis_index("c")
    for k in range(2):
        for m in range(2):
            for t in range(PAIRS):
                flat[256 * m + 4 * t : 256 * m + 4 * t + 4, :] = x_ref[k, m, :, 128 * t : 128 * t + 128].astype(F32)
        for m in range(2):
            for r in range(4):
                chip_ref[4 * k + r, m] = flat[pl.ds(256 * m + r, PAIRS, stride=4), :].astype(BF16)
    five_ref[...] = chip_ref[pl.ds(3 * c, 5)]


def spread_weights(in_ref, out_ref, seen_ref, first_ref, second_ref, obs_ref):
    first_ref[...] = jnp.zeros_like(first_ref)
    second_ref[...] = jnp.zeros_like(second_ref)
    for layer in range(2):
        for dr in range(3):
            for b, j in enumerate(BLOCKS):
                for h in range(2):
                    dc = j - h + 1
                    if 0 <= dc <= 2:
                        at = 64 * (3 * dr + dc)
                        first_ref[layer, 256 * dr + 64 * b : 256 * dr + 64 * b + 64, 256 * h : 256 * h + 256] = (
                            in_ref[layer, at : at + 64, :] * jnp.asarray(0.5, BF16)
                        )
                    dc = h - j + 1
                    if 0 <= dc <= 2:
                        at = 256 * (3 * dr + dc)
                        second_ref[layer, 64 * b : 64 * b + 64, 512 * dr + 256 * h : 512 * dr + 256 * h + 256] = (
                            out_ref[layer, :, at : at + 256]
                        )
    taps = seen_ref[...].astype(F32)
    none = jnp.zeros((8, 64), F32)
    rows = []
    for dr in range(3):
        for h in range(2):
            blocks = [j - h + 1 for j in BLOCKS]
            rows.append(jnp.concatenate(
                [taps[:, 64 * (3 * dr + dc) : 64 * (3 * dr + dc) + 64] if 0 <= dc <= 2 else none for dc in blocks],
                axis=1,
            ))
    obs_ref[...] = jnp.concatenate(rows, axis=0).astype(BF16)


def beside(values, lower):
    at = lax.broadcasted_iota(jnp.int32, values.shape, 1)
    after = jnp.where(at == PAIRS - 1, 0.0, pltpu.roll(values, PAIRS - 1, 1))
    before = jnp.where(at == 0, 0.0, pltpu.roll(values, 1, 1))
    return jnp.where(lower, after, before), jnp.where(lower, before, after)


def mean_over_channels():
    return jnp.where(
        (lax.broadcasted_iota(jnp.int32, (128, 128), 0) < 64) == (lax.broadcasted_iota(jnp.int32, (128, 128), 1) < 64),
        1.0 / 64, 0.0,
    ).astype(BF16)


def patches(a_ref, m, row, values, norm):
    count = values.shape[0]
    wide = values.astype(F32)
    lower = lax.broadcasted_iota(jnp.int32, wide.shape, 2) < 64
    if norm is not None:
        square = (values * values).reshape(count * PAIRS, 128)
        mean = jnp.dot(square, norm, preferred_element_type=F32).reshape(count, PAIRS, 128)
        wide = wide * lax.rsqrt(mean + EPS)
    a_ref[m, pl.ds(row, count), :, 0:128] = wide.astype(BF16)
    a_ref[m, pl.ds(row, count), :, 128:256] = beside(wide, lower)[0].astype(BF16)


def taps_of(ref, m, row, count):
    width = ref.shape[3]
    return jnp.concatenate(
        [ref[m, pl.ds(row + dr, count)].reshape(count * PAIRS, width) for dr in range(3)], axis=1
    )


def first_of(left, weight):
    return jnp.dot(left, weight, preferred_element_type=F32)


def silu(v):
    return v + v * jnp.tanh(v)


def hidden_of(left, weight):
    return silu(first_of(left, weight))


def scaled_rows(values, factors):
    return jnp.concatenate(
        [values[i : i + 1] * factors[i] if i in factors else values[i : i + 1] for i in range(values.shape[0])], axis=0
    )


def second(left, weight):
    return lax.dot_general(left, weight, NT, preferred_element_type=F32)


def updated(products, current):
    count = current.shape[0]
    y = products
    own = y[:, 0:128].reshape(count, PAIRS, 128)
    side = y[:, 128:256].reshape(count, PAIRS, 128)
    lower = lax.broadcasted_iota(jnp.int32, side.shape, 2) < 64
    return current.astype(F32) + own + beside(side, lower)[1]


def by_channel(values_ref, precision_ref, sides_ref):
    own = lax.broadcasted_iota(jnp.int32, (8, 256), 1) % 8 == lax.broadcasted_iota(jnp.int32, (8, 256), 0)
    spread = [
        jnp.concatenate(
            [jnp.where(own, jnp.broadcast_to(ref[r : r + 1, :], (8, 256)), 0.0) for r in range(4)], axis=1
        )
        for ref in (values_ref, precision_ref)
    ]
    whole = jnp.concatenate(spread, axis=0)
    at = lax.broadcasted_iota(jnp.int32, (1024, 128), 0)
    place = jnp.where(at // 8 == lax.broadcasted_iota(jnp.int32, (1024, 128), 1), 1.0, 0.0).astype(BF16)
    high = whole.astype(BF16)
    rest = whole - high.astype(F32)
    middle = rest.astype(BF16)
    low = (rest - middle.astype(F32)).astype(BF16)
    placed = jnp.dot(jnp.concatenate([high, middle, low], axis=0), place, preferred_element_type=F32)
    sides_ref[0:16] = placed[0:16] + placed[16:32] + placed[32:48]


def inner_kernel(chip_ref, in_hbm, out_hbm, seen_hbm, cells_hbm, values_hbm, precision_hbm,
                 a_ref, h_ref, x1_ref, a2_ref, h2_ref, w1_ref, w2_ref, obs_ref, pick_ref, sides_ref,
                 in_ref, out_ref, seen_ref, cells_ref, values_ref, precision_ref, sems):
    sources = (cells_hbm, values_hbm, precision_hbm, seen_hbm, in_hbm, out_hbm)
    targets = (cells_ref, values_ref, precision_ref, seen_ref, in_ref, out_ref)
    fetches = [pltpu.make_async_copy(a, b, sems.at[i]) for i, (a, b) in enumerate(zip(sources, targets))]
    for fetch in fetches:
        fetch.start()
    norm = mean_over_channels()
    for m in range(2):
        for row in (0, 4):
            patches(a_ref, m, row, chip_ref[row : row + 4, m], norm)
    for fetch in fetches[:3]:
        fetch.wait()
    by_channel(values_ref, precision_ref, sides_ref)
    cell = jnp.concatenate([cells_ref[r : r + 1, :] for r in range(4)], axis=1)
    pair = lax.shift_right_logical(cell, 1)
    lane_row = lax.broadcasted_iota(jnp.int32, (1, 128), 1) // 32
    index = lax.broadcasted_iota(jnp.int32, (384, 128), 0)
    for dr in range(3):
        pick_ref[384 * dr : 384 * dr + 384, :] = jnp.where(index == (lane_row + dr) * PAIRS + pair, 1.0, 0.0).astype(BF16)
    sides_ref[16:24] = jnp.broadcast_to((cell & 1).astype(F32), (8, 128))
    for fetch in fetches[3:]:
        fetch.wait()
    spread_weights(in_ref, out_ref, seen_ref, w1_ref, w2_ref, obs_ref)
    for m in range(2):
        for row in (0, 3):
            hidden = hidden_of(taps_of(a_ref, m, row, 3), w1_ref[0])
            h_ref[m, row : row + 3] = hidden.astype(BF16).reshape(3, PAIRS, 512)
    products = [second(taps_of(h_ref, m, 0, 4), w2_ref[0]) for m in range(2)]
    for m in range(2):
        x1_ref[:, m] = updated(products[m], chip_ref[2:6, m]).astype(BF16)
        patches(a2_ref, m, 0, x1_ref[:, m], norm)
    for m in range(2):
        h2_ref[m] = hidden_of(taps_of(a2_ref, m, 0, 2), w1_ref[1]).astype(BF16).reshape(2, PAIRS, 512)


def denoise_kernel(chip_ref, five_ref, one_ref, a_part, h_part, x1_part, a2_part, h2_part, w1_ref, w2_ref, obs_ref,
                   pick_ref, sides_ref, pay_ref, x_ref, a_ref, h_ref, x1_ref, a2_ref, h2_ref, x2_ref, flat):
    c = lax.axis_index("c")
    tile = 2 * lax.axis_index("z") + c
    first = jnp.where(tile == 0, 0.0, 1.0).astype(F32)
    last = jnp.where(tile == 15, 0.0, 1.0).astype(F32)
    start = 5 - 4 * c
    one = one_ref[1 - c]
    norm = mean_over_channels()
    for m in range(2):
        patches(a_ref, m, 9 * c, five_ref[:, m], norm)
        patches(a_ref, m, 13 - 13 * c, one[m : m + 1], norm)
        for k in (0, 6):
            a_ref[m, pl.ds(start + k, 2)] = a_part[m, k : k + 2]
        for k in (0, 4):
            h_ref[m, pl.ds(start + k, 2)] = h_part[m, k : k + 2]
        a2_ref[m, pl.ds(start, 4)] = a2_part[m]
        h2_ref[m, pl.ds(start, 2)] = h2_part[m]
    x_ref[pl.ds(start, 8)] = chip_ref[...]
    x1_ref[pl.ds(start, 4)] = x1_part[...]
    x_ref[pl.ds(9 * c, 5)] = five_ref[...]

    def edges(low, high):
        group = {}
        for q in range(5):
            if q < low or q >= high:
                group[q] = jnp.where(c == 1, last if q >= high else 1.0, first if q < low else 1.0)
        return group

    def split(values, factors):
        width = values.shape[1]
        rows = values.reshape(6, PAIRS, width)
        return scaled_rows(rows[0:5], factors).astype(BF16), rows[5].astype(BF16)

    products = []
    for m in range(2):
        left = jnp.concatenate([taps_of(a_ref, m, 7 * c, 5), taps_of(a_ref, m, 11 - 11 * c, 1)], axis=0)
        products.append(first_of(left, w1_ref[0]))
    for m in range(2):
        h_ref[m, pl.ds(7 * c, 5)], h_ref[m, 11 - 11 * c] = split(silu(products[m]), edges(4, 1))
    products = []
    for m in range(2):
        left = jnp.concatenate([taps_of(h_ref, m, 5 * c, 5), taps_of(h_ref, m, 9 - 9 * c, 1)], axis=0)
        products.append(second(left, w2_ref[0]))
    for m in range(2):
        current = jnp.concatenate([x_ref[pl.ds(5 * c + 2, 5), m], x_ref[pl.ds(11 - 9 * c, 1), m]], axis=0)
        group, single = split(updated(products[m], current).reshape(6 * PAIRS, 128), edges(3, 2))
        x1_ref[pl.ds(5 * c, 5), m] = group
        x1_ref[9 - 9 * c, m] = single
        patches(a2_ref, m, 5 * c, group, norm)
        patches(a2_ref, m, 9 - 9 * c, single[None], norm)
    products = []
    for m in range(2):
        left = jnp.concatenate([taps_of(a2_ref, m, 3 * c, 5), taps_of(a2_ref, m, 7 - 7 * c, 1)], axis=0)
        products.append(first_of(left, w1_ref[1]))
    for m in range(2):
        h2_ref[m, pl.ds(3 * c, 5)], h2_ref[m, 7 - 7 * c] = split(silu(products[m]), edges(2, 3))
    products = [second(taps_of(h2_ref, m, 0, 6), w2_ref[1]) for m in range(2)]
    seen = []
    for m in range(2):
        x2_ref[:, m] = scaled_rows(updated(products[m], x1_ref[2:8, m]), {0: first, 5: last}).astype(BF16)
        patches(a_ref, m, 0, x2_ref[:, m], None)
        y = lax.dot_general(obs_ref[...], a_ref[m, 0:6].reshape(384, 256), NT, preferred_element_type=F32)
        whole = jnp.concatenate([y[16 * dr : 16 * dr + 16] for dr in range(3)], axis=1)
        high = whole.astype(BF16).astype(F32)
        both = jnp.concatenate([high, whole - high], axis=0).astype(BF16)
        picked = jnp.dot(both, pick_ref[...], preferred_element_type=F32)
        seen.append(picked[0:16] + picked[16:32])
    odd = sides_ref[16:24] > 0.5
    got = jnp.concatenate([jnp.where(odd, y[8:16], y[0:8]) for y in seen], axis=0).astype(BF16)
    for m in range(2):
        for r in range(4):
            flat[pl.ds(256 * m + r, PAIRS, stride=4), :] = x2_ref[1 + r, m].astype(F32)
    for p in range(PEERS):
        both = jnp.concatenate([flat[8 * p : 8 * p + 8], flat[256 + 8 * p : 256 + 8 * p + 8]], axis=0)
        pay_ref[p, 0:16] = both.astype(BF16)
        pay_ref[p, 16:32] = got


def gram_kernel(got_ref, sides_ref, out_ref, flat):
    for p in range(PEERS):
        flat[16 * p : 16 * p + 16] = got_ref[p, 16:32].astype(F32)
    shape = (64, 128)
    left, right, values = [], [], []
    for o in range(8):
        members = flat[pl.ds(o, 64, stride=8), :]
        mean = jnp.sum(members, axis=0, keepdims=True) * (1.0 / 64)
        left.append((members - mean) * jnp.broadcast_to(sides_ref[8 + o : 9 + o], shape))
        right.append(members.astype(BF16))
        values.append(left[-1] * jnp.broadcast_to(sides_ref[o : o + 1], shape))
    offset = jnp.sum(functools.reduce(jnp.add, values), axis=1, keepdims=True)
    left = jnp.concatenate(left, axis=1)
    right = jnp.concatenate(right, axis=1)
    high = left.astype(BF16)
    halves = jnp.concatenate([high, (left - high.astype(F32)).astype(BF16)], axis=0)
    product = lax.dot_general(halves, jnp.concatenate([right, right], axis=0), NT, preferred_element_type=F32)
    total = offset - (product[0:64] + product[64:128])
    lower = lax.broadcasted_iota(jnp.int32, (32, 128), 1) < 64
    packed = jnp.where(lower, total[0:32], total[32:64]).astype(BF16)
    for t in range(16):
        out_ref[t] = packed


def update_kernel(got_ref, parts_ref, covariance_ref, back_ref, flat):
    total = parts_ref[0].astype(F32)
    for t in range(1, 16):
        total = total + parts_ref[t].astype(F32)
    total = total * (1.0 / 16384)
    covariance = jnp.concatenate([total[:, 0:64], total[:, 64:128]], axis=0)
    covariance_ref[...] = covariance
    center = (covariance - jnp.mean(covariance, axis=0, keepdims=True)) * STEP
    high = center.astype(BF16)
    both = jnp.concatenate([high, (center - high.astype(F32)).astype(BF16)], axis=0)
    for p in range(PEERS):
        flat[16 * p : 16 * p + 16] = got_ref[p, 0:16].astype(F32)
    for s in range(8):
        members = flat[pl.ds(s, 64, stride=8), :]
        narrow = members.astype(BF16)
        moved = lax.dot_general(both, jnp.concatenate([narrow, narrow], axis=0), TN, preferred_element_type=F32)
        flat[pl.ds(s, 64, stride=8), :] = members + moved
    for p in range(PEERS):
        back_ref[p] = flat[16 * p : 16 * p + 16].astype(BF16)


def final_kernel(got_ref, covariance_in, out_ref, covariance_ref):
    covariance_ref[...] = covariance_in[...]
    for p in range(PEERS):
        values = got_ref[p].astype(F32)
        for m in range(2):
            for t in range(2):
                at = 128 * (2 * p + t)
                out_ref[m, :, at : at + 128] = values[8 * m + 4 * t : 8 * m + 4 * t + 4]


def per_device(latents, in_weight, out_weight, observe_weight, obs_cells, obs_values, obs_precision):
    c = lax.axis_index("c")
    across = [pair for z in range(7) for pair in ((2 * z + 1, 2 * z + 2), (2 * z + 2, 2 * z + 1))]
    vmem = pl.BlockSpec(memory_space=pltpu.VMEM)
    hbm = pl.BlockSpec(memory_space=pltpu.HBM)
    chip, five = kernel_call(
        rows_kernel, (shaped((8, 2, PAIRS, 128)), shaped((5, 2, PAIRS, 128))),
        [pltpu.VMEM((512, 128), F32)], moved=300_000,
    )(lax.all_gather(latents, "c"))
    five = lax.ppermute(five, TILE, across)
    *parts, sides = pl.pallas_call(
        inner_kernel,
        out_shape=(
            shaped((2, 8, PAIRS, 256)), shaped((2, 6, PAIRS, 512)), shaped((4, 2, PAIRS, 128)),
            shaped((2, 4, PAIRS, 256)), shaped((2, 2, PAIRS, 512)), shaped((2, 768, 512)), shaped((2, 256, 1536)),
            shaped((48, 256)), shaped((1152, 128)), shaped((24, 128), F32),
        ),
        in_specs=[vmem] + [hbm] * 6,
        scratch_shapes=[
            pltpu.VMEM((2, 576, 256), BF16), pltpu.VMEM((2, 64, 2304), BF16), pltpu.VMEM((8, 576), BF16),
            pltpu.VMEM((4, 32), jnp.int32), pltpu.VMEM((4, 256), F32), pltpu.VMEM((4, 256), F32),
            pltpu.SemaphoreType.DMA((6,)),
        ],
        cost_estimate=pl.CostEstimate(flops=2_000_000_000, bytes_accessed=6_000_000, transcendentals=0),
        compiler_params=pltpu.CompilerParams(vmem_limit_bytes=16 * 1024 * 1024),
    )(chip, *(pltpu.with_memory_space_constraint(v, pltpu.HBM) for v in (
        in_weight, jnp.transpose(out_weight, (0, 2, 1)), jnp.transpose(observe_weight), obs_cells, obs_values,
        obs_precision,
    )))
    one = lax.all_gather(lax.dynamic_slice_in_dim(five, 4 * (1 - c), 1, axis=0), "c", axis=0, tiled=True)
    pay = kernel_call(
        denoise_kernel,
        shaped((PEERS, 32, 128)),
        [
            pltpu.VMEM((14, 2, PAIRS, 128), BF16),
            pltpu.VMEM((2, 14, PAIRS, 256), BF16),
            pltpu.VMEM((2, 12, PAIRS, 512), BF16),
            pltpu.VMEM((10, 2, PAIRS, 128), BF16),
            pltpu.VMEM((2, 10, PAIRS, 256), BF16),
            pltpu.VMEM((2, 8, PAIRS, 512), BF16),
            pltpu.VMEM((6, 2, PAIRS, 128), BF16),
            pltpu.VMEM((512, 128), F32),
        ],
        flops=3_000_000_000, moved=4_300_000,
    )(chip, five, one, *parts, sides)
    got = lax.all_to_all(pay, MEM, 0, 0, tiled=True)

    parts = kernel_call(
        gram_kernel, shaped((16, 32, 128)), [pltpu.VMEM((512, 128), F32)], moved=700_000,
    )(got, sides)
    parts = lax.all_to_all(parts, TILE, 0, 0, tiled=True)
    covariance, back = kernel_call(
        update_kernel, (shaped((64, 64), F32), shaped((PEERS, 16, 128))), [pltpu.VMEM((512, 128), F32)],
        moved=700_000,
    )(got, parts)
    back = lax.all_to_all(back, MEM, 0, 0, tiled=True)
    return kernel_call(final_kernel, (shaped((2, 4, 8192), F32), shaped((64, 64), F32)), moved=400_000)(back, covariance)


def solution(mesh):
    split = Mesh(mesh.devices.reshape(8, 4, 8, 2), ("y", "x", "z", "c"))
    return jax.shard_map(
        per_device,
        mesh=split,
        in_specs=(P(MEM, TILE, None), P(), P(), P(), P(TILE, None), P(TILE, None), P(TILE, None)),
        out_specs=(P(MEM, TILE, None), P()),
        check_vma=False,
    )
```

```python
import functools

import jax
import jax.numpy as jnp
from jax import lax
from jax.experimental import pallas as pl
from jax.experimental.pallas import tpu as pltpu
from jax.sharding import Mesh
from jax.sharding import PartitionSpec as P

MEM = ("y", "x")
TILE = ("z", "c")
PAIRS = 64
HID = 256
PEERS = 32
EPS = 1e-06
STEP = 0.5
F32 = jnp.float32
BF16 = jnp.bfloat16
LIMIT = 24 * 1024 * 1024
NT = (((1,), (1,)), ((), ()))
TN = (((0,), (0,)), ((), ()))
BLOCKS = (0, 1, 2, -1)


def kernel_call(body, outs, scratch=(), flops=0, moved=0, limit=LIMIT):
    return pl.pallas_call(
        body,
        out_shape=outs,
        scratch_shapes=scratch,
        cost_estimate=pl.CostEstimate(flops=flops, bytes_accessed=moved, transcendentals=0),
        compiler_params=pltpu.CompilerParams(vmem_limit_bytes=limit),
    )


def shaped(shape, dtype=BF16):
    return jax.ShapeDtypeStruct(shape, dtype)


def rows_kernel(x_ref, chip_ref, five_ref, flat):
    c = lax.axis_index("c")
    for k in range(2):
        for m in range(2):
            for t in range(PAIRS):
                flat[256 * m + 4 * t : 256 * m + 4 * t + 4, :] = x_ref[k, m, :, 128 * t : 128 * t + 128].astype(F32)
        for m in range(2):
            for r in range(4):
                chip_ref[4 * k + r, m] = flat[pl.ds(256 * m + r, PAIRS, stride=4), :].astype(BF16)
    five_ref[...] = chip_ref[pl.ds(3 * c, 5)]


def spread_weights(in_ref, out_ref, seen_ref, first_ref, second_ref, obs_ref):
    first_ref[...] = jnp.zeros_like(first_ref)
    second_ref[...] = jnp.zeros_like(second_ref)
    for layer in range(2):
        for dr in range(3):
            for b, j in enumerate(BLOCKS):
                for h in range(2):
                    dc = j - h + 1
                    if 0 <= dc <= 2:
                        at = 64 * (3 * dr + dc)
                        first_ref[layer, 256 * dr + 64 * b : 256 * dr + 64 * b + 64, 256 * h : 256 * h + 256] = (
                            in_ref[layer, at : at + 64, :] * jnp.asarray(0.5, BF16)
                        )
                    dc = h - j + 1
                    if 0 <= dc <= 2:
                        at = 256 * (3 * dr + dc)
                        second_ref[layer, 64 * b : 64 * b + 64, 512 * dr + 256 * h : 512 * dr + 256 * h + 256] = (
                            out_ref[layer, :, at : at + 256]
                        )
    taps = seen_ref[...].astype(F32)
    none = jnp.zeros((8, 64), F32)
    rows = []
    for dr in range(3):
        for h in range(2):
            blocks = [j - h + 1 for j in BLOCKS]
            rows.append(jnp.concatenate(
                [taps[:, 64 * (3 * dr + dc) : 64 * (3 * dr + dc) + 64] if 0 <= dc <= 2 else none for dc in blocks],
                axis=1,
            ))
    obs_ref[...] = jnp.concatenate(rows, axis=0).astype(BF16)


def beside(values, lower):
    at = lax.broadcasted_iota(jnp.int32, values.shape, 1)
    after = jnp.where(at == PAIRS - 1, 0.0, pltpu.roll(values, PAIRS - 1, 1))
    before = jnp.where(at == 0, 0.0, pltpu.roll(values, 1, 1))
    return jnp.where(lower, after, before), jnp.where(lower, before, after)


def mean_over_channels():
    return jnp.where(
        (lax.broadcasted_iota(jnp.int32, (128, 128), 0) < 64) == (lax.broadcasted_iota(jnp.int32, (128, 128), 1) < 64),
        1.0 / 64, 0.0,
    ).astype(BF16)


def patches(a_ref, m, row, values, norm):
    count = values.shape[0]
    wide = values.astype(F32)
    lower = lax.broadcasted_iota(jnp.int32, wide.shape, 2) < 64
    if norm is not None:
        square = (values * values).reshape(count * PAIRS, 128)
        mean = jnp.dot(square, norm, preferred_element_type=F32).reshape(count, PAIRS, 128)
        wide = wide * lax.rsqrt(mean + EPS)
    a_ref[m, pl.ds(row, count), :, 0:128] = wide.astype(BF16)
    a_ref[m, pl.ds(row, count), :, 128:256] = beside(wide, lower)[0].astype(BF16)


def taps_of(ref, m, row, count):
    width = ref.shape[3]
    return jnp.concatenate(
        [ref[m, pl.ds(row + dr, count)].reshape(count * PAIRS, width) for dr in range(3)], axis=1
    )


def first_of(left, weight):
    return jnp.dot(left, weight, preferred_element_type=F32)


def silu(v):
    return v + v * jnp.tanh(v)


def hidden_of(left, weight):
    return silu(first_of(left, weight))


def scaled_rows(values, factors):
    return jnp.concatenate(
        [values[i : i + 1] * factors[i] if i in factors else values[i : i + 1] for i in range(values.shape[0])], axis=0
    )


def second(left, weight):
    return lax.dot_general(left, weight, NT, preferred_element_type=F32)


def updated(products, current):
    count = current.shape[0]
    y = products
    own = y[:, 0:128].reshape(count, PAIRS, 128)
    side = y[:, 128:256].reshape(count, PAIRS, 128)
    lower = lax.broadcasted_iota(jnp.int32, side.shape, 2) < 64
    return current.astype(F32) + own + beside(side, lower)[1]


def by_channel(values_ref, precision_ref, sides_ref):
    own = lax.broadcasted_iota(jnp.int32, (8, 256), 1) % 8 == lax.broadcasted_iota(jnp.int32, (8, 256), 0)
    spread = [
        jnp.concatenate(
            [jnp.where(own, jnp.broadcast_to(ref[r : r + 1, :], (8, 256)), 0.0) for r in range(4)], axis=1
        )
        for ref in (values_ref, precision_ref)
    ]
    whole = jnp.concatenate(spread, axis=0)
    at = lax.broadcasted_iota(jnp.int32, (1024, 128), 0)
    place = jnp.where(at // 8 == lax.broadcasted_iota(jnp.int32, (1024, 128), 1), 1.0, 0.0).astype(BF16)
    high = whole.astype(BF16)
    rest = whole - high.astype(F32)
    middle = rest.astype(BF16)
    low = (rest - middle.astype(F32)).astype(BF16)
    placed = jnp.dot(jnp.concatenate([high, middle, low], axis=0), place, preferred_element_type=F32)
    sides_ref[0:16] = placed[0:16] + placed[16:32] + placed[32:48]


def inner_kernel(chip_ref, in_hbm, out_hbm, seen_hbm, cells_hbm, values_hbm, precision_hbm,
                 a_ref, h_ref, x1_ref, a2_ref, h2_ref, w1_ref, w2_ref, obs_ref, pick_ref, sides_ref,
                 in_ref, out_ref, seen_ref, cells_ref, values_ref, precision_ref, sems):
    sources = (cells_hbm, values_hbm, precision_hbm, seen_hbm, in_hbm, out_hbm)
    targets = (cells_ref, values_ref, precision_ref, seen_ref, in_ref, out_ref)
    fetches = [pltpu.make_async_copy(a, b, sems.at[i]) for i, (a, b) in enumerate(zip(sources, targets))]
    for fetch in fetches:
        fetch.start()
    norm = mean_over_channels()
    for m in range(2):
        for row in (0, 4):
            patches(a_ref, m, row, chip_ref[row : row + 4, m], norm)
    for fetch in fetches[:3]:
        fetch.wait()
    by_channel(values_ref, precision_ref, sides_ref)
    cell = jnp.concatenate([cells_ref[r : r + 1, :] for r in range(4)], axis=1)
    pair = lax.shift_right_logical(cell, 1)
    lane_row = lax.broadcasted_iota(jnp.int32, (1, 128), 1) // 32
    index = lax.broadcasted_iota(jnp.int32, (384, 128), 0)
    for dr in range(3):
        pick_ref[384 * dr : 384 * dr + 384, :] = jnp.where(index == (lane_row + dr) * PAIRS + pair, 1.0, 0.0).astype(BF16)
    sides_ref[16:24] = jnp.broadcast_to((cell & 1).astype(F32), (8, 128))
    for fetch in fetches[3:]:
        fetch.wait()
    spread_weights(in_ref, out_ref, seen_ref, w1_ref, w2_ref, obs_ref)
    for m in range(2):
        for row in (0, 3):
            hidden = hidden_of(taps_of(a_ref, m, row, 3), w1_ref[0])
            h_ref[m, row : row + 3] = hidden.astype(BF16).reshape(3, PAIRS, 512)
    products = [second(taps_of(h_ref, m, 0, 4), w2_ref[0]) for m in range(2)]
    for m in range(2):
        x1_ref[:, m] = updated(products[m], chip_ref[2:6, m]).astype(BF16)
        patches(a2_ref, m, 0, x1_ref[:, m], norm)
    for m in range(2):
        h2_ref[m] = hidden_of(taps_of(a2_ref, m, 0, 2), w1_ref[1]).astype(BF16).reshape(2, PAIRS, 512)


def denoise_kernel(chip_ref, five_ref, a_part, h_part, x1_part, a2_part, h2_part, w1_ref, w2_ref, obs_ref,
                   edge_ref, own_ref, seen_ref, x_ref, a_ref, h_ref, x1_ref, a2_ref, h2_ref, x2_ref, flat):
    c = lax.axis_index("c")
    tile = 2 * lax.axis_index("z") + c
    first = jnp.where(tile == 0, 0.0, 1.0).astype(F32)
    last = jnp.where(tile == 15, 0.0, 1.0).astype(F32)
    start = 5 - 4 * c
    norm = mean_over_channels()
    for m in range(2):
        patches(a_ref, m, 9 * c, five_ref[:, m], norm)
        for k in (0, 6):
            a_ref[m, pl.ds(start + k, 2)] = a_part[m, k : k + 2]
        for k in (0, 4):
            h_ref[m, pl.ds(start + k, 2)] = h_part[m, k : k + 2]
        a2_ref[m, pl.ds(start, 4)] = a2_part[m]
        h2_ref[m, pl.ds(start, 2)] = h2_part[m]
    x_ref[pl.ds(start, 8)] = chip_ref[...]
    x1_ref[pl.ds(start, 4)] = x1_part[...]
    x_ref[pl.ds(9 * c, 5)] = five_ref[...]

    def edges(low, high):
        group = {}
        for q in range(5):
            if q < low or q >= high:
                group[q] = jnp.where(c == 1, last if q >= high else 1.0, first if q < low else 1.0)
        return group

    products = [first_of(taps_of(a_ref, m, 7 * c, 5), w1_ref[0]) for m in range(2)]
    for m in range(2):
        hidden = silu(products[m]).reshape(5, PAIRS, 512)
        h_ref[m, pl.ds(7 * c, 5)] = scaled_rows(hidden, edges(4, 1)).astype(BF16)
    products = [second(taps_of(h_ref, m, 5 * c, 5), w2_ref[0]) for m in range(2)]
    for m in range(2):
        rows = scaled_rows(updated(products[m], x_ref[pl.ds(5 * c + 2, 5), m]), edges(3, 2)).astype(BF16)
        x1_ref[pl.ds(5 * c, 5), m] = rows
        patches(a2_ref, m, 5 * c, rows, norm)
    products = [first_of(taps_of(a2_ref, m, 3 * c, 5), w1_ref[1]) for m in range(2)]
    for m in range(2):
        hidden = silu(products[m]).reshape(5, PAIRS, 512)
        h2_ref[m, pl.ds(3 * c, 5)] = scaled_rows(hidden, edges(2, 3)).astype(BF16)
    products = [second(taps_of(h2_ref, m, c, 5), w2_ref[1]) for m in range(2)]
    for m in range(2):
        rows = scaled_rows(updated(products[m], x1_ref[pl.ds(2 + c, 5), m]), edges(1, 4)).astype(BF16)
        x2_ref[:, m] = rows
        patches(a2_ref, m, 0, rows, None)
    edge_ref[...] = x2_ref[4 - 4 * c]
    for m in range(2):
        seen_ref[m] = lax.dot_general(
            obs_ref[...], a2_ref[m, 0:5].reshape(320, 256), NT, preferred_element_type=F32
        )
    for m in range(2):
        for r in range(4):
            flat[pl.ds(256 * m + r, PAIRS, stride=4), :] = x2_ref[1 - c + r, m].astype(F32)
    for p in range(PEERS):
        both = jnp.concatenate([flat[8 * p : 8 * p + 8], flat[256 + 8 * p : 256 + 8 * p + 8]], axis=0)
        own_ref[p] = both.astype(BF16)


def observe_kernel(edge_ref, own_ref, seen_ref, obs_ref, pick_ref, sides_ref, pay_ref, a_ref):
    c = lax.axis_index("c")
    edge = edge_ref[1 - c]
    for m in range(2):
        patches(a_ref, m, 0, edge[m : m + 1], None)
    both = []
    for m in range(2):
        other = lax.dot_general(obs_ref[...], a_ref[m, 0], NT, preferred_element_type=F32)
        own = seen_ref[m]
        y = jnp.where(c == 1, jnp.concatenate([other, own], axis=1), jnp.concatenate([own, other], axis=1))
        whole = jnp.concatenate([y[16 * dr : 16 * dr + 16] for dr in range(3)], axis=1)
        high = whole.astype(BF16).astype(F32)
        both += [high, whole - high]
    picked = jnp.dot(jnp.concatenate(both, axis=0).astype(BF16), pick_ref[...], preferred_element_type=F32)
    odd = sides_ref[16:24] > 0.5
    got = []
    for m in range(2):
        y = picked[32 * m : 32 * m + 16] + picked[32 * m + 16 : 32 * m + 32]
        got.append(jnp.where(odd, y[8:16], y[0:8]))
    got = jnp.concatenate(got, axis=0).astype(BF16)
    for p in range(PEERS):
        pay_ref[p, 0:16] = own_ref[p]
        pay_ref[p, 16:32] = got


def gram_kernel(got_ref, sides_ref, out_ref, flat):
    for p in range(PEERS):
        flat[16 * p : 16 * p + 16] = got_ref[p, 16:32].astype(F32)
    shape = (64, 128)
    left, right, values = [], [], []
    for o in range(8):
        members = flat[pl.ds(o, 64, stride=8), :]
        mean = jnp.sum(members, axis=0, keepdims=True) * (1.0 / 64)
        left.append((members - mean) * jnp.broadcast_to(sides_ref[8 + o : 9 + o], shape))
        right.append(members.astype(BF16))
        values.append(left[-1] * jnp.broadcast_to(sides_ref[o : o + 1], shape))
    offset = jnp.sum(functools.reduce(jnp.add, values), axis=1, keepdims=True)
    left = jnp.concatenate(left, axis=1)
    right = jnp.concatenate(right, axis=1)
    high = left.astype(BF16)
    halves = jnp.concatenate([high, (left - high.astype(F32)).astype(BF16)], axis=0)
    product = lax.dot_general(halves, jnp.concatenate([right, right], axis=0), NT, preferred_element_type=F32)
    total = offset - (product[0:64] + product[64:128])
    lower = lax.broadcasted_iota(jnp.int32, (32, 128), 1) < 64
    packed = jnp.where(lower, total[0:32], total[32:64]).astype(BF16)
    for t in range(16):
        out_ref[t] = packed


def update_kernel(got_ref, parts_ref, covariance_ref, back_ref, flat):
    total = parts_ref[0].astype(F32)
    for t in range(1, 16):
        total = total + parts_ref[t].astype(F32)
    total = total * (1.0 / 16384)
    covariance = jnp.concatenate([total[:, 0:64], total[:, 64:128]], axis=0)
    covariance_ref[...] = covariance
    center = (covariance - jnp.mean(covariance, axis=0, keepdims=True)) * STEP
    high = center.astype(BF16)
    both = jnp.concatenate([high, (center - high.astype(F32)).astype(BF16)], axis=0)
    for p in range(PEERS):
        flat[16 * p : 16 * p + 16] = got_ref[p, 0:16].astype(F32)
    for s in range(8):
        members = flat[pl.ds(s, 64, stride=8), :]
        narrow = members.astype(BF16)
        moved = lax.dot_general(both, jnp.concatenate([narrow, narrow], axis=0), TN, preferred_element_type=F32)
        flat[pl.ds(s, 64, stride=8), :] = members + moved
    for p in range(PEERS):
        back_ref[p] = flat[16 * p : 16 * p + 16].astype(BF16)


def final_kernel(got_ref, covariance_in, out_hbm, covariance_hbm, out_ref, sems):
    copies = [pltpu.make_async_copy(covariance_in, covariance_hbm, sems.at[8])]
    copies[0].start()
    for part in range(4):
        for m in range(2):
            for p in range(8 * part, 8 * part + 8):
                values = got_ref[p, 8 * m : 8 * m + 8].astype(F32)
                for t in range(2):
                    at = 128 * (2 * p + t)
                    out_ref[m, :, at : at + 128] = values[4 * t : 4 * t + 4]
            span = pl.ds(2048 * part, 2048)
            copies.append(pltpu.make_async_copy(out_ref.at[m, :, span], out_hbm.at[m, :, span], sems.at[2 * part + m]))
            copies[-1].start()
    for copy in copies:
        copy.wait()


def per_device(latents, in_weight, out_weight, observe_weight, obs_cells, obs_values, obs_precision):
    c = lax.axis_index("c")
    across = [pair for z in range(7) for pair in ((2 * z + 1, 2 * z + 2), (2 * z + 2, 2 * z + 1))]
    vmem = pl.BlockSpec(memory_space=pltpu.VMEM)
    hbm = pl.BlockSpec(memory_space=pltpu.HBM)
    chip, five = kernel_call(
        rows_kernel, (shaped((8, 2, PAIRS, 128)), shaped((5, 2, PAIRS, 128))),
        [pltpu.VMEM((512, 128), F32)], moved=300_000,
    )(lax.all_gather(latents, "c"))
    five = lax.ppermute(five, TILE, across)
    *parts, sides = pl.pallas_call(
        inner_kernel,
        out_shape=(
            shaped((2, 8, PAIRS, 256)), shaped((2, 6, PAIRS, 512)), shaped((4, 2, PAIRS, 128)),
            shaped((2, 4, PAIRS, 256)), shaped((2, 2, PAIRS, 512)), shaped((2, 768, 512)), shaped((2, 256, 1536)),
            shaped((48, 256)), shaped((1152, 128)), shaped((24, 128), F32),
        ),
        in_specs=[vmem] + [hbm] * 6,
        scratch_shapes=[
            pltpu.VMEM((2, 576, 256), BF16), pltpu.VMEM((2, 64, 2304), BF16), pltpu.VMEM((8, 576), BF16),
            pltpu.VMEM((4, 32), jnp.int32), pltpu.VMEM((4, 256), F32), pltpu.VMEM((4, 256), F32),
            pltpu.SemaphoreType.DMA((6,)),
        ],
        cost_estimate=pl.CostEstimate(flops=2_000_000_000, bytes_accessed=6_000_000, transcendentals=0),
        compiler_params=pltpu.CompilerParams(vmem_limit_bytes=16 * 1024 * 1024),
    )(chip, *(pltpu.with_memory_space_constraint(v, pltpu.HBM) for v in (
        in_weight, jnp.transpose(out_weight, (0, 2, 1)), jnp.transpose(observe_weight), obs_cells, obs_values,
        obs_precision,
    )))
    *parts, obs, pick = parts
    edge, own, seen = kernel_call(
        denoise_kernel,
        (shaped((2, PAIRS, 128)), shaped((PEERS, 16, 128)), shaped((2, 48, 320), F32)),
        [
            pltpu.VMEM((14, 2, PAIRS, 128), BF16),
            pltpu.VMEM((2, 14, PAIRS, 256), BF16),
            pltpu.VMEM((2, 12, PAIRS, 512), BF16),
            pltpu.VMEM((10, 2, PAIRS, 128), BF16),
            pltpu.VMEM((2, 10, PAIRS, 256), BF16),
            pltpu.VMEM((2, 8, PAIRS, 512), BF16),
            pltpu.VMEM((5, 2, PAIRS, 128), BF16),
            pltpu.VMEM((512, 128), F32),
        ],
        flops=3_000_000_000, moved=4_300_000,
    )(chip, five, *parts, obs)
    pay = kernel_call(
        observe_kernel, shaped((PEERS, 32, 128)), [pltpu.VMEM((2, 1, PAIRS, 256), BF16)], moved=800_000,
    )(lax.all_gather(edge, "c"), own, seen, obs, pick, sides)
    got = lax.all_to_all(pay, MEM, 0, 0, tiled=True)

    parts = kernel_call(
        gram_kernel, shaped((16, 32, 128)), [pltpu.VMEM((512, 128), F32)], moved=700_000,
    )(got, sides)
    parts = lax.all_to_all(parts, TILE, 0, 0, tiled=True)
    covariance, back = kernel_call(
        update_kernel, (shaped((64, 64), F32), shaped((PEERS, 16, 128))), [pltpu.VMEM((512, 128), F32)],
        moved=700_000,
    )(got, parts)
    back = lax.all_to_all(back, MEM, 0, 0, tiled=True)
    return pl.pallas_call(
        final_kernel,
        out_shape=(shaped((2, 4, 8192), F32), shaped((64, 64), F32)),
        in_specs=[vmem, vmem],
        out_specs=(hbm, hbm),
        scratch_shapes=[pltpu.VMEM((2, 4, 8192), F32), pltpu.SemaphoreType.DMA((9,))],
        cost_estimate=pl.CostEstimate(flops=0, bytes_accessed=400_000, transcendentals=0),
        compiler_params=pltpu.CompilerParams(vmem_limit_bytes=LIMIT),
    )(back, covariance)


def solution(mesh):
    split = Mesh(mesh.devices.reshape(8, 4, 8, 2), ("y", "x", "z", "c"))
    return jax.shard_map(
        per_device,
        mesh=split,
        in_specs=(P(MEM, TILE, None), P(), P(), P(), P(TILE, None), P(TILE, None), P(TILE, None)),
        out_specs=(P(MEM, TILE, None), P()),
        check_vma=False,
    )
```

```python
import functools

import jax
import jax.numpy as jnp
from jax import lax
from jax.experimental import pallas as pl
from jax.experimental.pallas import tpu as pltpu
from jax.sharding import Mesh
from jax.sharding import PartitionSpec as P

MEM = ("y", "x")
TILE = ("z", "c")
PAIRS = 64
HID = 256
PEERS = 32
EPS = 1e-06
STEP = 0.5
F32 = jnp.float32
BF16 = jnp.bfloat16
LIMIT = 24 * 1024 * 1024
NT = (((1,), (1,)), ((), ()))
TN = (((0,), (0,)), ((), ()))
BLOCKS = (0, 1, 2, -1)


def kernel_call(body, outs, scratch=(), flops=0, moved=0, limit=LIMIT):
    return pl.pallas_call(
        body,
        out_shape=outs,
        scratch_shapes=scratch,
        cost_estimate=pl.CostEstimate(flops=flops, bytes_accessed=moved, transcendentals=0),
        compiler_params=pltpu.CompilerParams(vmem_limit_bytes=limit),
    )


def shaped(shape, dtype=BF16):
    return jax.ShapeDtypeStruct(shape, dtype)


def rows_kernel(x_ref, chip_ref, five_ref, flat):
    c = lax.axis_index("c")
    for k in range(2):
        for m in range(2):
            for t in range(PAIRS):
                flat[256 * m + 4 * t : 256 * m + 4 * t + 4, :] = x_ref[k, m, :, 128 * t : 128 * t + 128].astype(F32)
        for m in range(2):
            for r in range(4):
                chip_ref[4 * k + r, m] = flat[pl.ds(256 * m + r, PAIRS, stride=4), :].astype(BF16)
    five_ref[...] = chip_ref[pl.ds(3 * c, 5)]


def spread_weights(layer, in_ref, out_ref, first_ref, second_ref):
    for dr in range(3):
        for b, j in enumerate(BLOCKS):
            for h in range(2):
                dc, at = j - h + 1, (slice(256 * dr + 64 * b, 256 * dr + 64 * b + 64), slice(256 * h, 256 * h + 256))
                tap = 64 * (3 * dr + dc)
                if 0 <= dc <= 2:
                    first_ref[(layer, *at)] = in_ref[layer, tap : tap + 64, :] * jnp.asarray(0.5, BF16)
                else:
                    first_ref[(layer, *at)] = jnp.zeros((64, 256), BF16)
                dc, at = h - j + 1, (slice(64 * b, 64 * b + 64), slice(512 * dr + 256 * h, 512 * dr + 256 * h + 256))
                tap = 256 * (3 * dr + dc)
                if 0 <= dc <= 2:
                    second_ref[(layer, *at)] = out_ref[layer, :, tap : tap + 256]
                else:
                    second_ref[(layer, *at)] = jnp.zeros((64, 256), BF16)


def spread_observed(seen_ref, obs_ref):
    taps = seen_ref[...].astype(F32)
    none = jnp.zeros((8, 64), F32)
    rows = []
    for dr in range(3):
        for h in range(2):
            blocks = [j - h + 1 for j in BLOCKS]
            rows.append(jnp.concatenate(
                [taps[:, 64 * (3 * dr + dc) : 64 * (3 * dr + dc) + 64] if 0 <= dc <= 2 else none for dc in blocks],
                axis=1,
            ))
    obs_ref[...] = jnp.concatenate(rows, axis=0).astype(BF16)


def beside(values, lower):
    at = lax.broadcasted_iota(jnp.int32, values.shape, 1)
    after = jnp.where(at == PAIRS - 1, 0.0, pltpu.roll(values, PAIRS - 1, 1))
    before = jnp.where(at == 0, 0.0, pltpu.roll(values, 1, 1))
    return jnp.where(lower, after, before), jnp.where(lower, before, after)


def mean_over_channels():
    return jnp.where(
        (lax.broadcasted_iota(jnp.int32, (128, 128), 0) < 64) == (lax.broadcasted_iota(jnp.int32, (128, 128), 1) < 64),
        1.0 / 64, 0.0,
    ).astype(BF16)


def patches(a_ref, m, row, values, norm):
    count = values.shape[0]
    wide = values.astype(F32)
    lower = lax.broadcasted_iota(jnp.int32, wide.shape, 2) < 64
    if norm is not None:
        square = (values * values).reshape(count * PAIRS, 128)
        mean = jnp.dot(square, norm, preferred_element_type=F32).reshape(count, PAIRS, 128)
        wide = wide * lax.rsqrt(mean + EPS)
    a_ref[m, pl.ds(row, count), :, 0:128] = wide.astype(BF16)
    a_ref[m, pl.ds(row, count), :, 128:256] = beside(wide, lower)[0].astype(BF16)


def taps_of(ref, m, row, count):
    width = ref.shape[3]
    return jnp.concatenate(
        [ref[m, pl.ds(row + dr, count)].reshape(count * PAIRS, width) for dr in range(3)], axis=1
    )


def first_of(left, weight):
    return jnp.dot(left, weight, preferred_element_type=F32)


def silu(v):
    return v + v * jnp.tanh(v)


def scaled_rows(values, factors):
    return jnp.concatenate(
        [values[i : i + 1] * factors[i] if i in factors else values[i : i + 1] for i in range(values.shape[0])], axis=0
    )


def second(left, weight):
    return lax.dot_general(left, weight, NT, preferred_element_type=F32)


def updated(products, current):
    count = current.shape[0]
    y = products
    own = y[:, 0:128].reshape(count, PAIRS, 128)
    side = y[:, 128:256].reshape(count, PAIRS, 128)
    lower = lax.broadcasted_iota(jnp.int32, side.shape, 2) < 64
    return current.astype(F32) + own + beside(side, lower)[1]


def by_channel(values_ref, precision_ref, sides_ref):
    own = lax.broadcasted_iota(jnp.int32, (8, 256), 1) % 8 == lax.broadcasted_iota(jnp.int32, (8, 256), 0)
    spread = [
        jnp.concatenate(
            [jnp.where(own, jnp.broadcast_to(ref[r : r + 1, :], (8, 256)), 0.0) for r in range(4)], axis=1
        )
        for ref in (values_ref, precision_ref)
    ]
    whole = jnp.concatenate(spread, axis=0)
    at = lax.broadcasted_iota(jnp.int32, (1024, 128), 0)
    place = jnp.where(at // 8 == lax.broadcasted_iota(jnp.int32, (1024, 128), 1), 1.0, 0.0).astype(BF16)
    high = whole.astype(BF16)
    rest = whole - high.astype(F32)
    middle = rest.astype(BF16)
    low = (rest - middle.astype(F32)).astype(BF16)
    placed = jnp.dot(jnp.concatenate([high, middle, low], axis=0), place, preferred_element_type=F32)
    sides_ref[0:16] = placed[0:16] + placed[16:32] + placed[32:48]


def inner_kernel(chip_ref, in_hbm, out_hbm, seen_hbm, cells_hbm, values_hbm, precision_hbm,
                 a_ref, h_ref, x1_ref, a2_ref, h2_ref, w1_ref, w2_ref, obs_ref, pick_ref, sides_ref,
                 in_ref, out_ref, seen_ref, cells_ref, values_ref, precision_ref, sems):
    sources = (cells_hbm, values_hbm, precision_hbm, seen_hbm, in_hbm, out_hbm)
    targets = (cells_ref, values_ref, precision_ref, seen_ref, in_ref, out_ref)
    fetches = [pltpu.make_async_copy(a, b, sems.at[i]) for i, (a, b) in enumerate(zip(sources, targets))]
    for fetch in fetches:
        fetch.start()
    norm = mean_over_channels()
    for m in range(2):
        for row in (0, 4):
            patches(a_ref, m, row, chip_ref[row : row + 4, m], norm)
    for fetch in fetches:
        fetch.wait()
    spread_weights(0, in_ref, out_ref, w1_ref, w2_ref)
    products = [first_of(taps_of(a_ref, m, 0, 6), w1_ref[0]) for m in range(2)]
    by_channel(values_ref, precision_ref, sides_ref)
    spread_observed(seen_ref, obs_ref)
    cell = jnp.concatenate([cells_ref[r : r + 1, :] for r in range(4)], axis=1)
    pair = lax.shift_right_logical(cell, 1)
    lane_row = lax.broadcasted_iota(jnp.int32, (1, 128), 1) // 32
    index = lax.broadcasted_iota(jnp.int32, (384, 128), 0)
    for dr in range(3):
        pick_ref[384 * dr : 384 * dr + 384, :] = jnp.where(index == (lane_row + dr) * PAIRS + pair, 1.0, 0.0).astype(BF16)
    sides_ref[16:24] = jnp.broadcast_to((cell & 1).astype(F32), (8, 128))
    spread_weights(1, in_ref, out_ref, w1_ref, w2_ref)
    for m in range(2):
        h_ref[m] = silu(products[m]).astype(BF16).reshape(6, PAIRS, 512)
    products = [second(taps_of(h_ref, m, 0, 4), w2_ref[0]) for m in range(2)]
    for m in range(2):
        x1_ref[:, m] = updated(products[m], chip_ref[2:6, m]).astype(BF16)
        patches(a2_ref, m, 0, x1_ref[:, m], norm)
    products = [first_of(taps_of(a2_ref, m, 0, 2), w1_ref[1]) for m in range(2)]
    for m in range(2):
        h2_ref[m] = silu(products[m]).astype(BF16).reshape(2, PAIRS, 512)


def denoise_kernel(chip_ref, five_ref, a_part, h_part, x1_part, a2_part, h2_part, w1_ref, w2_ref, obs_ref,
                   edge_ref, own_ref, seen_ref, x_ref, a_ref, h_ref, x1_ref, a2_ref, h2_ref, x2_ref, flat):
    c = lax.axis_index("c")
    tile = 2 * lax.axis_index("z") + c
    first = jnp.where(tile == 0, 0.0, 1.0).astype(F32)
    last = jnp.where(tile == 15, 0.0, 1.0).astype(F32)
    start = 5 - 4 * c
    norm = mean_over_channels()
    for m in range(2):
        patches(a_ref, m, 9 * c, five_ref[:, m], norm)
        for k in (0, 6):
            a_ref[m, pl.ds(start + k, 2)] = a_part[m, k : k + 2]
        for k in (0, 4):
            h_ref[m, pl.ds(start + k, 2)] = h_part[m, k : k + 2]
        a2_ref[m, pl.ds(start, 4)] = a2_part[m]
        h2_ref[m, pl.ds(start, 2)] = h2_part[m]
    x_ref[pl.ds(start, 8)] = chip_ref[...]
    x1_ref[pl.ds(start, 4)] = x1_part[...]
    x_ref[pl.ds(9 * c, 5)] = five_ref[...]

    def edges(low, high):
        group = {}
        for q in range(5):
            if q < low or q >= high:
                group[q] = jnp.where(c == 1, last if q >= high else 1.0, first if q < low else 1.0)
        return group

    products = [first_of(taps_of(a_ref, m, 7 * c, 5), w1_ref[0]) for m in range(2)]
    for m in range(2):
        hidden = silu(products[m]).reshape(5, PAIRS, 512)
        h_ref[m, pl.ds(7 * c, 5)] = scaled_rows(hidden, edges(4, 1)).astype(BF16)
    products = [second(taps_of(h_ref, m, 5 * c, 5), w2_ref[0]) for m in range(2)]
    for m in range(2):
        rows = scaled_rows(updated(products[m], x_ref[pl.ds(5 * c + 2, 5), m]), edges(3, 2)).astype(BF16)
        x1_ref[pl.ds(5 * c, 5), m] = rows
        patches(a2_ref, m, 5 * c, rows, norm)
    products = [first_of(taps_of(a2_ref, m, 3 * c, 5), w1_ref[1]) for m in range(2)]
    for m in range(2):
        hidden = silu(products[m]).reshape(5, PAIRS, 512)
        h2_ref[m, pl.ds(3 * c, 5)] = scaled_rows(hidden, edges(2, 3)).astype(BF16)
    products = [second(taps_of(h2_ref, m, c, 5), w2_ref[1]) for m in range(2)]
    for m in range(2):
        rows = scaled_rows(updated(products[m], x1_ref[pl.ds(2 + c, 5), m]), edges(1, 4)).astype(BF16)
        x2_ref[:, m] = rows
        patches(a2_ref, m, 0, rows, None)
    edge_ref[...] = x2_ref[4 - 4 * c]
    for m in range(2):
        seen_ref[m] = lax.dot_general(
            obs_ref[...], a2_ref[m, 0:5].reshape(320, 256), NT, preferred_element_type=F32
        )
    for m in range(2):
        for r in range(4):
            flat[pl.ds(256 * m + r, PAIRS, stride=4), :] = x2_ref[1 - c + r, m].astype(F32)
    for p in range(PEERS):
        both = jnp.concatenate([flat[8 * p : 8 * p + 8], flat[256 + 8 * p : 256 + 8 * p + 8]], axis=0)
        own_ref[p] = both.astype(BF16)


def observe_kernel(edge_ref, own_ref, seen_ref, obs_ref, pick_ref, sides_ref, pay_ref, a_ref):
    c = lax.axis_index("c")
    edge = edge_ref[1 - c]
    for m in range(2):
        patches(a_ref, m, 0, edge[m : m + 1], None)
    both = []
    for m in range(2):
        other = lax.dot_general(obs_ref[...], a_ref[m, 0], NT, preferred_element_type=F32)
        own = seen_ref[m]
        y = jnp.where(c == 1, jnp.concatenate([other, own], axis=1), jnp.concatenate([own, other], axis=1))
        whole = jnp.concatenate([y[16 * dr : 16 * dr + 16] for dr in range(3)], axis=1)
        high = whole.astype(BF16).astype(F32)
        both += [high, whole - high]
    picked = jnp.dot(jnp.concatenate(both, axis=0).astype(BF16), pick_ref[...], preferred_element_type=F32)
    odd = sides_ref[16:24] > 0.5
    got = []
    for m in range(2):
        y = picked[32 * m : 32 * m + 16] + picked[32 * m + 16 : 32 * m + 32]
        got.append(jnp.where(odd, y[8:16], y[0:8]))
    got = jnp.concatenate(got, axis=0).astype(BF16)
    for p in range(PEERS):
        pay_ref[p, 0:16] = own_ref[p]
        pay_ref[p, 16:32] = got


def gram_kernel(got_ref, sides_ref, out_ref, flat):
    for p in range(PEERS):
        flat[16 * p : 16 * p + 16] = got_ref[p, 16:32].astype(F32)
    shape = (64, 128)
    left, right, values = [], [], []
    for o in range(8):
        members = flat[pl.ds(o, 64, stride=8), :]
        mean = jnp.sum(members, axis=0, keepdims=True) * (1.0 / 64)
        left.append((members - mean) * jnp.broadcast_to(sides_ref[8 + o : 9 + o], shape))
        right.append(members.astype(BF16))
        values.append(left[-1] * jnp.broadcast_to(sides_ref[o : o + 1], shape))
    offset = jnp.sum(functools.reduce(jnp.add, values), axis=1, keepdims=True)
    left = jnp.concatenate(left, axis=1)
    right = jnp.concatenate(right, axis=1)
    high = left.astype(BF16)
    halves = jnp.concatenate([high, (left - high.astype(F32)).astype(BF16)], axis=0)
    product = lax.dot_general(halves, jnp.concatenate([right, right], axis=0), NT, preferred_element_type=F32)
    total = offset - (product[0:64] + product[64:128])
    lower = lax.broadcasted_iota(jnp.int32, (32, 128), 1) < 64
    packed = jnp.where(lower, total[0:32], total[32:64]).astype(BF16)
    for t in range(16):
        out_ref[t] = packed


def update_kernel(got_ref, parts_ref, covariance_ref, back_ref, flat):
    total = parts_ref[0].astype(F32)
    for t in range(1, 16):
        total = total + parts_ref[t].astype(F32)
    total = total * (1.0 / 16384)
    covariance = jnp.concatenate([total[:, 0:64], total[:, 64:128]], axis=0)
    covariance_ref[...] = covariance
    center = (covariance - jnp.mean(covariance, axis=0, keepdims=True)) * STEP
    high = center.astype(BF16)
    both = jnp.concatenate([high, (center - high.astype(F32)).astype(BF16)], axis=0)
    for p in range(PEERS):
        flat[16 * p : 16 * p + 16] = got_ref[p, 0:16].astype(F32)
    for s in range(8):
        members = flat[pl.ds(s, 64, stride=8), :]
        narrow = members.astype(BF16)
        moved = lax.dot_general(both, jnp.concatenate([narrow, narrow], axis=0), TN, preferred_element_type=F32)
        flat[pl.ds(s, 64, stride=8), :] = members + moved
    for p in range(PEERS):
        back_ref[p] = flat[16 * p : 16 * p + 16].astype(BF16)


def final_kernel(got_ref, covariance_in, out_ref, covariance_ref):
    covariance_ref[...] = covariance_in[...]
    for p in range(PEERS):
        values = got_ref[p].astype(F32)
        for m in range(2):
            for t in range(2):
                at = 128 * (2 * p + t)
                out_ref[m, :, at : at + 128] = values[8 * m + 4 * t : 8 * m + 4 * t + 4]


def per_device(latents, in_weight, out_weight, observe_weight, obs_cells, obs_values, obs_precision):
    c = lax.axis_index("c")
    across = [pair for z in range(7) for pair in ((2 * z + 1, 2 * z + 2), (2 * z + 2, 2 * z + 1))]
    vmem = pl.BlockSpec(memory_space=pltpu.VMEM)
    hbm = pl.BlockSpec(memory_space=pltpu.HBM)
    chip, five = kernel_call(
        rows_kernel, (shaped((8, 2, PAIRS, 128)), shaped((5, 2, PAIRS, 128))),
        [pltpu.VMEM((512, 128), F32)], moved=300_000,
    )(lax.all_gather(latents, "c"))
    five = lax.ppermute(five, TILE, across)
    *parts, sides = pl.pallas_call(
        inner_kernel,
        out_shape=(
            shaped((2, 8, PAIRS, 256)), shaped((2, 6, PAIRS, 512)), shaped((4, 2, PAIRS, 128)),
            shaped((2, 4, PAIRS, 256)), shaped((2, 2, PAIRS, 512)), shaped((2, 768, 512)), shaped((2, 256, 1536)),
            shaped((48, 256)), shaped((1152, 128)), shaped((24, 128), F32),
        ),
        in_specs=[vmem] + [hbm] * 6,
        scratch_shapes=[
            pltpu.VMEM((2, 576, 256), BF16), pltpu.VMEM((2, 64, 2304), BF16), pltpu.VMEM((8, 576), BF16),
            pltpu.VMEM((4, 32), jnp.int32), pltpu.VMEM((4, 256), F32), pltpu.VMEM((4, 256), F32),
            pltpu.SemaphoreType.DMA((6,)),
        ],
        cost_estimate=pl.CostEstimate(flops=2_000_000_000, bytes_accessed=6_000_000, transcendentals=0),
        compiler_params=pltpu.CompilerParams(vmem_limit_bytes=16 * 1024 * 1024),
    )(chip, *(pltpu.with_memory_space_constraint(v, pltpu.HBM) for v in (
        in_weight, jnp.transpose(out_weight, (0, 2, 1)), jnp.transpose(observe_weight), obs_cells, obs_values,
        obs_precision,
    )))
    *parts, obs, pick = parts
    edge, own, seen = kernel_call(
        denoise_kernel,
        (shaped((2, PAIRS, 128)), shaped((PEERS, 16, 128)), shaped((2, 48, 320), F32)),
        [
            pltpu.VMEM((14, 2, PAIRS, 128), BF16),
            pltpu.VMEM((2, 14, PAIRS, 256), BF16),
            pltpu.VMEM((2, 12, PAIRS, 512), BF16),
            pltpu.VMEM((10, 2, PAIRS, 128), BF16),
            pltpu.VMEM((2, 10, PAIRS, 256), BF16),
            pltpu.VMEM((2, 8, PAIRS, 512), BF16),
            pltpu.VMEM((5, 2, PAIRS, 128), BF16),
            pltpu.VMEM((512, 128), F32),
        ],
        flops=3_000_000_000, moved=4_300_000,
    )(chip, five, *parts, obs)
    pay = kernel_call(
        observe_kernel, shaped((PEERS, 32, 128)), [pltpu.VMEM((2, 1, PAIRS, 256), BF16)], moved=800_000,
    )(lax.all_gather(edge, "c"), own, seen, obs, pick, sides)
    got = lax.all_to_all(pay, MEM, 0, 0, tiled=True)

    parts = kernel_call(
        gram_kernel, shaped((16, 32, 128)), [pltpu.VMEM((512, 128), F32)], moved=700_000,
    )(got, sides)
    parts = lax.all_to_all(parts, TILE, 0, 0, tiled=True)
    covariance, back = kernel_call(
        update_kernel, (shaped((64, 64), F32), shaped((PEERS, 16, 128))), [pltpu.VMEM((512, 128), F32)],
        moved=700_000,
    )(got, parts)
    back = lax.all_to_all(back, MEM, 0, 0, tiled=True)
    return kernel_call(final_kernel, (shaped((2, 4, 8192), F32), shaped((64, 64), F32)), moved=400_000)(back, covariance)


def solution(mesh):
    split = Mesh(mesh.devices.reshape(8, 4, 8, 2), ("y", "x", "z", "c"))
    return jax.shard_map(
        per_device,
        mesh=split,
        in_specs=(P(MEM, TILE, None), P(), P(), P(), P(TILE, None), P(TILE, None), P(TILE, None)),
        out_specs=(P(MEM, TILE, None), P()),
        check_vma=False,
    )
```

```python
import functools

import jax
import jax.numpy as jnp
from jax import lax
from jax.experimental import pallas as pl
from jax.experimental.pallas import tpu as pltpu
from jax.sharding import Mesh
from jax.sharding import PartitionSpec as P

MEM = ("y", "x")
TILE = ("z", "c")
PAIRS = 64
HID = 256
PEERS = 32
EPS = 1e-06
STEP = 0.5
F32 = jnp.float32
BF16 = jnp.bfloat16
LIMIT = 24 * 1024 * 1024
NT = (((1,), (1,)), ((), ()))
TN = (((0,), (0,)), ((), ()))
BLOCKS = (0, 1, 2, -1)


def kernel_call(body, outs, scratch=(), flops=0, moved=0, limit=LIMIT):
    return pl.pallas_call(
        body,
        out_shape=outs,
        scratch_shapes=scratch,
        cost_estimate=pl.CostEstimate(flops=flops, bytes_accessed=moved, transcendentals=0),
        compiler_params=pltpu.CompilerParams(vmem_limit_bytes=limit),
    )


def shaped(shape, dtype=BF16):
    return jax.ShapeDtypeStruct(shape, dtype)


def rows_kernel(x_ref, chip_ref, five_ref, flat):
    c = lax.axis_index("c")
    for k in range(2):
        for m in range(2):
            for t in range(PAIRS):
                flat[256 * m + 4 * t : 256 * m + 4 * t + 4, :] = x_ref[k, m, :, 128 * t : 128 * t + 128].astype(F32)
        for m in range(2):
            for r in range(4):
                chip_ref[4 * k + r, m] = flat[pl.ds(256 * m + r, PAIRS, stride=4), :].astype(BF16)
    five_ref[...] = chip_ref[pl.ds(3 * c, 5)]


def spread_weights(in_ref, out_ref, seen_ref, first_ref, second_ref, obs_ref):
    first_ref[...] = jnp.zeros_like(first_ref)
    second_ref[...] = jnp.zeros_like(second_ref)
    for layer in range(2):
        for dr in range(3):
            for b, j in enumerate(BLOCKS):
                for h in range(2):
                    dc = j - h + 1
                    if 0 <= dc <= 2:
                        at = 64 * (3 * dr + dc)
                        first_ref[layer, 256 * dr + 64 * b : 256 * dr + 64 * b + 64, 256 * h : 256 * h + 256] = (
                            in_ref[layer, at : at + 64, :] * jnp.asarray(0.5, BF16)
                        )
                    dc = h - j + 1
                    if 0 <= dc <= 2:
                        at = 256 * (3 * dr + dc)
                        second_ref[layer, 64 * b : 64 * b + 64, 512 * dr + 256 * h : 512 * dr + 256 * h + 256] = (
                            out_ref[layer, :, at : at + 256]
                        )
    taps = seen_ref[...].astype(F32)
    none = jnp.zeros((8, 64), F32)
    rows = []
    for dr in range(3):
        for h in range(2):
            blocks = [j - h + 1 for j in BLOCKS]
            rows.append(jnp.concatenate(
                [taps[:, 64 * (3 * dr + dc) : 64 * (3 * dr + dc) + 64] if 0 <= dc <= 2 else none for dc in blocks],
                axis=1,
            ))
    obs_ref[...] = jnp.concatenate(rows, axis=0).astype(BF16)


def beside(values, lower):
    at = lax.broadcasted_iota(jnp.int32, values.shape, 1)
    after = jnp.where(at == PAIRS - 1, 0.0, pltpu.roll(values, PAIRS - 1, 1))
    before = jnp.where(at == 0, 0.0, pltpu.roll(values, 1, 1))
    return jnp.where(lower, after, before), jnp.where(lower, before, after)


def mean_over_channels():
    return jnp.where(
        (lax.broadcasted_iota(jnp.int32, (128, 128), 0) < 64) == (lax.broadcasted_iota(jnp.int32, (128, 128), 1) < 64),
        1.0 / 64, 0.0,
    ).astype(BF16)


def patches(a_ref, m, row, values, norm):
    count = values.shape[0]
    wide = values.astype(F32)
    lower = lax.broadcasted_iota(jnp.int32, wide.shape, 2) < 64
    if norm is not None:
        square = (values * values).reshape(count * PAIRS, 128)
        mean = jnp.dot(square, norm, preferred_element_type=F32).reshape(count, PAIRS, 128)
        wide = wide * lax.rsqrt(mean + EPS)
    a_ref[m, pl.ds(row, count), :, 0:128] = wide.astype(BF16)
    a_ref[m, pl.ds(row, count), :, 128:256] = beside(wide, lower)[0].astype(BF16)


def taps_of(ref, m, row, count):
    width = ref.shape[3]
    return jnp.concatenate(
        [ref[m, pl.ds(row + dr, count)].reshape(count * PAIRS, width) for dr in range(3)], axis=1
    )


def first_of(left, weight):
    return jnp.dot(left, weight, preferred_element_type=F32)


def silu(v):
    return v + v * jnp.tanh(v)


def hidden_of(left, weight):
    return silu(first_of(left, weight))


def scaled_rows(values, factors):
    return jnp.concatenate(
        [values[i : i + 1] * factors[i] if i in factors else values[i : i + 1] for i in range(values.shape[0])], axis=0
    )


def second(left, weight):
    return lax.dot_general(left, weight, NT, preferred_element_type=F32)


def updated(products, current):
    count = current.shape[0]
    y = products
    own = y[:, 0:128].reshape(count, PAIRS, 128)
    side = y[:, 128:256].reshape(count, PAIRS, 128)
    lower = lax.broadcasted_iota(jnp.int32, side.shape, 2) < 64
    return current.astype(F32) + own + beside(side, lower)[1]


def by_channel(values_ref, precision_ref, sides_ref):
    own = lax.broadcasted_iota(jnp.int32, (8, 256), 1) % 8 == lax.broadcasted_iota(jnp.int32, (8, 256), 0)
    spread = [
        jnp.concatenate(
            [jnp.where(own, jnp.broadcast_to(ref[r : r + 1, :], (8, 256)), 0.0) for r in range(4)], axis=1
        )
        for ref in (values_ref, precision_ref)
    ]
    whole = jnp.concatenate(spread, axis=0)
    at = lax.broadcasted_iota(jnp.int32, (1024, 128), 0)
    place = jnp.where(at // 8 == lax.broadcasted_iota(jnp.int32, (1024, 128), 1), 1.0, 0.0).astype(BF16)
    high = whole.astype(BF16)
    rest = whole - high.astype(F32)
    middle = rest.astype(BF16)
    low = (rest - middle.astype(F32)).astype(BF16)
    placed = jnp.dot(jnp.concatenate([high, middle, low], axis=0), place, preferred_element_type=F32)
    sides_ref[0:16] = placed[0:16] + placed[16:32] + placed[32:48]


def inner_kernel(chip_ref, in_hbm, out_hbm, seen_hbm, cells_hbm, values_hbm, precision_hbm,
                 a_ref, h_ref, x1_ref, a2_ref, h2_ref, w1_ref, w2_ref, obs_ref, pick_ref, sides_ref,
                 in_ref, out_ref, seen_ref, cells_ref, values_ref, precision_ref, sems):
    sources = (cells_hbm, values_hbm, precision_hbm, seen_hbm, in_hbm, out_hbm)
    targets = (cells_ref, values_ref, precision_ref, seen_ref, in_ref, out_ref)
    fetches = [pltpu.make_async_copy(a, b, sems.at[i]) for i, (a, b) in enumerate(zip(sources, targets))]
    for fetch in fetches:
        fetch.start()
    norm = mean_over_channels()
    for m in range(2):
        for row in (0, 4):
            patches(a_ref, m, row, chip_ref[row : row + 4, m], norm)
    for fetch in fetches[:3]:
        fetch.wait()
    by_channel(values_ref, precision_ref, sides_ref)
    cell = jnp.concatenate([cells_ref[r : r + 1, :] for r in range(4)], axis=1)
    pair = lax.shift_right_logical(cell, 1)
    lane_row = lax.broadcasted_iota(jnp.int32, (1, 128), 1) // 32
    index = lax.broadcasted_iota(jnp.int32, (384, 128), 0)
    for dr in range(3):
        pick_ref[384 * dr : 384 * dr + 384, :] = jnp.where(index == (lane_row + dr) * PAIRS + pair, 1.0, 0.0).astype(BF16)
    sides_ref[16:24] = jnp.broadcast_to((cell & 1).astype(F32), (8, 128))
    for fetch in fetches[3:]:
        fetch.wait()
    spread_weights(in_ref, out_ref, seen_ref, w1_ref, w2_ref, obs_ref)
    for m in range(2):
        for row in (0, 3):
            hidden = hidden_of(taps_of(a_ref, m, row, 3), w1_ref[0])
            h_ref[m, row : row + 3] = hidden.astype(BF16).reshape(3, PAIRS, 512)
    products = [second(taps_of(h_ref, m, 0, 4), w2_ref[0]) for m in range(2)]
    for m in range(2):
        x1_ref[:, m] = updated(products[m], chip_ref[2:6, m]).astype(BF16)
        patches(a2_ref, m, 0, x1_ref[:, m], norm)
    for m in range(2):
        h2_ref[m] = hidden_of(taps_of(a2_ref, m, 0, 2), w1_ref[1]).astype(BF16).reshape(2, PAIRS, 512)


def denoise_kernel(chip_ref, five_ref, a_part, h_part, x1_part, a2_part, h2_part, w1_ref, w2_ref, obs_ref,
                   edge_ref, own_ref, seen_ref, x_ref, a_ref, h_ref, x1_ref, a2_ref, h2_ref, x2_ref, flat):
    c = lax.axis_index("c")
    tile = 2 * lax.axis_index("z") + c
    first = jnp.where(tile == 0, 0.0, 1.0).astype(F32)
    last = jnp.where(tile == 15, 0.0, 1.0).astype(F32)
    start = 5 - 4 * c
    norm = mean_over_channels()
    for m in range(2):
        patches(a_ref, m, 9 * c, five_ref[:, m], norm)
        for k in (0, 6):
            a_ref[m, pl.ds(start + k, 2)] = a_part[m, k : k + 2]
        for k in (0, 4):
            h_ref[m, pl.ds(start + k, 2)] = h_part[m, k : k + 2]
        a2_ref[m, pl.ds(start, 4)] = a2_part[m]
        h2_ref[m, pl.ds(start, 2)] = h2_part[m]
    x_ref[pl.ds(start, 8)] = chip_ref[...]
    x1_ref[pl.ds(start, 4)] = x1_part[...]
    x_ref[pl.ds(9 * c, 5)] = five_ref[...]

    def edges(low, high):
        group = {}
        for q in range(5):
            if q < low or q >= high:
                group[q] = jnp.where(c == 1, last if q >= high else 1.0, first if q < low else 1.0)
        return group

    products = [first_of(taps_of(a_ref, m, 7 * c, 5), w1_ref[0]) for m in range(2)]
    for m in range(2):
        hidden = silu(products[m]).reshape(5, PAIRS, 512)
        h_ref[m, pl.ds(7 * c, 5)] = scaled_rows(hidden, edges(4, 1)).astype(BF16)
    products = [second(taps_of(h_ref, m, 5 * c, 5), w2_ref[0]) for m in range(2)]
    for m in range(2):
        rows = scaled_rows(updated(products[m], x_ref[pl.ds(5 * c + 2, 5), m]), edges(3, 2)).astype(BF16)
        x1_ref[pl.ds(5 * c, 5), m] = rows
        patches(a2_ref, m, 5 * c, rows, norm)
    products = [first_of(taps_of(a2_ref, m, 3 * c, 5), w1_ref[1]) for m in range(2)]
    for m in range(2):
        hidden = silu(products[m]).reshape(5, PAIRS, 512)
        h2_ref[m, pl.ds(3 * c, 5)] = scaled_rows(hidden, edges(2, 3)).astype(BF16)
    products = [second(taps_of(h2_ref, m, c, 5), w2_ref[1]) for m in range(2)]
    for m in range(2):
        rows = scaled_rows(updated(products[m], x1_ref[pl.ds(2 + c, 5), m]), edges(1, 4)).astype(BF16)
        x2_ref[:, m] = rows
        patches(a2_ref, m, 0, rows, None)
    edge_ref[...] = x2_ref[4 - 4 * c]
    for m in range(2):
        seen_ref[m] = lax.dot_general(
            obs_ref[...], a2_ref[m, 0:5].reshape(320, 256), NT, preferred_element_type=F32
        )
    for m in range(2):
        for r in range(4):
            flat[pl.ds(256 * m + r, PAIRS, stride=4), :] = x2_ref[1 - c + r, m].astype(F32)
    for p in range(PEERS):
        both = jnp.concatenate([flat[8 * p : 8 * p + 8], flat[256 + 8 * p : 256 + 8 * p + 8]], axis=0)
        own_ref[p] = both.astype(BF16)


def observe_kernel(edge_ref, own_ref, seen_ref, obs_ref, pick_ref, sides_ref, pay_ref, a_ref):
    c = lax.axis_index("c")
    edge = edge_ref[1 - c]
    for m in range(2):
        patches(a_ref, m, 0, edge[m : m + 1], None)
    both = []
    for m in range(2):
        other = lax.dot_general(obs_ref[...], a_ref[m, 0], NT, preferred_element_type=F32)
        own = seen_ref[m]
        y = jnp.where(c == 1, jnp.concatenate([other, own], axis=1), jnp.concatenate([own, other], axis=1))
        whole = jnp.concatenate([y[16 * dr : 16 * dr + 16] for dr in range(3)], axis=1)
        high = whole.astype(BF16).astype(F32)
        both += [high, whole - high]
    picked = jnp.dot(jnp.concatenate(both, axis=0).astype(BF16), pick_ref[...], preferred_element_type=F32)
    odd = sides_ref[16:24] > 0.5
    got = []
    for m in range(2):
        y = picked[32 * m : 32 * m + 16] + picked[32 * m + 16 : 32 * m + 32]
        got.append(jnp.where(odd, y[8:16], y[0:8]))
    got = jnp.concatenate(got, axis=0).astype(BF16)
    for p in range(PEERS):
        pay_ref[p, 0:16] = own_ref[p]
        pay_ref[p, 16:32] = got


def gram_kernel(got_ref, sides_ref, out_ref, flat):
    for p in range(PEERS):
        flat[16 * p : 16 * p + 16] = got_ref[p, 16:32].astype(F32)
    shape = (64, 128)
    left, right, values = [], [], []
    for o in range(8):
        members = flat[pl.ds(o, 64, stride=8), :]
        mean = jnp.sum(members, axis=0, keepdims=True) * (1.0 / 64)
        left.append((members - mean) * jnp.broadcast_to(sides_ref[8 + o : 9 + o], shape))
        right.append(members.astype(BF16))
        values.append(left[-1] * jnp.broadcast_to(sides_ref[o : o + 1], shape))
    offset = jnp.sum(functools.reduce(jnp.add, values), axis=1, keepdims=True)
    left = jnp.concatenate(left, axis=1)
    right = jnp.concatenate(right, axis=1)
    high = left.astype(BF16)
    halves = jnp.concatenate([high, (left - high.astype(F32)).astype(BF16)], axis=0)
    product = lax.dot_general(halves, jnp.concatenate([right, right], axis=0), NT, preferred_element_type=F32)
    total = offset - (product[0:64] + product[64:128])
    lower = lax.broadcasted_iota(jnp.int32, (32, 128), 1) < 64
    packed = jnp.where(lower, total[0:32], total[32:64]).astype(BF16)
    for t in range(16):
        out_ref[t] = packed


def update_kernel(got_ref, parts_ref, covariance_ref, back_ref, flat):
    total = parts_ref[0].astype(F32)
    for t in range(1, 16):
        total = total + parts_ref[t].astype(F32)
    total = total * (1.0 / 16384)
    covariance = jnp.concatenate([total[:, 0:64], total[:, 64:128]], axis=0)
    covariance_ref[...] = covariance
    center = (covariance - jnp.mean(covariance, axis=0, keepdims=True)) * STEP
    high = center.astype(BF16)
    both = jnp.concatenate([high, (center - high.astype(F32)).astype(BF16)], axis=0)
    for p in range(PEERS):
        flat[16 * p : 16 * p + 16] = got_ref[p, 0:16].astype(F32)
    for s in range(8):
        members = flat[pl.ds(s, 64, stride=8), :]
        narrow = members.astype(BF16)
        moved = lax.dot_general(both, jnp.concatenate([narrow, narrow], axis=0), TN, preferred_element_type=F32)
        flat[pl.ds(s, 64, stride=8), :] = members + moved
    for p in range(PEERS):
        back_ref[p] = flat[16 * p : 16 * p + 16].astype(BF16)


def final_kernel(got_ref, covariance_in, out_ref, covariance_ref):
    covariance_ref[...] = covariance_in[...]
    for p in range(PEERS):
        values = got_ref[p].astype(F32)
        for m in range(2):
            for t in range(2):
                at = 128 * (2 * p + t)
                out_ref[m, :, at : at + 128] = values[8 * m + 4 * t : 8 * m + 4 * t + 4]


def per_device(latents, in_weight, out_weight, observe_weight, obs_cells, obs_values, obs_precision):
    c = lax.axis_index("c")
    across = [pair for z in range(7) for pair in ((2 * z + 1, 2 * z + 2), (2 * z + 2, 2 * z + 1))]
    vmem = pl.BlockSpec(memory_space=pltpu.VMEM)
    hbm = pl.BlockSpec(memory_space=pltpu.HBM)
    chip, five = kernel_call(
        rows_kernel, (shaped((8, 2, PAIRS, 128)), shaped((5, 2, PAIRS, 128))),
        [pltpu.VMEM((512, 128), F32)], moved=300_000,
    )(lax.all_gather(latents, "c"))
    five = lax.ppermute(five, TILE, across)
    *parts, sides = pl.pallas_call(
        inner_kernel,
        out_shape=(
            shaped((2, 8, PAIRS, 256)), shaped((2, 6, PAIRS, 512)), shaped((4, 2, PAIRS, 128)),
            shaped((2, 4, PAIRS, 256)), shaped((2, 2, PAIRS, 512)), shaped((2, 768, 512)), shaped((2, 256, 1536)),
            shaped((48, 256)), shaped((1152, 128)), shaped((24, 128), F32),
        ),
        in_specs=[vmem] + [hbm] * 6,
        scratch_shapes=[
            pltpu.VMEM((2, 576, 256), BF16), pltpu.VMEM((2, 64, 2304), BF16), pltpu.VMEM((8, 576), BF16),
            pltpu.VMEM((4, 32), jnp.int32), pltpu.VMEM((4, 256), F32), pltpu.VMEM((4, 256), F32),
            pltpu.SemaphoreType.DMA((6,)),
        ],
        cost_estimate=pl.CostEstimate(flops=2_000_000_000, bytes_accessed=6_000_000, transcendentals=0),
        compiler_params=pltpu.CompilerParams(vmem_limit_bytes=16 * 1024 * 1024),
    )(chip, *(pltpu.with_memory_space_constraint(v, pltpu.HBM) for v in (
        in_weight, jnp.transpose(out_weight, (0, 2, 1)), jnp.transpose(observe_weight), obs_cells, obs_values,
        obs_precision,
    )))
    *parts, obs, pick = parts
    edge, own, seen = kernel_call(
        denoise_kernel,
        (shaped((2, PAIRS, 128)), shaped((PEERS, 16, 128)), shaped((2, 48, 320), F32)),
        [
            pltpu.VMEM((14, 2, PAIRS, 128), BF16),
            pltpu.VMEM((2, 14, PAIRS, 256), BF16),
            pltpu.VMEM((2, 12, PAIRS, 512), BF16),
            pltpu.VMEM((10, 2, PAIRS, 128), BF16),
            pltpu.VMEM((2, 10, PAIRS, 256), BF16),
            pltpu.VMEM((2, 8, PAIRS, 512), BF16),
            pltpu.VMEM((5, 2, PAIRS, 128), BF16),
            pltpu.VMEM((512, 128), F32),
        ],
        flops=3_000_000_000, moved=4_300_000,
    )(chip, five, *parts, obs)
    pay = kernel_call(
        observe_kernel, shaped((PEERS, 32, 128)), [pltpu.VMEM((2, 1, PAIRS, 256), BF16)], moved=800_000,
    )(lax.all_gather(edge, "c"), own, seen, obs, pick, sides)
    got = lax.all_to_all(pay, MEM, 0, 0, tiled=True)

    parts = kernel_call(
        gram_kernel, shaped((16, 32, 128)), [pltpu.VMEM((512, 128), F32)], moved=700_000,
    )(got, sides)
    parts = lax.all_to_all(parts, TILE, 0, 0, tiled=True)
    covariance, back = kernel_call(
        update_kernel, (shaped((64, 64), F32), shaped((PEERS, 16, 128))), [pltpu.VMEM((512, 128), F32)],
        moved=700_000,
    )(got, parts)
    back = lax.all_to_all(back, MEM, 0, 0, tiled=True)
    return kernel_call(final_kernel, (shaped((2, 4, 8192), F32), shaped((64, 64), F32)), moved=400_000)(back, covariance)


def solution(mesh):
    split = Mesh(mesh.devices.reshape(8, 4, 8, 2), ("y", "x", "z", "c"))
    return jax.shard_map(
        per_device,
        mesh=split,
        in_specs=(P(MEM, TILE, None), P(), P(), P(), P(TILE, None), P(TILE, None), P(TILE, None)),
        out_specs=(P(MEM, TILE, None), P()),
        check_vma=False,
    )
```

```python
import functools

import jax
import jax.numpy as jnp
from jax import lax
from jax.experimental import pallas as pl
from jax.experimental.pallas import tpu as pltpu
from jax.sharding import Mesh
from jax.sharding import PartitionSpec as P

MEM = ("y", "x")
TILE = ("z", "c")
PAIRS = 64
HID = 256
PEERS = 32
EPS = 1e-06
STEP = 0.5
F32 = jnp.float32
BF16 = jnp.bfloat16
LIMIT = 24 * 1024 * 1024
NT = (((1,), (1,)), ((), ()))
TN = (((0,), (0,)), ((), ()))
BLOCKS = (0, 1, 2, -1)


def kernel_call(body, outs, scratch=(), flops=0, moved=0, limit=LIMIT):
    return pl.pallas_call(
        body,
        out_shape=outs,
        scratch_shapes=scratch,
        cost_estimate=pl.CostEstimate(flops=flops, bytes_accessed=moved, transcendentals=0),
        compiler_params=pltpu.CompilerParams(vmem_limit_bytes=limit),
    )


def shaped(shape, dtype=BF16):
    return jax.ShapeDtypeStruct(shape, dtype)


def rows_kernel(x_ref, chip_ref, five_ref, flat):
    c = lax.axis_index("c")
    for k in range(2):
        for m in range(2):
            for t in range(PAIRS):
                flat[256 * m + 4 * t : 256 * m + 4 * t + 4, :] = x_ref[k, m, :, 128 * t : 128 * t + 128].astype(F32)
        for m in range(2):
            for r in range(4):
                chip_ref[4 * k + r, m] = flat[pl.ds(256 * m + r, PAIRS, stride=4), :].astype(BF16)
    five_ref[...] = chip_ref[pl.ds(3 * c, 5)]


def spread_weights(layer, in_ref, out_ref, first_ref, second_ref):
    for dr in range(3):
        for b, j in enumerate(BLOCKS):
            for h in range(2):
                dc, at = j - h + 1, (slice(256 * dr + 64 * b, 256 * dr + 64 * b + 64), slice(256 * h, 256 * h + 256))
                tap = 64 * (3 * dr + dc)
                if 0 <= dc <= 2:
                    first_ref[(layer, *at)] = in_ref[layer, tap : tap + 64, :] * jnp.asarray(0.5, BF16)
                else:
                    first_ref[(layer, *at)] = jnp.zeros((64, 256), BF16)
                dc, at = h - j + 1, (slice(64 * b, 64 * b + 64), slice(512 * dr + 256 * h, 512 * dr + 256 * h + 256))
                tap = 256 * (3 * dr + dc)
                if 0 <= dc <= 2:
                    second_ref[(layer, *at)] = out_ref[layer, :, tap : tap + 256]
                else:
                    second_ref[(layer, *at)] = jnp.zeros((64, 256), BF16)


def spread_observed(seen_ref, obs_ref):
    taps = seen_ref[...].astype(F32)
    none = jnp.zeros((8, 64), F32)
    rows = []
    for dr in range(3):
        for h in range(2):
            blocks = [j - h + 1 for j in BLOCKS]
            rows.append(jnp.concatenate(
                [taps[:, 64 * (3 * dr + dc) : 64 * (3 * dr + dc) + 64] if 0 <= dc <= 2 else none for dc in blocks],
                axis=1,
            ))
    obs_ref[...] = jnp.concatenate(rows, axis=0).astype(BF16)


def beside(values, lower):
    at = lax.broadcasted_iota(jnp.int32, values.shape, 1)
    after = jnp.where(at == PAIRS - 1, 0.0, pltpu.roll(values, PAIRS - 1, 1))
    before = jnp.where(at == 0, 0.0, pltpu.roll(values, 1, 1))
    return jnp.where(lower, after, before), jnp.where(lower, before, after)


def mean_over_channels():
    return jnp.where(
        (lax.broadcasted_iota(jnp.int32, (128, 128), 0) < 64) == (lax.broadcasted_iota(jnp.int32, (128, 128), 1) < 64),
        1.0 / 64, 0.0,
    ).astype(BF16)


def patches(a_ref, m, row, values, norm):
    count = values.shape[0]
    wide = values.astype(F32)
    lower = lax.broadcasted_iota(jnp.int32, wide.shape, 2) < 64
    if norm is not None:
        square = (values * values).reshape(count * PAIRS, 128)
        mean = jnp.dot(square, norm, preferred_element_type=F32).reshape(count, PAIRS, 128)
        wide = wide * lax.rsqrt(mean + EPS)
    a_ref[m, pl.ds(row, count), :, 0:128] = wide.astype(BF16)
    a_ref[m, pl.ds(row, count), :, 128:256] = beside(wide, lower)[0].astype(BF16)


def taps_of(ref, m, row, count):
    width = ref.shape[3]
    return jnp.concatenate(
        [ref[m, pl.ds(row + dr, count)].reshape(count * PAIRS, width) for dr in range(3)], axis=1
    )


def first_of(left, weight):
    return jnp.dot(left, weight, preferred_element_type=F32)


def silu(v):
    return v + v * jnp.tanh(v)


def scaled_rows(values, factors):
    return jnp.concatenate(
        [values[i : i + 1] * factors[i] if i in factors else values[i : i + 1] for i in range(values.shape[0])], axis=0
    )


def second(left, weight):
    return lax.dot_general(left, weight, NT, preferred_element_type=F32)


def updated(products, current):
    count = current.shape[0]
    y = products
    own = y[:, 0:128].reshape(count, PAIRS, 128)
    side = y[:, 128:256].reshape(count, PAIRS, 128)
    lower = lax.broadcasted_iota(jnp.int32, side.shape, 2) < 64
    return current.astype(F32) + own + beside(side, lower)[1]


def by_channel(values_ref, precision_ref, sides_ref):
    own = lax.broadcasted_iota(jnp.int32, (8, 256), 1) % 8 == lax.broadcasted_iota(jnp.int32, (8, 256), 0)
    spread = [
        jnp.concatenate(
            [jnp.where(own, jnp.broadcast_to(ref[r : r + 1, :], (8, 256)), 0.0) for r in range(4)], axis=1
        )
        for ref in (values_ref, precision_ref)
    ]
    whole = jnp.concatenate(spread, axis=0)
    at = lax.broadcasted_iota(jnp.int32, (1024, 128), 0)
    place = jnp.where(at // 8 == lax.broadcasted_iota(jnp.int32, (1024, 128), 1), 1.0, 0.0).astype(BF16)
    high = whole.astype(BF16)
    rest = whole - high.astype(F32)
    middle = rest.astype(BF16)
    low = (rest - middle.astype(F32)).astype(BF16)
    placed = jnp.dot(jnp.concatenate([high, middle, low], axis=0), place, preferred_element_type=F32)
    sides_ref[0:16] = placed[0:16] + placed[16:32] + placed[32:48]


def inner_kernel(chip_ref, in_hbm, out_hbm, seen_hbm, cells_hbm, values_hbm, precision_hbm,
                 a_ref, h_ref, x1_ref, a2_ref, h2_ref, w1_ref, w2_ref, obs_ref, pick_ref, sides_ref,
                 in_ref, out_ref, seen_ref, cells_ref, values_ref, precision_ref, sems):
    sources = (cells_hbm, values_hbm, precision_hbm, seen_hbm, in_hbm, out_hbm)
    targets = (cells_ref, values_ref, precision_ref, seen_ref, in_ref, out_ref)
    fetches = [pltpu.make_async_copy(a, b, sems.at[i]) for i, (a, b) in enumerate(zip(sources, targets))]
    for fetch in fetches:
        fetch.start()
    norm = mean_over_channels()
    for m in range(2):
        for row in (0, 4):
            patches(a_ref, m, row, chip_ref[row : row + 4, m], norm)
    for fetch in fetches[:3]:
        fetch.wait()
    by_channel(values_ref, precision_ref, sides_ref)
    for fetch in fetches[3:]:
        fetch.wait()
    spread_weights(0, in_ref, out_ref, w1_ref, w2_ref)
    products = [first_of(taps_of(a_ref, m, 0, 6), w1_ref[0]) for m in range(2)]
    spread_observed(seen_ref, obs_ref)
    cell = jnp.concatenate([cells_ref[r : r + 1, :] for r in range(4)], axis=1)
    pair = lax.shift_right_logical(cell, 1)
    lane_row = lax.broadcasted_iota(jnp.int32, (1, 128), 1) // 32
    index = lax.broadcasted_iota(jnp.int32, (384, 128), 0)
    for dr in range(3):
        pick_ref[384 * dr : 384 * dr + 384, :] = jnp.where(index == (lane_row + dr) * PAIRS + pair, 1.0, 0.0).astype(BF16)
    sides_ref[16:24] = jnp.broadcast_to((cell & 1).astype(F32), (8, 128))
    spread_weights(1, in_ref, out_ref, w1_ref, w2_ref)
    for m in range(2):
        h_ref[m] = silu(products[m]).astype(BF16).reshape(6, PAIRS, 512)
    products = [second(taps_of(h_ref, m, 0, 4), w2_ref[0]) for m in range(2)]
    for m in range(2):
        x1_ref[:, m] = updated(products[m], chip_ref[2:6, m]).astype(BF16)
        patches(a2_ref, m, 0, x1_ref[:, m], norm)
    products = [first_of(taps_of(a2_ref, m, 0, 2), w1_ref[1]) for m in range(2)]
    for m in range(2):
        h2_ref[m] = silu(products[m]).astype(BF16).reshape(2, PAIRS, 512)


def denoise_kernel(chip_ref, five_ref, a_part, h_part, x1_part, a2_part, h2_part, w1_ref, w2_ref, obs_ref,
                   edge_ref, own_ref, seen_ref, x_ref, a_ref, h_ref, x1_ref, a2_ref, h2_ref, x2_ref, flat):
    c = lax.axis_index("c")
    tile = 2 * lax.axis_index("z") + c
    first = jnp.where(tile == 0, 0.0, 1.0).astype(F32)
    last = jnp.where(tile == 15, 0.0, 1.0).astype(F32)
    start = 5 - 4 * c
    norm = mean_over_channels()
    for m in range(2):
        patches(a_ref, m, 9 * c, five_ref[:, m], norm)
        for k in (0, 6):
            a_ref[m, pl.ds(start + k, 2)] = a_part[m, k : k + 2]
        for k in (0, 4):
            h_ref[m, pl.ds(start + k, 2)] = h_part[m, k : k + 2]
        a2_ref[m, pl.ds(start, 4)] = a2_part[m]
        h2_ref[m, pl.ds(start, 2)] = h2_part[m]
    x_ref[pl.ds(start, 8)] = chip_ref[...]
    x1_ref[pl.ds(start, 4)] = x1_part[...]
    x_ref[pl.ds(9 * c, 5)] = five_ref[...]

    def edges(low, high):
        group = {}
        for q in range(5):
            if q < low or q >= high:
                group[q] = jnp.where(c == 1, last if q >= high else 1.0, first if q < low else 1.0)
        return group

    products = [first_of(taps_of(a_ref, m, 7 * c, 5), w1_ref[0]) for m in range(2)]
    for m in range(2):
        hidden = silu(products[m]).reshape(5, PAIRS, 512)
        h_ref[m, pl.ds(7 * c, 5)] = scaled_rows(hidden, edges(4, 1)).astype(BF16)
    products = [second(taps_of(h_ref, m, 5 * c, 5), w2_ref[0]) for m in range(2)]
    for m in range(2):
        rows = scaled_rows(updated(products[m], x_ref[pl.ds(5 * c + 2, 5), m]), edges(3, 2)).astype(BF16)
        x1_ref[pl.ds(5 * c, 5), m] = rows
        patches(a2_ref, m, 5 * c, rows, norm)
    products = [first_of(taps_of(a2_ref, m, 3 * c, 5), w1_ref[1]) for m in range(2)]
    for m in range(2):
        hidden = silu(products[m]).reshape(5, PAIRS, 512)
        h2_ref[m, pl.ds(3 * c, 5)] = scaled_rows(hidden, edges(2, 3)).astype(BF16)
    products = [second(taps_of(h2_ref, m, c, 5), w2_ref[1]) for m in range(2)]
    for m in range(2):
        rows = scaled_rows(updated(products[m], x1_ref[pl.ds(2 + c, 5), m]), edges(1, 4)).astype(BF16)
        x2_ref[:, m] = rows
        patches(a2_ref, m, 0, rows, None)
    edge_ref[...] = x2_ref[4 - 4 * c]
    for m in range(2):
        seen_ref[m] = lax.dot_general(
            obs_ref[...], a2_ref[m, 0:5].reshape(320, 256), NT, preferred_element_type=F32
        )
    for m in range(2):
        for r in range(4):
            flat[pl.ds(256 * m + r, PAIRS, stride=4), :] = x2_ref[1 - c + r, m].astype(F32)
    for p in range(PEERS):
        both = jnp.concatenate([flat[8 * p : 8 * p + 8], flat[256 + 8 * p : 256 + 8 * p + 8]], axis=0)
        own_ref[p] = both.astype(BF16)


def observe_kernel(edge_ref, own_ref, seen_ref, obs_ref, pick_ref, sides_ref, pay_ref, a_ref):
    c = lax.axis_index("c")
    edge = edge_ref[1 - c]
    for m in range(2):
        patches(a_ref, m, 0, edge[m : m + 1], None)
    both = []
    for m in range(2):
        other = lax.dot_general(obs_ref[...], a_ref[m, 0], NT, preferred_element_type=F32)
        own = seen_ref[m]
        y = jnp.where(c == 1, jnp.concatenate([other, own], axis=1), jnp.concatenate([own, other], axis=1))
        whole = jnp.concatenate([y[16 * dr : 16 * dr + 16] for dr in range(3)], axis=1)
        high = whole.astype(BF16).astype(F32)
        both += [high, whole - high]
    picked = jnp.dot(jnp.concatenate(both, axis=0).astype(BF16), pick_ref[...], preferred_element_type=F32)
    odd = sides_ref[16:24] > 0.5
    got = []
    for m in range(2):
        y = picked[32 * m : 32 * m + 16] + picked[32 * m + 16 : 32 * m + 32]
        got.append(jnp.where(odd, y[8:16], y[0:8]))
    got = jnp.concatenate(got, axis=0).astype(BF16)
    for p in range(PEERS):
        pay_ref[p, 0:16] = own_ref[p]
        pay_ref[p, 16:32] = got


def gram_kernel(got_ref, sides_ref, out_ref, flat):
    for p in range(PEERS):
        flat[16 * p : 16 * p + 16] = got_ref[p, 16:32].astype(F32)
    shape = (64, 128)
    left, right, values = [], [], []
    for o in range(8):
        members = flat[pl.ds(o, 64, stride=8), :]
        mean = jnp.sum(members, axis=0, keepdims=True) * (1.0 / 64)
        left.append((members - mean) * jnp.broadcast_to(sides_ref[8 + o : 9 + o], shape))
        right.append(members.astype(BF16))
        values.append(left[-1] * jnp.broadcast_to(sides_ref[o : o + 1], shape))
    offset = jnp.sum(functools.reduce(jnp.add, values), axis=1, keepdims=True)
    left = jnp.concatenate(left, axis=1)
    right = jnp.concatenate(right, axis=1)
    high = left.astype(BF16)
    halves = jnp.concatenate([high, (left - high.astype(F32)).astype(BF16)], axis=0)
    product = lax.dot_general(halves, jnp.concatenate([right, right], axis=0), NT, preferred_element_type=F32)
    total = offset - (product[0:64] + product[64:128])
    lower = lax.broadcasted_iota(jnp.int32, (32, 128), 1) < 64
    packed = jnp.where(lower, total[0:32], total[32:64]).astype(BF16)
    for t in range(16):
        out_ref[t] = packed


def update_kernel(got_ref, parts_ref, covariance_ref, back_ref, flat):
    total = parts_ref[0].astype(F32)
    for t in range(1, 16):
        total = total + parts_ref[t].astype(F32)
    total = total * (1.0 / 16384)
    covariance = jnp.concatenate([total[:, 0:64], total[:, 64:128]], axis=0)
    covariance_ref[...] = covariance
    center = (covariance - jnp.mean(covariance, axis=0, keepdims=True)) * STEP
    high = center.astype(BF16)
    both = jnp.concatenate([high, (center - high.astype(F32)).astype(BF16)], axis=0)
    for p in range(PEERS):
        flat[16 * p : 16 * p + 16] = got_ref[p, 0:16].astype(F32)
    for s in range(8):
        members = flat[pl.ds(s, 64, stride=8), :]
        narrow = members.astype(BF16)
        moved = lax.dot_general(both, jnp.concatenate([narrow, narrow], axis=0), TN, preferred_element_type=F32)
        flat[pl.ds(s, 64, stride=8), :] = members + moved
    for p in range(PEERS):
        back_ref[p] = flat[16 * p : 16 * p + 16].astype(BF16)


def final_kernel(got_ref, covariance_in, out_ref, covariance_ref):
    covariance_ref[...] = covariance_in[...]
    for p in range(PEERS):
        values = got_ref[p].astype(F32)
        for m in range(2):
            for t in range(2):
                at = 128 * (2 * p + t)
                out_ref[m, :, at : at + 128] = values[8 * m + 4 * t : 8 * m + 4 * t + 4]


def per_device(latents, in_weight, out_weight, observe_weight, obs_cells, obs_values, obs_precision):
    c = lax.axis_index("c")
    across = [pair for z in range(7) for pair in ((2 * z + 1, 2 * z + 2), (2 * z + 2, 2 * z + 1))]
    vmem = pl.BlockSpec(memory_space=pltpu.VMEM)
    hbm = pl.BlockSpec(memory_space=pltpu.HBM)
    chip, five = kernel_call(
        rows_kernel, (shaped((8, 2, PAIRS, 128)), shaped((5, 2, PAIRS, 128))),
        [pltpu.VMEM((512, 128), F32)], moved=300_000,
    )(lax.all_gather(latents, "c"))
    five = lax.ppermute(five, TILE, across)
    *parts, sides = pl.pallas_call(
        inner_kernel,
        out_shape=(
            shaped((2, 8, PAIRS, 256)), shaped((2, 6, PAIRS, 512)), shaped((4, 2, PAIRS, 128)),
            shaped((2, 4, PAIRS, 256)), shaped((2, 2, PAIRS, 512)), shaped((2, 768, 512)), shaped((2, 256, 1536)),
            shaped((48, 256)), shaped((1152, 128)), shaped((24, 128), F32),
        ),
        in_specs=[vmem] + [hbm] * 6,
        scratch_shapes=[
            pltpu.VMEM((2, 576, 256), BF16), pltpu.VMEM((2, 64, 2304), BF16), pltpu.VMEM((8, 576), BF16),
            pltpu.VMEM((4, 32), jnp.int32), pltpu.VMEM((4, 256), F32), pltpu.VMEM((4, 256), F32),
            pltpu.SemaphoreType.DMA((6,)),
        ],
        cost_estimate=pl.CostEstimate(flops=2_000_000_000, bytes_accessed=6_000_000, transcendentals=0),
        compiler_params=pltpu.CompilerParams(vmem_limit_bytes=16 * 1024 * 1024),
    )(chip, *(pltpu.with_memory_space_constraint(v, pltpu.HBM) for v in (
        in_weight, jnp.transpose(out_weight, (0, 2, 1)), jnp.transpose(observe_weight), obs_cells, obs_values,
        obs_precision,
    )))
    *parts, obs, pick = parts
    edge, own, seen = kernel_call(
        denoise_kernel,
        (shaped((2, PAIRS, 128)), shaped((PEERS, 16, 128)), shaped((2, 48, 320), F32)),
        [
            pltpu.VMEM((14, 2, PAIRS, 128), BF16),
            pltpu.VMEM((2, 14, PAIRS, 256), BF16),
            pltpu.VMEM((2, 12, PAIRS, 512), BF16),
            pltpu.VMEM((10, 2, PAIRS, 128), BF16),
            pltpu.VMEM((2, 10, PAIRS, 256), BF16),
            pltpu.VMEM((2, 8, PAIRS, 512), BF16),
            pltpu.VMEM((5, 2, PAIRS, 128), BF16),
            pltpu.VMEM((512, 128), F32),
        ],
        flops=3_000_000_000, moved=4_300_000,
    )(chip, five, *parts, obs)
    pay = kernel_call(
        observe_kernel, shaped((PEERS, 32, 128)), [pltpu.VMEM((2, 1, PAIRS, 256), BF16)], moved=800_000,
    )(lax.all_gather(edge, "c"), own, seen, obs, pick, sides)
    got = lax.all_to_all(pay, MEM, 0, 0, tiled=True)

    parts = kernel_call(
        gram_kernel, shaped((16, 32, 128)), [pltpu.VMEM((512, 128), F32)], moved=700_000,
    )(got, sides)
    parts = lax.all_to_all(parts, TILE, 0, 0, tiled=True)
    covariance, back = kernel_call(
        update_kernel, (shaped((64, 64), F32), shaped((PEERS, 16, 128))), [pltpu.VMEM((512, 128), F32)],
        moved=700_000,
    )(got, parts)
    back = lax.all_to_all(back, MEM, 0, 0, tiled=True)
    return kernel_call(final_kernel, (shaped((2, 4, 8192), F32), shaped((64, 64), F32)), moved=400_000)(back, covariance)


def solution(mesh):
    split = Mesh(mesh.devices.reshape(8, 4, 8, 2), ("y", "x", "z", "c"))
    return jax.shard_map(
        per_device,
        mesh=split,
        in_specs=(P(MEM, TILE, None), P(), P(), P(), P(TILE, None), P(TILE, None), P(TILE, None)),
        out_specs=(P(MEM, TILE, None), P()),
        check_vma=False,
    )
```

```python
import functools

import jax
import jax.numpy as jnp
from jax import lax
from jax.experimental import pallas as pl
from jax.experimental.pallas import tpu as pltpu
from jax.sharding import Mesh
from jax.sharding import PartitionSpec as P

MEM = ("y", "x")
TILE = ("z", "c")
PAIRS = 64
HID = 256
PEERS = 32
EPS = 1e-06
STEP = 0.5
F32 = jnp.float32
BF16 = jnp.bfloat16
LIMIT = 24 * 1024 * 1024
NT = (((1,), (1,)), ((), ()))
TN = (((0,), (0,)), ((), ()))
BLOCKS = (0, 1, 2, -1)


def kernel_call(body, outs, scratch=(), flops=0, moved=0, limit=LIMIT):
    return pl.pallas_call(
        body,
        out_shape=outs,
        scratch_shapes=scratch,
        cost_estimate=pl.CostEstimate(flops=flops, bytes_accessed=moved, transcendentals=0),
        compiler_params=pltpu.CompilerParams(vmem_limit_bytes=limit),
    )


def shaped(shape, dtype=BF16):
    return jax.ShapeDtypeStruct(shape, dtype)


def rows_kernel(x_ref, chip_ref, five_ref, flat):
    c = lax.axis_index("c")
    for k in range(2):
        for m in range(2):
            for t in range(PAIRS):
                flat[256 * m + 4 * t : 256 * m + 4 * t + 4, :] = x_ref[k, m, :, 128 * t : 128 * t + 128].astype(F32)
        for m in range(2):
            for r in range(4):
                chip_ref[4 * k + r, m] = flat[pl.ds(256 * m + r, PAIRS, stride=4), :].astype(BF16)
    five_ref[...] = chip_ref[pl.ds(3 * c, 5)]


def spread_weights(layer, in_ref, out_ref, first_ref, second_ref):
    for dr in range(3):
        for b, j in enumerate(BLOCKS):
            for h in range(2):
                dc, at = j - h + 1, (slice(256 * dr + 64 * b, 256 * dr + 64 * b + 64), slice(256 * h, 256 * h + 256))
                tap = 64 * (3 * dr + dc)
                if 0 <= dc <= 2:
                    first_ref[(layer, *at)] = in_ref[layer, tap : tap + 64, :] * jnp.asarray(0.5, BF16)
                else:
                    first_ref[(layer, *at)] = jnp.zeros((64, 256), BF16)
                dc, at = h - j + 1, (slice(64 * b, 64 * b + 64), slice(512 * dr + 256 * h, 512 * dr + 256 * h + 256))
                tap = 256 * (3 * dr + dc)
                if 0 <= dc <= 2:
                    second_ref[(layer, *at)] = out_ref[layer, :, tap : tap + 256]
                else:
                    second_ref[(layer, *at)] = jnp.zeros((64, 256), BF16)


def spread_observed(seen_ref, obs_ref):
    taps = seen_ref[...].astype(F32)
    none = jnp.zeros((8, 64), F32)
    rows = []
    for dr in range(3):
        for h in range(2):
            blocks = [j - h + 1 for j in BLOCKS]
            rows.append(jnp.concatenate(
                [taps[:, 64 * (3 * dr + dc) : 64 * (3 * dr + dc) + 64] if 0 <= dc <= 2 else none for dc in blocks],
                axis=1,
            ))
    obs_ref[...] = jnp.concatenate(rows, axis=0).astype(BF16)


def beside(values, lower):
    at = lax.broadcasted_iota(jnp.int32, values.shape, 1)
    after = jnp.where(at == PAIRS - 1, 0.0, pltpu.roll(values, PAIRS - 1, 1))
    before = jnp.where(at == 0, 0.0, pltpu.roll(values, 1, 1))
    return jnp.where(lower, after, before), jnp.where(lower, before, after)


def mean_over_channels():
    return jnp.where(
        (lax.broadcasted_iota(jnp.int32, (128, 128), 0) < 64) == (lax.broadcasted_iota(jnp.int32, (128, 128), 1) < 64),
        1.0 / 64, 0.0,
    ).astype(BF16)


def patches(a_ref, m, row, values, norm):
    count = values.shape[0]
    wide = values.astype(F32)
    lower = lax.broadcasted_iota(jnp.int32, wide.shape, 2) < 64
    if norm is not None:
        square = (values * values).reshape(count * PAIRS, 128)
        mean = jnp.dot(square, norm, preferred_element_type=F32).reshape(count, PAIRS, 128)
        wide = wide * lax.rsqrt(mean + EPS)
    a_ref[m, pl.ds(row, count), :, 0:128] = wide.astype(BF16)
    a_ref[m, pl.ds(row, count), :, 128:256] = beside(wide, lower)[0].astype(BF16)


def taps_of(ref, m, row, count):
    width = ref.shape[3]
    return jnp.concatenate(
        [ref[m, pl.ds(row + dr, count)].reshape(count * PAIRS, width) for dr in range(3)], axis=1
    )


def first_of(left, weight):
    return jnp.dot(left, weight, preferred_element_type=F32)


def silu(v):
    return v + v * jnp.tanh(v)


def scaled_rows(values, factors):
    return jnp.concatenate(
        [values[i : i + 1] * factors[i] if i in factors else values[i : i + 1] for i in range(values.shape[0])], axis=0
    )


def second(left, weight):
    return lax.dot_general(left, weight, NT, preferred_element_type=F32)


def updated(products, current):
    count = current.shape[0]
    y = products
    own = y[:, 0:128].reshape(count, PAIRS, 128)
    side = y[:, 128:256].reshape(count, PAIRS, 128)
    lower = lax.broadcasted_iota(jnp.int32, side.shape, 2) < 64
    return current.astype(F32) + own + beside(side, lower)[1]


def by_channel(values_ref, precision_ref, sides_ref):
    own = lax.broadcasted_iota(jnp.int32, (8, 256), 1) % 8 == lax.broadcasted_iota(jnp.int32, (8, 256), 0)
    spread = [
        jnp.concatenate(
            [jnp.where(own, jnp.broadcast_to(ref[r : r + 1, :], (8, 256)), 0.0) for r in range(4)], axis=1
        )
        for ref in (values_ref, precision_ref)
    ]
    whole = jnp.concatenate(spread, axis=0)
    at = lax.broadcasted_iota(jnp.int32, (1024, 128), 0)
    place = jnp.where(at // 8 == lax.broadcasted_iota(jnp.int32, (1024, 128), 1), 1.0, 0.0).astype(BF16)
    high = whole.astype(BF16)
    rest = whole - high.astype(F32)
    middle = rest.astype(BF16)
    low = (rest - middle.astype(F32)).astype(BF16)
    placed = jnp.dot(jnp.concatenate([high, middle, low], axis=0), place, preferred_element_type=F32)
    sides_ref[0:16] = placed[0:16] + placed[16:32] + placed[32:48]


def inner_kernel(chip_ref, in_hbm, out_hbm, seen_hbm, cells_hbm, values_hbm, precision_hbm,
                 a_ref, h_ref, x1_ref, a2_ref, h2_ref, w1_ref, w2_ref, obs_ref, pick_ref, sides_ref,
                 in_ref, out_ref, seen_ref, cells_ref, values_ref, precision_ref, sems):
    sources = (in_hbm, out_hbm, cells_hbm, values_hbm, precision_hbm, seen_hbm)
    targets = (in_ref, out_ref, cells_ref, values_ref, precision_ref, seen_ref)
    fetches = [pltpu.make_async_copy(a, b, sems.at[i]) for i, (a, b) in enumerate(zip(sources, targets))]
    for fetch in fetches:
        fetch.start()
    norm = mean_over_channels()
    for m in range(2):
        for row in (0, 4):
            patches(a_ref, m, row, chip_ref[row : row + 4, m], norm)
    for fetch in fetches[2:5]:
        fetch.wait()
    by_channel(values_ref, precision_ref, sides_ref)
    for fetch in fetches[:2] + fetches[5:]:
        fetch.wait()
    spread_weights(0, in_ref, out_ref, w1_ref, w2_ref)
    products = [first_of(taps_of(a_ref, m, 0, 6), w1_ref[0]) for m in range(2)]
    spread_observed(seen_ref, obs_ref)
    cell = jnp.concatenate([cells_ref[r : r + 1, :] for r in range(4)], axis=1)
    pair = lax.shift_right_logical(cell, 1)
    lane_row = lax.broadcasted_iota(jnp.int32, (1, 128), 1) // 32
    index = lax.broadcasted_iota(jnp.int32, (384, 128), 0)
    for dr in range(3):
        pick_ref[384 * dr : 384 * dr + 384, :] = jnp.where(index == (lane_row + dr) * PAIRS + pair, 1.0, 0.0).astype(BF16)
    sides_ref[16:24] = jnp.broadcast_to((cell & 1).astype(F32), (8, 128))
    spread_weights(1, in_ref, out_ref, w1_ref, w2_ref)
    for m in range(2):
        h_ref[m] = silu(products[m]).astype(BF16).reshape(6, PAIRS, 512)
    products = [second(taps_of(h_ref, m, 0, 4), w2_ref[0]) for m in range(2)]
    for m in range(2):
        x1_ref[:, m] = updated(products[m], chip_ref[2:6, m]).astype(BF16)
        patches(a2_ref, m, 0, x1_ref[:, m], norm)
    products = [first_of(taps_of(a2_ref, m, 0, 2), w1_ref[1]) for m in range(2)]
    for m in range(2):
        h2_ref[m] = silu(products[m]).astype(BF16).reshape(2, PAIRS, 512)


def denoise_kernel(chip_ref, five_ref, a_part, h_part, x1_part, a2_part, h2_part, w1_ref, w2_ref, obs_ref,
                   edge_ref, own_ref, seen_ref, x_ref, a_ref, h_ref, x1_ref, a2_ref, h2_ref, x2_ref, flat):
    c = lax.axis_index("c")
    tile = 2 * lax.axis_index("z") + c
    first = jnp.where(tile == 0, 0.0, 1.0).astype(F32)
    last = jnp.where(tile == 15, 0.0, 1.0).astype(F32)
    start = 5 - 4 * c
    norm = mean_over_channels()
    for m in range(2):
        patches(a_ref, m, 9 * c, five_ref[:, m], norm)
        for k in (0, 6):
            a_ref[m, pl.ds(start + k, 2)] = a_part[m, k : k + 2]
        for k in (0, 4):
            h_ref[m, pl.ds(start + k, 2)] = h_part[m, k : k + 2]
        a2_ref[m, pl.ds(start, 4)] = a2_part[m]
        h2_ref[m, pl.ds(start, 2)] = h2_part[m]
    x_ref[pl.ds(start, 8)] = chip_ref[...]
    x1_ref[pl.ds(start, 4)] = x1_part[...]
    x_ref[pl.ds(9 * c, 5)] = five_ref[...]

    def edges(low, high):
        group = {}
        for q in range(5):
            if q < low or q >= high:
                group[q] = jnp.where(c == 1, last if q >= high else 1.0, first if q < low else 1.0)
        return group

    products = [first_of(taps_of(a_ref, m, 7 * c, 5), w1_ref[0]) for m in range(2)]
    for m in range(2):
        hidden = silu(products[m]).reshape(5, PAIRS, 512)
        h_ref[m, pl.ds(7 * c, 5)] = scaled_rows(hidden, edges(4, 1)).astype(BF16)
    products = [second(taps_of(h_ref, m, 5 * c, 5), w2_ref[0]) for m in range(2)]
    for m in range(2):
        rows = scaled_rows(updated(products[m], x_ref[pl.ds(5 * c + 2, 5), m]), edges(3, 2)).astype(BF16)
        x1_ref[pl.ds(5 * c, 5), m] = rows
        patches(a2_ref, m, 5 * c, rows, norm)
    products = [first_of(taps_of(a2_ref, m, 3 * c, 5), w1_ref[1]) for m in range(2)]
    for m in range(2):
        hidden = silu(products[m]).reshape(5, PAIRS, 512)
        h2_ref[m, pl.ds(3 * c, 5)] = scaled_rows(hidden, edges(2, 3)).astype(BF16)
    products = [second(taps_of(h2_ref, m, c, 5), w2_ref[1]) for m in range(2)]
    for m in range(2):
        rows = scaled_rows(updated(products[m], x1_ref[pl.ds(2 + c, 5), m]), edges(1, 4)).astype(BF16)
        x2_ref[:, m] = rows
        patches(a2_ref, m, 0, rows, None)
    edge_ref[...] = x2_ref[4 - 4 * c]
    for m in range(2):
        seen_ref[m] = lax.dot_general(
            obs_ref[...], a2_ref[m, 0:5].reshape(320, 256), NT, preferred_element_type=F32
        )
    for m in range(2):
        for r in range(4):
            flat[pl.ds(256 * m + r, PAIRS, stride=4), :] = x2_ref[1 - c + r, m].astype(F32)
    for p in range(PEERS):
        both = jnp.concatenate([flat[8 * p : 8 * p + 8], flat[256 + 8 * p : 256 + 8 * p + 8]], axis=0)
        own_ref[p] = both.astype(BF16)


def observe_kernel(edge_ref, own_ref, seen_ref, obs_ref, pick_ref, sides_ref, pay_ref, a_ref):
    c = lax.axis_index("c")
    edge = edge_ref[1 - c]
    for m in range(2):
        patches(a_ref, m, 0, edge[m : m + 1], None)
    both = []
    for m in range(2):
        other = lax.dot_general(obs_ref[...], a_ref[m, 0], NT, preferred_element_type=F32)
        own = seen_ref[m]
        y = jnp.where(c == 1, jnp.concatenate([other, own], axis=1), jnp.concatenate([own, other], axis=1))
        whole = jnp.concatenate([y[16 * dr : 16 * dr + 16] for dr in range(3)], axis=1)
        high = whole.astype(BF16).astype(F32)
        both += [high, whole - high]
    picked = jnp.dot(jnp.concatenate(both, axis=0).astype(BF16), pick_ref[...], preferred_element_type=F32)
    odd = sides_ref[16:24] > 0.5
    got = []
    for m in range(2):
        y = picked[32 * m : 32 * m + 16] + picked[32 * m + 16 : 32 * m + 32]
        got.append(jnp.where(odd, y[8:16], y[0:8]))
    got = jnp.concatenate(got, axis=0).astype(BF16)
    for p in range(PEERS):
        pay_ref[p, 0:16] = own_ref[p]
        pay_ref[p, 16:32] = got


def gram_kernel(got_ref, sides_ref, out_ref, flat):
    for p in range(PEERS):
        flat[16 * p : 16 * p + 16] = got_ref[p, 16:32].astype(F32)
    shape = (64, 128)
    left, right, values = [], [], []
    for o in range(8):
        members = flat[pl.ds(o, 64, stride=8), :]
        mean = jnp.sum(members, axis=0, keepdims=True) * (1.0 / 64)
        left.append((members - mean) * jnp.broadcast_to(sides_ref[8 + o : 9 + o], shape))
        right.append(members.astype(BF16))
        values.append(left[-1] * jnp.broadcast_to(sides_ref[o : o + 1], shape))
    offset = jnp.sum(functools.reduce(jnp.add, values), axis=1, keepdims=True)
    left = jnp.concatenate(left, axis=1)
    right = jnp.concatenate(right, axis=1)
    high = left.astype(BF16)
    halves = jnp.concatenate([high, (left - high.astype(F32)).astype(BF16)], axis=0)
    product = lax.dot_general(halves, jnp.concatenate([right, right], axis=0), NT, preferred_element_type=F32)
    total = offset - (product[0:64] + product[64:128])
    lower = lax.broadcasted_iota(jnp.int32, (32, 128), 1) < 64
    packed = jnp.where(lower, total[0:32], total[32:64]).astype(BF16)
    for t in range(16):
        out_ref[t] = packed


def update_kernel(got_ref, parts_ref, covariance_ref, back_ref, flat):
    total = parts_ref[0].astype(F32)
    for t in range(1, 16):
        total = total + parts_ref[t].astype(F32)
    total = total * (1.0 / 16384)
    covariance = jnp.concatenate([total[:, 0:64], total[:, 64:128]], axis=0)
    covariance_ref[...] = covariance
    center = (covariance - jnp.mean(covariance, axis=0, keepdims=True)) * STEP
    high = center.astype(BF16)
    both = jnp.concatenate([high, (center - high.astype(F32)).astype(BF16)], axis=0)
    for p in range(PEERS):
        flat[16 * p : 16 * p + 16] = got_ref[p, 0:16].astype(F32)
    for s in range(8):
        members = flat[pl.ds(s, 64, stride=8), :]
        narrow = members.astype(BF16)
        moved = lax.dot_general(both, jnp.concatenate([narrow, narrow], axis=0), TN, preferred_element_type=F32)
        flat[pl.ds(s, 64, stride=8), :] = members + moved
    for p in range(PEERS):
        back_ref[p] = flat[16 * p : 16 * p + 16].astype(BF16)


def final_kernel(got_ref, covariance_in, out_ref, covariance_ref):
    covariance_ref[...] = covariance_in[...]
    for p in range(PEERS):
        values = got_ref[p].astype(F32)
        for m in range(2):
            for t in range(2):
                at = 128 * (2 * p + t)
                out_ref[m, :, at : at + 128] = values[8 * m + 4 * t : 8 * m + 4 * t + 4]


def per_device(latents, in_weight, out_weight, observe_weight, obs_cells, obs_values, obs_precision):
    c = lax.axis_index("c")
    across = [pair for z in range(7) for pair in ((2 * z + 1, 2 * z + 2), (2 * z + 2, 2 * z + 1))]
    vmem = pl.BlockSpec(memory_space=pltpu.VMEM)
    hbm = pl.BlockSpec(memory_space=pltpu.HBM)
    chip, five = kernel_call(
        rows_kernel, (shaped((8, 2, PAIRS, 128)), shaped((5, 2, PAIRS, 128))),
        [pltpu.VMEM((512, 128), F32)], moved=300_000,
    )(lax.all_gather(latents, "c"))
    five = lax.ppermute(five, TILE, across)
    *parts, sides = pl.pallas_call(
        inner_kernel,
        out_shape=(
            shaped((2, 8, PAIRS, 256)), shaped((2, 6, PAIRS, 512)), shaped((4, 2, PAIRS, 128)),
            shaped((2, 4, PAIRS, 256)), shaped((2, 2, PAIRS, 512)), shaped((2, 768, 512)), shaped((2, 256, 1536)),
            shaped((48, 256)), shaped((1152, 128)), shaped((24, 128), F32),
        ),
        in_specs=[vmem] + [hbm] * 6,
        scratch_shapes=[
            pltpu.VMEM((2, 576, 256), BF16), pltpu.VMEM((2, 64, 2304), BF16), pltpu.VMEM((8, 576), BF16),
            pltpu.VMEM((4, 32), jnp.int32), pltpu.VMEM((4, 256), F32), pltpu.VMEM((4, 256), F32),
            pltpu.SemaphoreType.DMA((6,)),
        ],
        cost_estimate=pl.CostEstimate(flops=2_000_000_000, bytes_accessed=6_000_000, transcendentals=0),
        compiler_params=pltpu.CompilerParams(vmem_limit_bytes=16 * 1024 * 1024),
    )(chip, *(pltpu.with_memory_space_constraint(v, pltpu.HBM) for v in (
        in_weight, jnp.transpose(out_weight, (0, 2, 1)), jnp.transpose(observe_weight), obs_cells, obs_values,
        obs_precision,
    )))
    *parts, obs, pick = parts
    edge, own, seen = kernel_call(
        denoise_kernel,
        (shaped((2, PAIRS, 128)), shaped((PEERS, 16, 128)), shaped((2, 48, 320), F32)),
        [
            pltpu.VMEM((14, 2, PAIRS, 128), BF16),
            pltpu.VMEM((2, 14, PAIRS, 256), BF16),
            pltpu.VMEM((2, 12, PAIRS, 512), BF16),
            pltpu.VMEM((10, 2, PAIRS, 128), BF16),
            pltpu.VMEM((2, 10, PAIRS, 256), BF16),
            pltpu.VMEM((2, 8, PAIRS, 512), BF16),
            pltpu.VMEM((5, 2, PAIRS, 128), BF16),
            pltpu.VMEM((512, 128), F32),
        ],
        flops=3_000_000_000, moved=4_300_000,
    )(chip, five, *parts, obs)
    pay = kernel_call(
        observe_kernel, shaped((PEERS, 32, 128)), [pltpu.VMEM((2, 1, PAIRS, 256), BF16)], moved=800_000,
    )(lax.all_gather(edge, "c"), own, seen, obs, pick, sides)
    got = lax.all_to_all(pay, MEM, 0, 0, tiled=True)

    parts = kernel_call(
        gram_kernel, shaped((16, 32, 128)), [pltpu.VMEM((512, 128), F32)], moved=700_000,
    )(got, sides)
    parts = lax.all_to_all(parts, TILE, 0, 0, tiled=True)
    covariance, back = kernel_call(
        update_kernel, (shaped((64, 64), F32), shaped((PEERS, 16, 128))), [pltpu.VMEM((512, 128), F32)],
        moved=700_000,
    )(got, parts)
    back = lax.all_to_all(back, MEM, 0, 0, tiled=True)
    return kernel_call(final_kernel, (shaped((2, 4, 8192), F32), shaped((64, 64), F32)), moved=400_000)(back, covariance)


def solution(mesh):
    split = Mesh(mesh.devices.reshape(8, 4, 8, 2), ("y", "x", "z", "c"))
    return jax.shard_map(
        per_device,
        mesh=split,
        in_specs=(P(MEM, TILE, None), P(), P(), P(), P(TILE, None), P(TILE, None), P(TILE, None)),
        out_specs=(P(MEM, TILE, None), P()),
        check_vma=False,
    )
```
